32 devices in a mesh: dp: 2 (over core), row: 4 (over y, x), col: 4 (over z).
Axes of the slice: x: 2, y: 2, z: 4, core: 2. Of those that a mesh axis runs over, the one named last changes fastest.
Arguments:
- block_input: bfloat16 [768, 8192], P('row', ('dp', 'col')), may hold values from -6 to 6
- norm_gains: float32 [2, 768], P(None, 'row'), may hold values from 0.1 to 1.9
- row_biases: float32 [4, 768], P(None, 'row'), may hold values from -3 to 3
- w_qkv: bfloat16 [768, 3, 768], P('row', None, 'col'), may hold values from -0.21875 to 0.21875
- qv_bias: float32 [2, 768], P(None, 'col'), may hold values from -3 to 3
- w_out: bfloat16 [768, 768], P('col', 'row'), may hold values from -0.625 to 0.625
- w_up: bfloat16 [768, 3072], P('row', 'col'), may hold values from -0.21875 to 0.21875
- up_bias: float32 [3072], P('col'), may hold values from -3 to 3
- w_down: bfloat16 [768, 3072], P('row', 'col'), may hold values from -0.15625 to 0.15625
- cotangent: bfloat16 [768, 8192], P('row', ('dp', 'col')), may hold values from -6 to 6
Outputs:
- block_output: bfloat16 [768, 8192], P('row', ('dp', 'col'))
- grad_x: bfloat16 [768, 8192], P('row', ('dp', 'col'))
- grad_norm_gains: float32 [2, 768], P(None, 'row')
- grad_row_biases: float32 [4, 768], P(None, 'row')
- grad_w_qkv: float32 [768, 3, 768], P('row', None, 'col')
- grad_qv_bias: float32 [2, 768], P(None, 'col')
- grad_w_out: float32 [768, 768], P('col', 'row')
- grad_w_up: float32 [768, 3072], P('row', 'col')
- grad_up_bias: float32 [3072], P('col')
- grad_w_down: float32 [768, 3072], P('row', 'col')
The draws below stay inside these ranges and needn't reach their ends.
All inputs are finite; a program needn't handle non-finite values.
Results may differ from the reference program's by a relative error of at most 0.013.
Values may be sent and summed in bfloat16 or wider, within the bound.
A program may use at most 192 MiB of HBM per device.

```python
import jax
import jax.numpy as jnp
from jax import lax

D = 768
HEADS = 12
HEAD = 64
FF = 3072
LENGTH = 512
SEQS_DEV = 2
TOKENS = 8192


def block_levels(key, extent, split, low, high):
    def one(dim, shards_of):
        steps = jax.random.uniform(jax.random.fold_in(jax.random.fold_in(key, 6), dim), (shards_of,), jnp.float32, low / len(split), high / len(split))
        return jnp.repeat(jnp.exp(steps), extent[dim] // shards_of).reshape((-1,) + (1,) * (len(extent) - dim - 1))

    loudness = one(*split[0])
    for cut in split[1:]:
        loudness = loudness * one(*cut)
    return loudness


def centred(own_key, extent, scale, bound, cuts=(), dtype=jnp.bfloat16):
    level = block_levels(own_key, extent, cuts, -0.22, 0.18) if cuts else 1.0
    drawn = jax.random.normal(own_key, extent, jnp.float32) * scale * level
    return jnp.minimum(jnp.maximum(drawn, -bound), bound).astype(dtype)


def setup_inputs(seed: int = 0) -> dict:
    splits = jax.random.split(jax.random.key(seed), 11)
    return {
        "block_input": centred(splits[0], (D, TOKENS), 1.0, 6.0, ((0, 4), (1, 8))),
        "norm_gains": jnp.clip(1.0 + 0.18 * jax.random.normal(splits[1], (2, D), jnp.float32), 0.1, 1.9),
        "row_biases": centred(splits[2], (4, D), 0.5, 3.0, ((1, 4),), jnp.float32),
        "w_qkv": centred(splits[3], (D, 3, D), D ** -0.5, 0.21875, ((0, 4), (2, 4))),
        "qv_bias": centred(splits[4], (2, D), 0.5, 3.0, ((1, 4),), jnp.float32),
        "w_out": centred(splits[5], (D, D), (D // 8) ** -0.5, 0.625, ((0, 4), (1, 4))),
        "w_up": centred(splits[6], (D, FF), D ** -0.5, 0.21875, ((0, 4), (1, 4))),
        "up_bias": centred(splits[7], (FF,), 0.5, 3.0, ((0, 4),), jnp.float32),
        "w_down": centred(splits[8], (D, FF), (FF // 2) ** -0.5, 0.15625, ((0, 4), (1, 4))),
        "cotangent": centred(splits[9], (D, TOKENS), 1.0, 6.0, ((0, 4), (1, 8))),
    }


EPSILON = 1e-05
GELU_COEF = 0.7978845608028654

@jax.custom_vjp
def low(v):
    return lax.optimization_barrier(v.astype(jnp.bfloat16)).astype(jnp.float32)

@jax.custom_vjp
def low_back(v):
    return v

def low_keep(v):
    return (low(v), None)

def low_pass(kept, grad):
    return (grad,)

def back_keep(v):
    return (v, None)

def back_low(kept, grad):
    return (low(grad),)
low.defvjp(low_keep, low_pass)
low_back.defvjp(back_keep, back_low)

def matmul(left, right):
    return jnp.dot(left, right, precision=lax.Precision.HIGHEST)

def layer_norm(values, gain, bias):
    center = lax.optimization_barrier(jnp.mean(values, axis=-1, keepdims=True))
    offset = values - center
    spread = lax.optimization_barrier(jnp.mean(offset * offset, axis=-1, keepdims=True))
    return offset * lax.rsqrt(spread + EPSILON) * gain + bias

def gelu_tanh(values):
    return 0.5 * values * (1.0 + jnp.tanh(GELU_COEF * (values + 0.044715 * values * values * values)))

def attend(pieces):
    queries, keys, values = pieces
    scores = jnp.einsum('qhd,khd->hqk', queries, keys, precision=lax.Precision.HIGHEST) * HEAD ** (-0.5)
    scores = low_back(scores)
    positions = jnp.arange(queries.shape[0])
    causal = positions[None, :] <= positions[:, None]
    scores = jnp.where(causal[None], scores, -1e+30)
    summit = lax.optimization_barrier(jnp.max(scores, axis=-1, keepdims=True))
    expos = jnp.exp(scores - summit)
    probs = expos / lax.optimization_barrier(jnp.sum(expos, axis=-1, keepdims=True))
    return jnp.einsum('hqk,khd->qhd', low(probs), values, precision=lax.Precision.HIGHEST)

def forward(block, gains, biases, weight_qkv, bias_qv, weight_out, weight_up, bias_up, weight_down):
    normed = low(layer_norm(block, gains[0], biases[0]))
    mixed = matmul(normed, weight_qkv.reshape(D, 3 * D)).reshape(-1, 3, D)
    bias_three = jnp.stack([bias_qv[0], jnp.zeros_like(bias_qv[0]), bias_qv[1]])
    mixed = low(low_back(mixed + bias_three[None]))
    shaped = (-1, LENGTH, HEADS, HEAD)
    attended = lax.map(jax.checkpoint(attend), (mixed[:, 0].reshape(shaped), mixed[:, 1].reshape(shaped), mixed[:, 2].reshape(shaped)))
    attended = low(low_back(attended.reshape(-1, D)))
    middle = block + low_back(matmul(attended, weight_out) + biases[2])
    normed_two = low(layer_norm(middle, gains[1], biases[1]))
    before = low_back(matmul(normed_two, weight_up) + bias_up)
    hidden = low(gelu_tanh(before))
    return middle + matmul(hidden, weight_down.T) + biases[3]

def reference(block_input, norm_gains, row_biases, w_qkv, qv_bias, w_out, w_up, up_bias, w_down, cotangent):
    params = tuple((arr.astype(jnp.float32) for arr in (norm_gains, row_biases, w_qkv, qv_bias, w_out, w_up, up_bias, w_down)))
    blocks = block_input.astype(jnp.float32).T.reshape(-1, SEQS_DEV * LENGTH, D)
    cots = cotangent.astype(jnp.float32).T.reshape(-1, SEQS_DEV * LENGTH, D)

    def step(totals, pieces):
        block, cot = pieces
        result, pull = jax.vjp(forward, block, *params)
        grads = pull(cot)
        totals = tuple((total + grad for total, grad in zip(totals, grads[1:])))
        return (totals, (result, grads[0]))
    starts = tuple((jnp.zeros_like(param) for param in params))
    totals, (results, input_grads) = lax.scan(step, starts, (blocks, cots))
    return (results.reshape(TOKENS, D).astype(jnp.bfloat16).T, input_grads.reshape(TOKENS, D).astype(jnp.bfloat16).T, totals[0], totals[1], totals[2], totals[3], totals[4], totals[5], totals[6], totals[7])
```

```python
import functools

import jax
import jax.numpy as jnp
from jax import lax
from jax.experimental import pallas as pl
from jax.experimental.pallas import tpu as pltpu
from jax.sharding import PartitionSpec as P

D = 768
HEAD = 64
LENGTH = 512


EPSILON = 1e-05
GELU_COEF = 0.7978845608028654


def gelu_tanh(values):
    return (
        0.5 * values * (1.0 + jnp.tanh(GELU_COEF * (values + 0.044715 * values * values * values)))
    )


def multiply(rows, weight, flipped):
    if flipped:
        return lax.dot_general(
            rows, weight, (((1,), (1,)), ((), ())), preferred_element_type=jnp.float32
        )
    return jnp.dot(rows, weight, preferred_element_type=jnp.float32)


def contract_tokens(left, right):
    return lax.dot_general(
        left, right, (((0,), (0,)), ((), ())), preferred_element_type=jnp.float32
    )


def swap_kernel(axis_name, count, shared, x_ref, o_ref, send_sem, recv_sem, own_sem):
    me = lax.axis_index(axis_name)
    barrier = pltpu.get_barrier_semaphore()
    peers = [lax.rem(me + step, count) for step in range(1, count)]
    for peer in peers:
        pl.semaphore_signal(
            barrier, inc=1, device_id={axis_name: peer}, device_id_type=pl.DeviceIdType.MESH
        )
    own = pltpu.make_async_copy(x_ref if shared else x_ref.at[me], o_ref.at[me], own_sem)
    own.start()
    pl.semaphore_wait(barrier, count - 1)
    copies = []
    for slot, peer in enumerate(peers):
        copy = pltpu.make_async_remote_copy(
            src_ref=x_ref if shared else x_ref.at[peer],
            dst_ref=o_ref.at[me],
            send_sem=send_sem.at[slot],
            recv_sem=recv_sem.at[slot],
            device_id={axis_name: peer},
            device_id_type=pl.DeviceIdType.MESH,
        )
        copy.start()
        copies.append(copy)
    own.wait()
    for copy in copies:
        copy.wait()


def swap(values, axis_name, shared, ident):
    count = lax.axis_size(axis_name)
    block = values.shape if shared else values.shape[1:]
    moved = values.size * values.dtype.itemsize
    return pl.pallas_call(
        functools.partial(swap_kernel, axis_name, count, shared),
        out_shape=jax.ShapeDtypeStruct((count, *block), values.dtype),
        in_specs=[pl.BlockSpec(memory_space=pltpu.VMEM)],
        out_specs=pl.BlockSpec(memory_space=pltpu.VMEM),
        scratch_shapes=[
            pltpu.SemaphoreType.DMA((count - 1,)),
            pltpu.SemaphoreType.DMA((count - 1,)),
            pltpu.SemaphoreType.DMA,
        ],
        compiler_params=pltpu.CompilerParams(collective_id=ident, has_side_effects=True),
        cost_estimate=pl.CostEstimate(
            flops=0, bytes_accessed=(20 if not shared else 60) * moved, transcendentals=0
        ),
    )(values)


def gather_async(local, axis_name):
    return lax.all_gather(local, axis_name, axis=0, tiled=True)


def scatter_sum_async(partial, axis_name):
    return lax.psum_scatter(
        partial.astype(jnp.bfloat16), axis_name, scatter_dimension=0, tiled=True
    ).astype(jnp.float32)


def gather(local, axis_name, ident):
    return swap(local, axis_name, True, ident).reshape(-1, *local.shape[1:])


def scatter_sum(partial, axis_name, ident):
    count = lax.axis_size(axis_name)
    pieces = partial.astype(jnp.bfloat16).reshape(count, -1, *partial.shape[1:])
    return jnp.sum(swap(pieces, axis_name, False, ident).astype(jnp.float32), axis=0)


def to_tokens(first, second, ident):
    rows, cols = lax.axis_size("row"), lax.axis_size("col")
    share = first.shape[0]
    block = jnp.concatenate([first.T, second.T], axis=1).reshape(rows, -1, 2 * share)
    block = swap(block, "row", False, ident)
    if rows != cols:
        moves = [(r * cols + c, c * rows + r) for r in range(rows) for c in range(cols)]
        block = lax.ppermute(block, ("row", "col"), moves)
    first = jnp.concatenate([block[r, :, :share] for r in range(rows)], axis=1)
    second = jnp.concatenate([block[r, :, share:] for r in range(rows)], axis=1)
    return first, second


def to_features(first, second, ident):
    rows, cols = lax.axis_size("row"), lax.axis_size("col")
    share = first.shape[1] // rows
    block = jnp.stack(
        [
            jnp.concatenate(
                [first[:, r * share : (r + 1) * share], second[:, r * share : (r + 1) * share]], axis=1
            )
            for r in range(rows)
        ]
    )
    if rows != cols:
        moves = [(c * rows + r, r * cols + c) for r in range(rows) for c in range(cols)]
        block = lax.ppermute(block, ("row", "col"), moves)
    block = swap(block, "row", False, ident).reshape(-1, 2 * share)
    return block[:, :share].T, block[:, share:].T


def flip(block):
    rows, cols = lax.axis_size("row"), lax.axis_size("col")
    if rows != cols:
        return block
    moves = [(r * cols + c, c * rows + r) for r in range(rows) for c in range(cols)]
    return lax.ppermute(block, ("row", "col"), moves)


def norm_forward(values, gain, bias):
    center = jnp.mean(values, axis=1, keepdims=True)
    offset = values - center
    inverse = lax.rsqrt(jnp.mean(offset * offset, axis=1, keepdims=True) + EPSILON)
    normal = offset * inverse
    return (normal * gain + bias, normal, inverse)


def norm_backward(grad, gain, normal, inverse):
    scaled = grad * gain
    first = jnp.mean(scaled, axis=1, keepdims=True)
    second = jnp.mean(scaled * normal, axis=1, keepdims=True)
    result = inverse * (scaled - first - normal * second)
    return (result, jnp.sum(grad * normal, axis=0), jnp.sum(grad, axis=0))


def causal_mask(length):
    positions = jnp.arange(length)
    return positions[None, :] <= positions[:, None]


def attention_forward(queries, keys, values):
    factor = HEAD ** (-0.5)

    def one_sequence(pieces):
        seq_q, seq_k, seq_v = pieces
        scores = (
            jnp.einsum("qhd,khd->hqk", seq_q, seq_k, preferred_element_type=jnp.float32) * factor
        )
        scores = jnp.where(causal_mask(seq_q.shape[0])[None], scores, -1e30)
        summit = jnp.max(scores, axis=-1, keepdims=True)
        expos = jnp.exp(scores - summit)
        total = jnp.sum(expos, axis=-1, keepdims=True)
        probs = (expos / total).astype(jnp.bfloat16)
        output = jnp.einsum("hqk,khd->qhd", probs, seq_v, preferred_element_type=jnp.float32)
        return (output, summit[..., 0] + jnp.log(total[..., 0]))

    return lax.map(one_sequence, (queries, keys, values))


def attention_backward(queries, keys, values, grad_out, log_sums):
    factor = HEAD ** (-0.5)

    def one_sequence(pieces):
        seq_q, seq_k, seq_v, seq_g, seq_l = pieces
        scores = (
            jnp.einsum("qhd,khd->hqk", seq_q, seq_k, preferred_element_type=jnp.float32) * factor
        )
        scores = jnp.where(causal_mask(seq_q.shape[0])[None], scores, -1e30)
        probs = jnp.exp(scores - seq_l[..., None])
        grad_v = jnp.einsum(
            "hqk,qhd->khd", probs.astype(jnp.bfloat16), seq_g, preferred_element_type=jnp.float32
        )
        grad_p = jnp.einsum("qhd,khd->hqk", seq_g, seq_v, preferred_element_type=jnp.float32)
        inner = jnp.sum(grad_p * probs, axis=-1, keepdims=True)
        grad_s = (probs * (grad_p - inner)).astype(jnp.bfloat16)
        grad_q = (
            jnp.einsum("hqk,khd->qhd", grad_s, seq_k, preferred_element_type=jnp.float32) * factor
        )
        grad_k = (
            jnp.einsum("hqk,qhd->khd", grad_s, seq_q, preferred_element_type=jnp.float32) * factor
        )
        return (grad_q, grad_k, grad_v)

    return lax.map(one_sequence, (queries, keys, values, grad_out, log_sums))


def body(
    block_input, norm_gains, row_biases, w_qkv, qv_bias, w_out, w_up, up_bias, w_down, cotangent
):
    head_cols = w_qkv.shape[2]
    square = lax.axis_size("row") == lax.axis_size("col")
    heads_axis, split_axis = ("row", "col") if square else ("col", "row")
    qv_bias, up_bias = flip(qv_bias), flip(up_bias)
    inputs, cot = to_tokens(block_input, cotangent, 0)
    inputs = inputs.astype(jnp.float32)
    vectors = swap(jnp.concatenate([norm_gains, row_biases], axis=0), "row", True, 1)
    vectors = jnp.concatenate([vectors[r] for r in range(vectors.shape[0])], axis=1)
    gains, biases = vectors[:2], vectors[2:]
    qkv_weight = gather_async(flip(w_qkv.reshape(w_qkv.shape[0], -1)), split_axis)
    rest = gather_async(flip(jnp.concatenate([w_out.T, w_up, w_down], axis=1)), split_axis)
    width = w_up.shape[1]
    out_t = rest[:, :head_cols]
    up = rest[:, head_cols : head_cols + width]
    down = rest[:, head_cols + width :]

    normed_one, normal_one, inverse_one = norm_forward(inputs, gains[0], biases[0])
    source_one = gather(normed_one.astype(jnp.bfloat16), heads_axis, 2)
    qkv_sum = multiply(source_one, qkv_weight, False)
    rows_here = qkv_sum.shape[0]
    qkv_sum = qkv_sum.reshape(rows_here, 3, head_cols)
    shape_four = (rows_here // LENGTH, LENGTH, head_cols // HEAD, HEAD)
    queries = (qkv_sum[:, 0] + qv_bias[0]).astype(jnp.bfloat16).reshape(shape_four)
    keys_all = qkv_sum[:, 1].astype(jnp.bfloat16).reshape(shape_four)
    values_all = (qkv_sum[:, 2] + qv_bias[1]).astype(jnp.bfloat16).reshape(shape_four)
    attended, log_sums = attention_forward(queries, keys_all, values_all)
    attended_low = attended.reshape(rows_here, head_cols).astype(jnp.bfloat16)
    middle = inputs + scatter_sum(multiply(attended_low, out_t, True), heads_axis, 3) + biases[2]
    normed_two, normal_two, inverse_two = norm_forward(middle, gains[1], biases[1])
    source_two = gather(normed_two.astype(jnp.bfloat16), heads_axis, 4)
    cot_all = gather_async(cot, heads_axis)
    before = multiply(source_two, up, False) + up_bias
    hidden_low = gelu_tanh(before).astype(jnp.bfloat16)
    grad_hidden = multiply(cot_all, down, False)
    grad_before = jax.vjp(gelu_tanh, before)[1](grad_hidden)[0].astype(jnp.bfloat16)
    grad_normed_two = scatter_sum(multiply(grad_before, up, True), heads_axis, 5)
    output = middle + scatter_sum_async(multiply(hidden_low, down, True), heads_axis) + biases[3]
    grad_w_down = contract_tokens(cot_all, hidden_low)
    grad_up_bias = jnp.sum(grad_before.astype(jnp.float32), axis=0)
    grad_w_up = contract_tokens(source_two, grad_before)
    grad_out = cot.astype(jnp.float32)
    back_two, gain_two, shift_two = norm_backward(
        grad_normed_two, gains[1], normal_two, inverse_two
    )
    grad_middle = grad_out + back_two
    grad_middle_low = grad_middle.astype(jnp.bfloat16)
    grad_out_bias = jnp.sum(grad_middle_low.astype(jnp.float32), axis=0)
    grad_down_bias = jnp.sum(grad_out, axis=0)
    grad_middle_all = gather(grad_middle_low, heads_axis, 6)
    grad_att_low = multiply(grad_middle_all, out_t, False).astype(jnp.bfloat16).reshape(shape_four)
    grad_w_out_t = contract_tokens(grad_middle_all, attended_low)
    grad_q, grad_k, grad_v = attention_backward(
        queries, keys_all, values_all, grad_att_low, log_sums
    )
    grad_q = grad_q.reshape(rows_here, head_cols).astype(jnp.bfloat16)
    grad_k = grad_k.reshape(rows_here, head_cols).astype(jnp.bfloat16)
    grad_v = grad_v.reshape(rows_here, head_cols).astype(jnp.bfloat16)
    grad_qkv_low = jnp.concatenate([grad_q, grad_k, grad_v], axis=1)
    grad_qv = jnp.stack(
        [jnp.sum(grad_q.astype(jnp.float32), axis=0), jnp.sum(grad_v.astype(jnp.float32), axis=0)]
    )
    grad_normed_one = scatter_sum(multiply(grad_qkv_low, qkv_weight, True), heads_axis, 7)
    grad_w_qkv = contract_tokens(source_one, grad_qkv_low)
    back_one, gain_one, shift_one = norm_backward(
        grad_normed_one, gains[0], normal_one, inverse_one
    )
    grad_input = grad_middle + back_one

    mlp_sum = scatter_sum_async(jnp.concatenate([grad_w_up, grad_w_down], axis=1), split_axis)
    mlp_sum = flip(lax.psum(mlp_sum.astype(jnp.bfloat16), "dp")).astype(jnp.float32)
    att_sum = scatter_sum(jnp.concatenate([grad_w_qkv, grad_w_out_t], axis=1), split_axis, 8)
    att_sum = jnp.sum(
        swap(flip(att_sum.astype(jnp.bfloat16)), "dp", True, 9).astype(jnp.float32), axis=0
    )
    sum_up = mlp_sum[:, :width]
    sum_down = mlp_sum[:, width:]
    sum_qkv = att_sum[:, : 3 * head_cols].reshape(w_qkv.shape)
    sum_out = att_sum[:, 3 * head_cols :].T
    features = gains.shape[1]
    longest = max(features, width, 2 * head_cols)
    small = [gain_one, gain_two, shift_one, shift_two, grad_out_bias, grad_down_bias]
    small = small + [grad_up_bias, grad_qv.reshape(-1)]
    small = jnp.stack([jnp.pad(row, (0, longest - row.shape[0])) for row in small])
    small = jnp.sum(swap(small, "dp", True, 10), axis=0)
    small = jnp.sum(swap(small, split_axis, True, 11), axis=0)
    projected = flip(small[6:])
    sum_upb = projected[0, :width]
    sum_qv = projected[1, : 2 * head_cols].reshape(2, head_cols)
    share = norm_gains.shape[1]
    small = jnp.sum(swap(small[:6], heads_axis, True, 12), axis=0)
    small = lax.dynamic_slice_in_dim(small, lax.axis_index("row") * share, share, axis=1)
    output_t, grad_input_t = to_features(
        output.astype(jnp.bfloat16), grad_input.astype(jnp.bfloat16), 13
    )
    return (
        output_t,
        grad_input_t,
        small[:2],
        small[2:],
        sum_qkv,
        sum_qv,
        sum_out,
        sum_up,
        sum_upb,
        sum_down,
    )


MESH = pl.DeviceIdType.MESH
BIG = 60 * 1024 * 1024


def send(axis_name, peer, source, target, send_sem, recv_sem):
    copy = pltpu.make_async_remote_copy(
        src_ref=source,
        dst_ref=target,
        send_sem=send_sem,
        recv_sem=recv_sem,
        device_id={axis_name: peer},
        device_id_type=MESH,
    )
    copy.start()
    return copy


def keep(source, target, sem):
    copy = pltpu.make_async_copy(source, target, sem)
    copy.start()
    return copy


def others(axis_name):
    count = lax.axis_size(axis_name)
    me = lax.axis_index(axis_name)
    return me, [lax.rem(me + step, count) for step in range(1, count)]


def meet():
    barrier = pltpu.get_barrier_semaphore()
    total = 0
    for name in ("row", "col", "dp"):
        _, peers = others(name)
        for peer in peers:
            pl.semaphore_signal(barrier, inc=1, device_id={name: peer}, device_id_type=MESH)
        total += len(peers)
    pl.semaphore_wait(barrier, total)


def rows_of(index, size):
    return pl.ds(pl.multiple_of(index * size, size), size)


def left_t(weight, acts):
    return lax.dot_general(weight, acts, (((0,), (0,)), ((), ())), preferred_element_type=jnp.float32)


def right_t(left, right):
    return lax.dot_general(left, right, (((1,), (1,)), ((), ())), preferred_element_type=jnp.float32)


def plain(left, right):
    return jnp.dot(left, right, preferred_element_type=jnp.float32)


def lane_sums(values):
    ones = jnp.ones((8, values.shape[1]), jnp.float32)
    return lax.dot_general(
        ones,
        values,
        (((1,), (1,)), ((), ())),
        precision=lax.Precision.HIGHEST,
        preferred_element_type=jnp.float32,
    )


def spread_weight(stage, own_ref, full_ref, buf, piece, sems):
    half = own_ref.shape[0] // 2
    core = lax.axis_index("dp")
    row, row_peers = others("row")
    col, col_peers = others("col")
    other = 1 - core
    z_send, z_recv, p_send, p_recv, c_send, c_recv = (sem.at[piece] for sem in sems)
    slots = buf.at[piece]
    size = 2 * half

    def rows_at(index, which):
        return pl.ds(pl.multiple_of(index * size + which * half, half), half)

    if stage == 0:
        mine = own_ref.at[pl.ds(pl.multiple_of(core * half, half), half)]
        copies = [keep(mine, slots.at[col], z_recv.at[col])]
        for step, peer in enumerate(col_peers):
            copies.append(send("col", peer, mine, slots.at[col], z_send.at[step], z_recv.at[col]))
        return copies
    if stage == 1:
        place = rows_at(row, core)
        copies = [keep(slots.at[row], full_ref.at[place], p_recv.at[row])]
        for step, peer in enumerate(row_peers):
            copies.append(
                send("row", peer, slots.at[peer], full_ref.at[place], p_send.at[step], p_recv.at[row])
            )
        return copies
    copies = []
    for index in range(len(row_peers) + 1):
        place = rows_at(index, core)
        copies.append(
            send("dp", other, full_ref.at[place], full_ref.at[place], c_send.at[index], c_recv.at[index])
        )
    return copies


def wait_recv_all(block, sems, count):
    for index in range(count):
        pltpu.make_async_copy(block, block, sems.at[index]).wait()


def enter_kernel(
    seqs,
    x_ref,
    c_ref,
    vec_ref,
    tip_ref,
    wa_ref,
    wu_ref,
    wd_ref,
    x_all,
    c_all,
    wa_all,
    wu_all,
    wd_all,
    ln_ref,
    qkv_ref,
    att_ref,
    lse_ref,
    stat_ref,
    x1_ref,
    l2_ref,
    vcol_ref,
    tcol_ref,
    vec_all,
    tip_all,
    zbuf,
    part,
    got,
    l2_own,
    x_send,
    x_recv,
    c_send,
    c_recv,
    v_send,
    v_recv,
    t_send,
    t_recv,
    z_send,
    z_recv,
    p_send,
    p_recv,
    d_send,
    d_recv,
    r_send,
    r_recv,
    a_send,
    a_recv,
):
    share = x_ref.shape[0]
    length = x_ref.shape[1] // seqs
    row, row_peers = others("row")
    col, col_peers = others("col")
    rows = len(row_peers) + 1
    head_cols = wa_ref.shape[1] // 4
    heads = head_cols // HEAD
    piece = length // rows
    sems = (z_send, z_recv, p_send, p_recv, d_send, d_recv)
    half = wa_ref.shape[0] // 2
    meet()
    waits = []
    slab = rows_of(row, share)
    local = [
        keep(vec_ref, vec_all.at[row], v_recv.at[row]),
        keep(tip_ref, tip_all.at[col], t_recv.at[col]),
    ]
    vec_copies = [
        send("row", peer, vec_ref, vec_all.at[row], v_send.at[step], v_recv.at[row])
        for step, peer in enumerate(row_peers)
    ]
    tip_copies = [
        send("col", peer, tip_ref, tip_all.at[col], t_send.at[step], t_recv.at[col])
        for step, peer in enumerate(col_peers)
    ]
    spread = [None, None, None]
    z_copies = [spread_weight(0, wa_ref, wa_all, zbuf, 0, sems)]
    x_copies = []
    for seq in range(seqs):
        cols = pl.ds(seq * length, length)
        keep(x_ref.at[:, cols], x_all.at[slab, cols], x_recv.at[seq, row])
        x_copies.append(
            [
                send(
                    "row",
                    peer,
                    x_ref.at[:, cols],
                    x_all.at[slab, cols],
                    x_send.at[seq, step],
                    x_recv.at[seq, row],
                )
                for step, peer in enumerate(row_peers)
            ]
        )
    z_copies.append(spread_weight(0, wu_ref, wu_all, zbuf, 1, sems))
    z_copies.append(spread_weight(0, wd_ref, wd_all, zbuf, 2, sems))
    wait_recv_all(zbuf.at[0, 0], z_recv.at[0], len(col_peers) + 1)
    p_copies = [spread_weight(1, wa_ref, wa_all, zbuf, 0, sems)]
    wait_recv_all(vec_all.at[0], v_recv, rows)
    for index in range(rows):
        flipped = vec_all[index].T
        vcol_ref[index * share : (index + 1) * share, :] = flipped[:share]
    wait_recv_all(tip_all.at[0], t_recv, len(col_peers) + 1)
    tip = tip_all[row].T
    bias_q, bias_v = tip[:head_cols, 0:1], tip[:head_cols, 1:2]
    for index in range(tcol_ref.shape[0] // tip.shape[0]):
        tcol_ref[index * tip.shape[0] : (index + 1) * tip.shape[0], :] = jnp.broadcast_to(
            tip[:, 2 + index : 3 + index], (tip.shape[0], 8)
        )

    chunk = length // 2

    def first_norm(step, carry):
        cols = pl.ds(pl.multiple_of(step * chunk, chunk), chunk)
        values = x_all[:, cols].astype(jnp.float32)
        center = jnp.mean(values, axis=0, keepdims=True)
        offset = values - center
        inverse = lax.rsqrt(jnp.mean(offset * offset, axis=0, keepdims=True) + EPSILON)
        normed = offset * inverse * vcol_ref[:, 0:1] + vcol_ref[:, 2:3]
        ln_ref[:, cols] = normed.astype(jnp.bfloat16)
        stat_ref[0:1, cols] = center
        stat_ref[1:2, cols] = inverse
        return carry

    for seq in range(seqs):
        wait_recv_all(x_ref.at[:, pl.ds(0, length)], x_recv.at[seq], rows)
        lax.fori_loop(2 * seq, 2 * seq + 2, first_norm, 0)
    wait_recv_all(zbuf.at[0, 0], p_recv.at[0], rows)
    d_copies = [spread_weight(2, wa_ref, wa_all, zbuf, 0, sems)]
    for copy in d_copies[0]:
        copy.wait()
    for peer_list in (row_peers,):
        keep(c_ref, c_all.at[slab], c_recv.at[row])
        c_copies = [
            send("row", peer, c_ref, c_all.at[slab], c_send.at[step], c_recv.at[row])
            for step, peer in enumerate(peer_list)
        ]
    lse_ref[...] = jnp.zeros_like(lse_ref)

    def project(step, carry):
        cols = pl.ds(pl.multiple_of(step * chunk, chunk), chunk)
        acts = ln_ref[:, cols]
        mixed = left_t(wa_all[:, : 3 * head_cols], acts)
        qkv_ref[:head_cols, cols] = ((mixed[:head_cols] + bias_q) * HEAD**-0.5).astype(jnp.bfloat16)
        qkv_ref[head_cols : 2 * head_cols, cols] = mixed[head_cols : 2 * head_cols].astype(jnp.bfloat16)
        qkv_ref[2 * head_cols :, cols] = (mixed[2 * head_cols :] + bias_v).astype(jnp.bfloat16)
        return carry

    def attend(seq):
        def one(head, carry):
            at = pl.multiple_of(head * HEAD, HEAD)
            for part_q in range(2):
                cols = pl.ds(seq * length + part_q * chunk, chunk)
                keys = (part_q + 1) * chunk
                span = pl.ds(seq * length, keys)
                queries = qkv_ref[pl.ds(at, HEAD), cols]
                scores = left_t(qkv_ref[pl.ds(at + head_cols, HEAD), span], queries)
                key_at = lax.broadcasted_iota(jnp.int32, (keys, chunk), 0)
                query_at = lax.broadcasted_iota(jnp.int32, (keys, chunk), 1) + part_q * chunk
                scores = jnp.where(key_at <= query_at, scores, -1e30)
                summit = jnp.max(scores, axis=0, keepdims=True)
                expos = jnp.exp(scores - summit)
                total = jnp.sum(expos, axis=0, keepdims=True)
                mixed = plain(qkv_ref[pl.ds(at + 2 * head_cols, HEAD), span], expos.astype(jnp.bfloat16))
                att_ref[pl.ds(at, HEAD), cols] = (mixed / total).astype(jnp.bfloat16)
                lse_ref[seq * heads + head, :, pl.ds(part_q * chunk, chunk)] = jnp.broadcast_to(
                    summit + jnp.log(total), (8, chunk)
                )
            return carry

        lax.fori_loop(0, heads, one, 0)

    out_copies = []
    for seq in range(seqs):
        lax.fori_loop(2 * seq, 2 * seq + 2, project, 0)
        attend(seq)
        mixed = plain(wa_all[:, 3 * head_cols :], att_ref[:, seq * length : (seq + 1) * length])
        for index in range(rows):
            part[seq, index] = mixed[:, index * piece : (index + 1) * piece].astype(jnp.bfloat16)
        out_copies.append(
            [
                send(
                    "row",
                    peer,
                    part.at[seq, peer],
                    got.at[seq, step],
                    r_send.at[seq, step],
                    r_recv.at[seq, step],
                )
                for step, peer in enumerate(row_peers)
            ]
        )
        if seq == 0:
            for index, (own, full) in enumerate(((wu_ref, wu_all), (wd_ref, wd_all))):
                wait_recv_all(zbuf.at[0, 0], z_recv.at[1 + index], len(col_peers) + 1)
                p_copies.append(spread_weight(1, own, full, zbuf, 1 + index, sems))
    gather_copies = []
    for seq in range(seqs):
        for copy in out_copies[seq]:
            copy.wait_recv()
        own = pl.ds(pl.multiple_of(seq * length + row * piece, piece), piece)
        total = part[seq, row].astype(jnp.float32)
        for step in range(rows - 1):
            total = total + got[seq, step].astype(jnp.float32)
        middle = x_all[:, own].astype(jnp.float32) + total + vcol_ref[:, 4:5]
        x1_ref[:, seq * piece : (seq + 1) * piece] = middle
        center = jnp.mean(middle, axis=0, keepdims=True)
        offset = middle - center
        inverse = lax.rsqrt(jnp.mean(offset * offset, axis=0, keepdims=True) + EPSILON)
        normed = (offset * inverse * vcol_ref[:, 1:2] + vcol_ref[:, 3:4]).astype(jnp.bfloat16)
        l2_own[seq] = normed
        keep(l2_own.at[seq], l2_ref.at[:, own], a_recv.at[seq, row])
        gather_copies.append(
            [
                send(
                    "row",
                    peer,
                    l2_own.at[seq],
                    l2_ref.at[:, own],
                    a_send.at[seq, step],
                    a_recv.at[seq, row],
                )
                for step, peer in enumerate(row_peers)
            ]
        )
    for index, (own, full) in enumerate(((wu_ref, wu_all), (wd_ref, wd_all))):
        wait_recv_all(zbuf.at[0, 0], p_recv.at[1 + index], rows)
        d_copies.append(spread_weight(2, own, full, zbuf, 1 + index, sems))
    for copies in d_copies[1:]:
        for copy in copies:
            copy.wait()
    wait_recv_all(c_ref, c_recv, rows)
    for seq in range(seqs):
        wait_recv_all(l2_own.at[0], a_recv.at[seq], rows)
    for group in [vec_copies, tip_copies, c_copies] + x_copies + out_copies + gather_copies:
        for copy in group:
            copy.wait_send()
    for group in z_copies + p_copies:
        for copy in group[1:]:
            copy.wait_send()


def dma(*shape):
    return pltpu.SemaphoreType.DMA(shape)


def enter(x, cot, vec, tip, wa, wu, wd):
    share, tokens = x.shape
    rows, cols = lax.axis_size("row"), lax.axis_size("col")
    width = share * rows
    head_cols = wa.shape[1] // 4
    seqs = tokens // LENGTH
    heads = head_cols // HEAD
    piece = LENGTH // rows
    low, full = jnp.bfloat16, jnp.float32
    shapes = [
        ((width, tokens), low),
        ((width, tokens), low),
        ((width, wa.shape[1]), low),
        ((width, wu.shape[1]), low),
        ((width, wd.shape[1]), low),
        ((width, tokens), low),
        ((3 * head_cols, tokens), low),
        ((head_cols, tokens), low),
        ((seqs * heads, 8, LENGTH), full),
        ((8, tokens), full),
        ((width, seqs * piece), full),
        ((width, tokens), low),
        ((width, 8), full),
        ((wu.shape[1], 8), full),
    ]
    return pl.pallas_call(
        functools.partial(enter_kernel, seqs),
        out_shape=[jax.ShapeDtypeStruct(*shape) for shape in shapes],
        in_specs=[pl.BlockSpec(memory_space=pltpu.VMEM)] * 7,
        out_specs=[pl.BlockSpec(memory_space=pltpu.VMEM)] * len(shapes),
        scratch_shapes=[
            pltpu.VMEM((rows, *vec.shape), full),
            pltpu.VMEM((cols, *tip.shape), full),
            pltpu.VMEM((3, cols, share // 2, wa.shape[1]), low),
            pltpu.VMEM((seqs, rows, width, piece), low),
            pltpu.VMEM((seqs, rows - 1, width, piece), low),
            pltpu.VMEM((seqs, width, piece), low),
            dma(seqs, rows - 1),
            dma(seqs, rows),
            dma(rows - 1),
            dma(rows),
            dma(rows - 1),
            dma(rows),
            dma(cols - 1),
            dma(cols),
            dma(3, cols - 1),
            dma(3, cols),
            dma(3, rows - 1),
            dma(3, rows),
            dma(3, rows),
            dma(3, rows),
            dma(seqs, rows - 1),
            dma(seqs, rows - 1),
            dma(seqs, rows - 1),
            dma(seqs, rows),
        ],
        compiler_params=pltpu.CompilerParams(
            collective_id=0, has_side_effects=True, vmem_limit_bytes=BIG
        ),
    )(x, cot, vec, tip, wa, wu, wd)


def mlp_kernel(
    seqs,
    l2_ref,
    c_ref,
    x1_ref,
    wu_ref,
    wd_ref,
    vcol_ref,
    tcol_ref,
    gx_ref,
    y_ref,
    du_ref,
    dd_ref,
    small_ref,
    up_ref,
    wu_t,
    wd_t,
    hid,
    gra,
    x1_wide,
    part,
    got,
    gx_own,
    r_send,
    r_recv,
    a_send,
    a_recv,
):
    width, tokens = l2_ref.shape
    length = tokens // seqs
    row, row_peers = others("row")
    rows = len(row_peers) + 1
    piece = length // rows
    chunk = length // 2
    barrier = pltpu.get_barrier_semaphore()
    for peer in row_peers:
        pl.semaphore_signal(barrier, inc=1, device_id={"row": peer}, device_id_type=MESH)
    wu_t[...] = wu_ref[...].T
    wd_t[...] = wd_ref[...].T
    pieces = chunk // piece

    def forward(step, carry):
        cols = pl.ds(pl.multiple_of(step * chunk, chunk), chunk)
        before = plain(wu_t[...], l2_ref[:, cols]) + tcol_ref[:, 0:1]
        square = before * before
        tanh = jnp.tanh(GELU_COEF * (before + 0.044715 * before * square))
        hid[:, cols] = (0.5 * before * (1.0 + tanh)).astype(jnp.bfloat16)
        slope = 0.5 * (1.0 + tanh) + 0.5 * before * (1.0 - tanh * tanh) * (
            GELU_COEF * (1.0 + 3.0 * 0.044715 * square)
        )
        grad = (plain(wd_t[...], c_ref[:, cols]) * slope).astype(jnp.bfloat16)
        gra[:, cols] = grad
        back = plain(wu_ref[...], grad)
        for index in range(pieces):
            part[step * pieces + index] = back[:, index * piece : (index + 1) * piece].astype(
                jnp.bfloat16
            )
        return carry

    out_copies = []
    for seq in range(seqs):
        lax.fori_loop(2 * seq, 2 * seq + 2, forward, 0)
        if seq == 0:
            pl.semaphore_wait(barrier, rows - 1)
        out_copies.append(
            [
                send(
                    "row",
                    peer,
                    part.at[seq * rows + peer],
                    got.at[seq, step],
                    r_send.at[seq, step],
                    r_recv.at[seq, step],
                )
                for step, peer in enumerate(row_peers)
            ]
        )
    x1_wide[...] = jnp.zeros_like(x1_wide)
    for seq in range(seqs):
        own = pl.ds(pl.multiple_of(seq * length + row * piece, piece), piece)
        x1_wide[:, own] = x1_ref[:, seq * piece : (seq + 1) * piece] + vcol_ref[:, 5:6]

    def finish(step, carry):
        cols = pl.ds(pl.multiple_of(step * chunk, chunk), chunk)
        y_ref[:, cols] = (plain(wd_ref[...], hid[:, cols]) + x1_wide[:, cols]).astype(jnp.bfloat16)
        return carry

    block = width // 4

    def up_weight(step, carry):
        place = pl.ds(pl.multiple_of(step * block, block), block)
        du_ref[place, :] = right_t(l2_ref[place, :], gra[...]).astype(jnp.bfloat16)
        return carry

    def down_weight(step, carry):
        place = pl.ds(pl.multiple_of(step * block, block), block)
        dd_ref[place, :] = right_t(c_ref[place, :], hid[...]).astype(jnp.bfloat16)
        return carry

    lax.fori_loop(0, 2 * seqs, finish, 0)
    gather_copies = []
    sums = [0.0] * 4
    for seq in range(seqs):
        for copy in out_copies[seq]:
            copy.wait_recv()
        own = pl.ds(pl.multiple_of(seq * length + row * piece, piece), piece)
        grad = part[seq * rows + row].astype(jnp.float32)
        for step in range(rows - 1):
            grad = grad + got[seq, step].astype(jnp.float32)
        middle = x1_ref[:, seq * piece : (seq + 1) * piece]
        center = jnp.mean(middle, axis=0, keepdims=True)
        offset = middle - center
        inverse = lax.rsqrt(jnp.mean(offset * offset, axis=0, keepdims=True) + EPSILON)
        normal = offset * inverse
        scaled = grad * vcol_ref[:, 1:2]
        first = jnp.mean(scaled, axis=0, keepdims=True)
        second = jnp.mean(scaled * normal, axis=0, keepdims=True)
        outer = c_ref[:, own].astype(jnp.float32)
        result = (outer + inverse * (scaled - first - normal * second)).astype(jnp.bfloat16)
        gx_own[seq] = result
        keep(gx_own.at[seq], gx_ref.at[:, own], a_recv.at[seq, row])
        gather_copies.append(
            [
                send(
                    "row",
                    peer,
                    gx_own.at[seq],
                    gx_ref.at[:, own],
                    a_send.at[seq, step],
                    a_recv.at[seq, row],
                )
                for step, peer in enumerate(row_peers)
            ]
        )
        terms = (grad * normal, grad, result.astype(jnp.float32), outer)
        sums = [old + new for old, new in zip(sums, terms)]
    lax.fori_loop(0, 4, up_weight, 0)
    lax.fori_loop(0, 4, down_weight, 0)
    small_ref[...] = jnp.zeros_like(small_ref)
    for index in range(4):
        small_ref[index : index + 1, :] = lane_sums(sums[index])[0:1]
    up_ref[...] = right_t(jnp.ones((8, tokens), jnp.bfloat16), gra[...])
    for seq in range(seqs):
        wait_recv_all(gx_own.at[0], a_recv.at[seq], rows)
    for group in out_copies + gather_copies:
        for copy in group:
            copy.wait_send()


def mlp(l2, cot, x1, wu, wd, vcol, tcol):
    width, tokens = l2.shape
    rows = lax.axis_size("row")
    seqs = tokens // LENGTH
    piece = LENGTH // rows
    hidden = wu.shape[1]
    low, full = jnp.bfloat16, jnp.float32
    shapes = [
        ((width, tokens), low),
        ((width, tokens), low),
        ((width, hidden), low),
        ((width, hidden), low),
        ((8, width), full),
        ((8, hidden), full),
    ]
    return pl.pallas_call(
        functools.partial(mlp_kernel, seqs),
        out_shape=[jax.ShapeDtypeStruct(*shape) for shape in shapes],
        in_specs=[pl.BlockSpec(memory_space=pltpu.VMEM)] * 7,
        out_specs=[pl.BlockSpec(memory_space=pltpu.VMEM)] * len(shapes),
        scratch_shapes=[
            pltpu.VMEM((hidden, width), low),
            pltpu.VMEM((hidden, width), low),
            pltpu.VMEM((hidden, tokens), low),
            pltpu.VMEM((hidden, tokens), low),
            pltpu.VMEM((width, tokens), full),
            pltpu.VMEM((seqs * rows, width, piece), low),
            pltpu.VMEM((seqs, rows - 1, width, piece), low),
            pltpu.VMEM((seqs, width, piece), low),
            dma(seqs, rows - 1),
            dma(seqs, rows - 1),
            dma(seqs, rows - 1),
            dma(seqs, rows),
        ],
        compiler_params=pltpu.CompilerParams(
            collective_id=1, has_side_effects=True, vmem_limit_bytes=BIG
        ),
    )(l2, cot, x1, wu, wd, vcol, tcol)


def leave_kernel(
    seqs,
    x_ref,
    gx_ref,
    y_ref,
    wa_ref,
    qkv_ref,
    att_ref,
    lse_ref,
    ln_ref,
    stat_ref,
    vcol_ref,
    small_ref,
    up_ref,
    du_ref,
    dd_ref,
    out_ref,
    gin_ref,
    gu_ref,
    gd_ref,
    ga_ref,
    a_ref,
    b_ref,
    y_got,
    back,
    mixed_grad,
    head_grad,
    got,
    stat_own,
    stat_all,
    da_ref,
    pair,
    summed,
    plane,
    line,
    small_all,
    tip_own,
    tip_all,
    a_own,
    a_all,
    b_all,
    a_sum,
    b_sum,
    a_pair,
    b_pair,
    y_send,
    y_recv,
    r_send,
    r_recv,
    s_send,
    s_recv,
    g_send,
    g_recv,
    p_send,
    p_recv,
    z_send,
    z_recv,
    f_send,
    f_recv,
    m_send,
    m_recv,
    t_send,
    t_recv,
    n_send,
    n_recv,
    e_send,
    e_recv,
):
    share, tokens = x_ref.shape
    length = tokens // seqs
    row, row_peers = others("row")
    col, col_peers = others("col")
    core = lax.axis_index("dp")
    twin = 1 - core
    rows, cols = len(row_peers) + 1, len(col_peers) + 1
    width = gx_ref.shape[0]
    head_cols = att_ref.shape[0]
    heads = head_cols // HEAD
    chunk = length // 2
    half = share // 2
    slab = rows_of(row, share)
    grads = (du_ref, dd_ref, da_ref)
    finals = (gu_ref, gd_ref, ga_ref)
    meet()
    y_copies = [
        send("row", peer, y_ref.at[rows_of(peer, share)], y_got.at[step], y_send.at[step], y_recv.at[step])
        for step, peer in enumerate(row_peers)
    ]

    def pair_start(piece):
        copies = []
        for index in range(rows):
            place = pl.ds(pl.multiple_of(index * share + twin * half, half), half)
            copies.append(
                send(
                    "dp",
                    twin,
                    grads[piece].at[place],
                    pair.at[piece, index],
                    g_send.at[piece, index],
                    g_recv.at[piece, index],
                )
            )
        return copies

    def pair_finish(piece, copies):
        for copy in copies:
            copy.wait_recv()
        for index in range(rows):
            place = pl.ds(pl.multiple_of(index * share + core * half, half), half)
            total = grads[piece][place, :].astype(jnp.float32) + pair[piece, index].astype(jnp.float32)
            summed[piece, index] = total.astype(jnp.bfloat16)
        keep(summed.at[piece, row], plane.at[piece, row], p_recv.at[piece, row])
        return [
            send(
                "row",
                peer,
                summed.at[piece, peer],
                plane.at[piece, row],
                p_send.at[piece, step],
                p_recv.at[piece, row],
            )
            for step, peer in enumerate(row_peers)
        ]

    def line_start(piece):
        wait_recv_all(plane.at[0, 0], p_recv.at[piece], rows)
        keep(plane.at[piece, col], line.at[piece, col], z_recv.at[piece, col])
        return [
            send(
                "col",
                peer,
                plane.at[piece, peer],
                line.at[piece, col],
                z_send.at[piece, step],
                z_recv.at[piece, col],
            )
            for step, peer in enumerate(col_peers)
        ]

    def line_finish(piece):
        wait_recv_all(line.at[0, 0], z_recv.at[piece], cols)
        total = line[piece, 0].astype(jnp.float32)
        for index in range(1, cols):
            total = total + line[piece, index].astype(jnp.float32)
        place = pl.ds(pl.multiple_of(core * half, half), half)
        finals[piece][place, :] = total
        return send(
            "dp", twin, finals[piece].at[place], finals[piece].at[place], f_send.at[piece], f_recv.at[piece]
        )

    pair_copies = [pair_start(0), pair_start(1)]

    def head_side(step, carry):
        at = pl.ds(pl.multiple_of(step * chunk, chunk), chunk)
        mixed_grad[:, at] = left_t(wa_ref[:, 3 * head_cols :], gx_ref[:, at]).astype(jnp.bfloat16)
        return carry

    def attend(seq):
        def one(head, carry):
            at = pl.multiple_of(head * HEAD, HEAD)
            key_rows = pl.ds(at + head_cols, HEAD)
            value_rows = pl.ds(at + 2 * head_cols, HEAD)
            kept = []
            for part_q in range(2):
                here = pl.ds(seq * length + part_q * chunk, chunk)
                keys = (part_q + 1) * chunk
                span = pl.ds(seq * length, keys)
                queries = qkv_ref[pl.ds(at, HEAD), here]
                key = qkv_ref[key_rows, span]
                outer = mixed_grad[pl.ds(at, HEAD), here]
                scores = left_t(key, queries)
                key_at = lax.broadcasted_iota(jnp.int32, (keys, chunk), 0)
                query_at = lax.broadcasted_iota(jnp.int32, (keys, chunk), 1) + part_q * chunk
                shift = lse_ref[seq * heads + head, 0:1, pl.ds(part_q * chunk, chunk)]
                probs = jnp.exp(jnp.where(key_at <= query_at, scores - shift, -1e30))
                delta = jnp.sum(
                    outer.astype(jnp.float32) * att_ref[pl.ds(at, HEAD), here].astype(jnp.float32),
                    axis=0,
                    keepdims=True,
                )
                inner = left_t(qkv_ref[value_rows, span], outer)
                slope = (probs * (inner - delta)).astype(jnp.bfloat16)
                head_grad[pl.ds(at, HEAD), here] = (plain(key, slope) * HEAD**-0.5).astype(jnp.bfloat16)
                kept.append((right_t(queries, slope), right_t(outer, probs.astype(jnp.bfloat16))))
            early, late = pl.ds(seq * length, chunk), pl.ds(seq * length + chunk, chunk)
            for rows_at, index in ((key_rows, 0), (value_rows, 1)):
                second = kept[1][index]
                head_grad[rows_at, early] = (second[:, :chunk] + kept[0][index]).astype(jnp.bfloat16)
                head_grad[rows_at, late] = second[:, chunk:].astype(jnp.bfloat16)
            return carry

        lax.fori_loop(0, heads, one, 0)

    def backward(step, carry):
        at = pl.ds(pl.multiple_of(step * chunk, chunk), chunk)
        back[:, at] = plain(wa_ref[:, : 3 * head_cols], head_grad[:, at]).astype(jnp.bfloat16)
        return carry

    out_copies = []
    p_copies = [None] * 3
    for seq in range(seqs):
        lax.fori_loop(2 * seq, 2 * seq + 2, head_side, 0)
        attend(seq)
        lax.fori_loop(2 * seq, 2 * seq + 2, backward, 0)
        at = pl.ds(seq * length, length)
        out_copies.append(
            [
                send(
                    "row",
                    peer,
                    back.at[rows_of(peer, share), at],
                    got.at[seq, step],
                    r_send.at[seq, step],
                    r_recv.at[seq, step],
                )
                for step, peer in enumerate(row_peers)
            ]
        )
        if seq == 0:
            for piece in range(2):
                p_copies[piece] = pair_finish(piece, pair_copies[piece])
    block = width // 4

    def weight(step, carry):
        place = pl.ds(pl.multiple_of(step * block, block), block)
        da_ref[place, : 3 * head_cols] = right_t(ln_ref[place, :], head_grad[...]).astype(jnp.bfloat16)
        da_ref[place, 3 * head_cols :] = right_t(gx_ref[place, :], att_ref[...]).astype(jnp.bfloat16)
        return carry

    lax.fori_loop(0, 4, weight, 0)
    pair_copies.append(pair_start(2))
    tip_own[...] = jnp.zeros_like(tip_own)
    tip_own[:, : up_ref.shape[1]] = up_ref[...]
    tip_own[:, up_ref.shape[1] : up_ref.shape[1] + 3 * head_cols] = right_t(
        jnp.ones((8, tokens), jnp.bfloat16), head_grad[...]
    )
    keep(small_ref, small_all.at[row], m_recv.at[row])
    keep(tip_own, tip_all.at[row], t_recv.at[row])
    m_copies = [
        send("row", peer, small_ref, small_all.at[row], m_send.at[step], m_recv.at[row])
        for step, peer in enumerate(row_peers)
    ] + [
        send("row", peer, tip_own, tip_all.at[row], t_send.at[step], t_recv.at[row])
        for step, peer in enumerate(row_peers)
    ]
    z_copies = [line_start(0), line_start(1)]
    for group in out_copies:
        for copy in group:
            copy.wait_recv()
    gain = vcol_ref[slab, 0:1]
    a_own[...] = jnp.zeros_like(a_own)
    stat_own[...] = jnp.zeros_like(stat_own)
    scale_sum, shift_sum = 0.0, 0.0
    saved = []
    for seq in range(seqs):
        at = pl.ds(seq * length, length)
        grad = back[slab, at].astype(jnp.float32)
        for step in range(rows - 1):
            grad = grad + got[seq, step].astype(jnp.float32)
        normal = (x_ref[:, at].astype(jnp.float32) - stat_ref[0:1, at]) * stat_ref[1:2, at]
        scaled = grad * gain
        stat_own[0:1, at] = jnp.sum(scaled, axis=0, keepdims=True)
        stat_own[1:2, at] = jnp.sum(scaled * normal, axis=0, keepdims=True)
        saved.append((scaled, normal))
        scale_sum = scale_sum + grad * normal
        shift_sum = shift_sum + grad
    keep(stat_own, stat_all.at[row], s_recv.at[row])
    s_copies = [
        send("row", peer, stat_own, stat_all.at[row], s_send.at[step], s_recv.at[row])
        for step, peer in enumerate(row_peers)
    ]
    p_copies[2] = pair_finish(2, pair_copies[2])
    for step, peer in enumerate(row_peers):
        y_copies[step].wait_recv()
    total = y_ref[slab, :].astype(jnp.float32)
    for step in range(rows - 1):
        total = total + y_got[step].astype(jnp.float32)
    out_ref[...] = total.astype(jnp.bfloat16)
    wait_recv_all(small_ref, m_recv, rows)
    wait_recv_all(tip_own, t_recv, rows)
    total = small_all[0]
    for index in range(1, rows):
        total = total + small_all[index]
    a_own[:, :width] = total
    a_own[0:1, width : width + share] = lane_sums(scale_sum)[0:1]
    a_own[1:2, width : width + share] = lane_sums(shift_sum)[0:1]
    keep(a_own, a_all.at[col], n_recv.at[0, col])
    keep(tip_all.at[col], b_all.at[col], n_recv.at[1, col])
    n_copies = [
        send("col", peer, a_own, a_all.at[col], n_send.at[0, step], n_recv.at[0, col])
        for step, peer in enumerate(col_peers)
    ] + [
        send("col", peer, tip_all.at[peer], b_all.at[col], n_send.at[1, step], n_recv.at[1, col])
        for step, peer in enumerate(col_peers)
    ]
    wait_recv_all(stat_own, s_recv, rows)
    total = stat_all[0]
    for index in range(1, rows):
        total = total + stat_all[index]
    total = total * (1.0 / width)
    for seq in range(seqs):
        at = pl.ds(seq * length, length)
        scaled, normal = saved[seq]
        first, second = total[0:1, seq * length : (seq + 1) * length], total[1:2, seq * length : (seq + 1) * length]
        result = stat_ref[1:2, at] * (scaled - first - normal * second)
        gin_ref[:, at] = (gx_ref[slab, at].astype(jnp.float32) + result).astype(jnp.bfloat16)
    z_copies.append(line_start(2))
    wait_recv_all(a_own, n_recv.at[0], cols)
    wait_recv_all(tip_own, n_recv.at[1], cols)
    first, second = a_all[0], b_all[0]
    for index in range(1, cols):
        first, second = first + a_all[index], second + b_all[index]
    a_sum[...] = first
    b_sum[...] = second
    e_copies = [
        send("dp", twin, a_sum, a_pair, e_send.at[0], e_recv.at[0]),
        send("dp", twin, b_sum, b_pair, e_send.at[1], e_recv.at[1]),
    ]
    f_copies = [line_finish(0), line_finish(1)]
    for copy in e_copies:
        copy.wait()
    a_ref[...] = a_sum[...] + a_pair[...]
    b_ref[...] = b_sum[...] + b_pair[...]
    f_copies.append(line_finish(2))
    for copy in f_copies:
        copy.wait()
    for group in [y_copies, m_copies, n_copies, s_copies] + out_copies + pair_copies + p_copies + z_copies:
        for copy in group:
            copy.wait_send()


def leave(x, gx, y, wa, qkv, att, lse, ln, stat, vcol, small, up, du, dd):
    share, tokens = x.shape
    rows, cols = lax.axis_size("row"), lax.axis_size("col")
    width = gx.shape[0]
    head_cols = att.shape[0]
    seqs = tokens // LENGTH
    half = share // 2
    low, full = jnp.bfloat16, jnp.float32
    a_lanes = -(-(width + share) // 128) * 128
    b_lanes = -(-(up.shape[1] + 3 * head_cols) // 128) * 128
    shapes = [
        ((share, tokens), low),
        ((share, tokens), low),
        ((share, du.shape[1]), full),
        ((share, dd.shape[1]), full),
        ((share, wa.shape[1]), full),
        ((8, a_lanes), full),
        ((8, b_lanes), full),
    ]
    return pl.pallas_call(
        functools.partial(leave_kernel, seqs),
        out_shape=[jax.ShapeDtypeStruct(*shape) for shape in shapes],
        in_specs=[pl.BlockSpec(memory_space=pltpu.VMEM)] * 14,
        out_specs=[pl.BlockSpec(memory_space=pltpu.VMEM)] * len(shapes),
        scratch_shapes=[
            pltpu.VMEM((rows - 1, share, tokens), low),
            pltpu.VMEM((width, tokens), low),
            pltpu.VMEM((head_cols, tokens), low),
            pltpu.VMEM((3 * head_cols, tokens), low),
            pltpu.VMEM((seqs, rows - 1, share, LENGTH), low),
            pltpu.VMEM((8, tokens), full),
            pltpu.VMEM((rows, 8, tokens), full),
            pltpu.VMEM((width, wa.shape[1]), low),
            pltpu.VMEM((3, rows, half, wa.shape[1]), low),
            pltpu.VMEM((3, rows, half, wa.shape[1]), low),
            pltpu.VMEM((3, rows, half, wa.shape[1]), low),
            pltpu.VMEM((3, cols, half, wa.shape[1]), low),
            pltpu.VMEM((rows, 8, width), full),
            pltpu.VMEM((8, b_lanes), full),
            pltpu.VMEM((rows, 8, b_lanes), full),
            pltpu.VMEM((8, a_lanes), full),
            pltpu.VMEM((cols, 8, a_lanes), full),
            pltpu.VMEM((cols, 8, b_lanes), full),
            pltpu.VMEM((8, a_lanes), full),
            pltpu.VMEM((8, b_lanes), full),
            pltpu.VMEM((8, a_lanes), full),
            pltpu.VMEM((8, b_lanes), full),
            dma(rows - 1),
            dma(rows - 1),
            dma(seqs, rows - 1),
            dma(seqs, rows - 1),
            dma(rows - 1),
            dma(rows),
            dma(3, rows),
            dma(3, rows),
            dma(3, rows - 1),
            dma(3, rows),
            dma(3, cols - 1),
            dma(3, cols),
            dma(3),
            dma(3),
            dma(rows - 1),
            dma(rows),
            dma(rows - 1),
            dma(rows),
            dma(2, cols - 1),
            dma(2, cols),
            dma(2),
            dma(2),
        ],
        compiler_params=pltpu.CompilerParams(
            collective_id=2, has_side_effects=True, vmem_limit_bytes=BIG
        ),
    )(x, gx, y, wa, qkv, att, lse, ln, stat, vcol, small, up, du, dd)


def square_body(
    block_input, norm_gains, row_biases, w_qkv, qv_bias, w_out, w_up, up_bias, w_down, cotangent
):
    share = block_input.shape[0]
    head_cols = w_qkv.shape[2]
    hidden = w_up.shape[1]
    lanes = -(-share // 128) * 128
    vec = jnp.concatenate([norm_gains, row_biases], axis=0)
    vec = jnp.pad(vec, ((0, 2), (0, lanes - share)))
    tip = jnp.concatenate(
        [jnp.pad(qv_bias, ((0, 0), (0, lanes - head_cols))), up_bias.reshape(-1, lanes)], axis=0
    )
    tip = jnp.pad(tip, ((0, -tip.shape[0] % 8), (0, 0)))
    wa = jnp.concatenate([w_qkv.reshape(share, -1), w_out.T], axis=1)
    (x_all, c_all, wa_all, wu_all, wd_all, ln, qkv, att, lse, stat, x1, l2, vcol, tcol) = enter(
        block_input, cotangent, vec, tip, wa, w_up, w_down
    )
    gx, y, du, dd, small, up = mlp(l2, c_all, x1, wu_all, wd_all, vcol, tcol)
    out, gin, gu, gd, ga, a_sum, b_sum = leave(
        block_input, gx, y, wa_all, qkv, att, lse, ln, stat, vcol, small, up, du, dd
    )
    width = c_all.shape[0]
    start = lax.axis_index("row") * share
    wide = lax.dynamic_slice_in_dim(a_sum, start, share, axis=1)
    near = a_sum[:, width : width + share]
    gains = jnp.concatenate([near[0:1], wide[0:1]], axis=0)
    biases = jnp.concatenate([near[1:2], wide[1:4]], axis=0)
    grad_qv = jnp.stack(
        [b_sum[0, hidden : hidden + head_cols], b_sum[0, hidden + 2 * head_cols : hidden + 3 * head_cols]]
    )
    return (
        out,
        gin,
        gains,
        biases,
        ga[:, : 3 * head_cols].reshape(w_qkv.shape),
        grad_qv,
        ga[:, 3 * head_cols :].T,
        gu,
        b_sum[0, :hidden],
        gd,
    )


def fits(mesh):
    sizes = mesh.shape
    return sizes["row"] == sizes["col"] and sizes["dp"] == 2 and D % (4 * sizes["row"]) == 0


def solution(mesh):
    in_specs = (
        P("row", ("dp", "col")),
        P(None, "row"),
        P(None, "row"),
        P("row", None, "col"),
        P(None, "col"),
        P("col", "row"),
        P("row", "col"),
        P("col"),
        P("row", "col"),
        P("row", ("dp", "col")),
    )
    out_specs = (
        P("row", ("dp", "col")),
        P("row", ("dp", "col")),
        P(None, "row"),
        P(None, "row"),
        P("row", None, "col"),
        P(None, "col"),
        P("col", "row"),
        P("row", "col"),
        P("col"),
        P("row", "col"),
    )
    chosen = square_body if fits(mesh) else body
    return jax.shard_map(chosen, mesh=mesh, in_specs=in_specs, out_specs=out_specs, check_vma=False)
```

```python
import functools

import jax
import jax.numpy as jnp
from jax import lax
from jax.experimental import pallas as pl
from jax.experimental.pallas import tpu as pltpu
from jax.sharding import PartitionSpec as P

D = 768
HEAD = 64
LENGTH = 512


EPSILON = 1e-05
GELU_COEF = 0.7978845608028654


def gelu_tanh(values):
    return (
        0.5 * values * (1.0 + jnp.tanh(GELU_COEF * (values + 0.044715 * values * values * values)))
    )


def multiply(rows, weight, flipped):
    if flipped:
        return lax.dot_general(
            rows, weight, (((1,), (1,)), ((), ())), preferred_element_type=jnp.float32
        )
    return jnp.dot(rows, weight, preferred_element_type=jnp.float32)


def contract_tokens(left, right):
    return lax.dot_general(
        left, right, (((0,), (0,)), ((), ())), preferred_element_type=jnp.float32
    )


def swap_kernel(axis_name, count, shared, x_ref, o_ref, send_sem, recv_sem, own_sem):
    me = lax.axis_index(axis_name)
    barrier = pltpu.get_barrier_semaphore()
    peers = [lax.rem(me + step, count) for step in range(1, count)]
    for peer in peers:
        pl.semaphore_signal(
            barrier, inc=1, device_id={axis_name: peer}, device_id_type=pl.DeviceIdType.MESH
        )
    own = pltpu.make_async_copy(x_ref if shared else x_ref.at[me], o_ref.at[me], own_sem)
    own.start()
    pl.semaphore_wait(barrier, count - 1)
    copies = []
    for slot, peer in enumerate(peers):
        copy = pltpu.make_async_remote_copy(
            src_ref=x_ref if shared else x_ref.at[peer],
            dst_ref=o_ref.at[me],
            send_sem=send_sem.at[slot],
            recv_sem=recv_sem.at[slot],
            device_id={axis_name: peer},
            device_id_type=pl.DeviceIdType.MESH,
        )
        copy.start()
        copies.append(copy)
    own.wait()
    for copy in copies:
        copy.wait()


def swap(values, axis_name, shared, ident):
    count = lax.axis_size(axis_name)
    block = values.shape if shared else values.shape[1:]
    moved = values.size * values.dtype.itemsize
    return pl.pallas_call(
        functools.partial(swap_kernel, axis_name, count, shared),
        out_shape=jax.ShapeDtypeStruct((count, *block), values.dtype),
        in_specs=[pl.BlockSpec(memory_space=pltpu.VMEM)],
        out_specs=pl.BlockSpec(memory_space=pltpu.VMEM),
        scratch_shapes=[
            pltpu.SemaphoreType.DMA((count - 1,)),
            pltpu.SemaphoreType.DMA((count - 1,)),
            pltpu.SemaphoreType.DMA,
        ],
        compiler_params=pltpu.CompilerParams(collective_id=ident, has_side_effects=True),
        cost_estimate=pl.CostEstimate(
            flops=0, bytes_accessed=(20 if not shared else 60) * moved, transcendentals=0
        ),
    )(values)


def gather_async(local, axis_name):
    return lax.all_gather(local, axis_name, axis=0, tiled=True)


def scatter_sum_async(partial, axis_name):
    return lax.psum_scatter(
        partial.astype(jnp.bfloat16), axis_name, scatter_dimension=0, tiled=True
    ).astype(jnp.float32)


def gather(local, axis_name, ident):
    return swap(local, axis_name, True, ident).reshape(-1, *local.shape[1:])


def scatter_sum(partial, axis_name, ident):
    count = lax.axis_size(axis_name)
    pieces = partial.astype(jnp.bfloat16).reshape(count, -1, *partial.shape[1:])
    return jnp.sum(swap(pieces, axis_name, False, ident).astype(jnp.float32), axis=0)


def to_tokens(first, second, ident):
    rows, cols = lax.axis_size("row"), lax.axis_size("col")
    share = first.shape[0]
    block = jnp.concatenate([first.T, second.T], axis=1).reshape(rows, -1, 2 * share)
    block = swap(block, "row", False, ident)
    if rows != cols:
        moves = [(r * cols + c, c * rows + r) for r in range(rows) for c in range(cols)]
        block = lax.ppermute(block, ("row", "col"), moves)
    first = jnp.concatenate([block[r, :, :share] for r in range(rows)], axis=1)
    second = jnp.concatenate([block[r, :, share:] for r in range(rows)], axis=1)
    return first, second


def to_features(first, second, ident):
    rows, cols = lax.axis_size("row"), lax.axis_size("col")
    share = first.shape[1] // rows
    block = jnp.stack(
        [
            jnp.concatenate(
                [first[:, r * share : (r + 1) * share], second[:, r * share : (r + 1) * share]], axis=1
            )
            for r in range(rows)
        ]
    )
    if rows != cols:
        moves = [(c * rows + r, r * cols + c) for r in range(rows) for c in range(cols)]
        block = lax.ppermute(block, ("row", "col"), moves)
    block = swap(block, "row", False, ident).reshape(-1, 2 * share)
    return block[:, :share].T, block[:, share:].T


def flip(block):
    rows, cols = lax.axis_size("row"), lax.axis_size("col")
    if rows != cols:
        return block
    moves = [(r * cols + c, c * rows + r) for r in range(rows) for c in range(cols)]
    return lax.ppermute(block, ("row", "col"), moves)


def norm_forward(values, gain, bias):
    center = jnp.mean(values, axis=1, keepdims=True)
    offset = values - center
    inverse = lax.rsqrt(jnp.mean(offset * offset, axis=1, keepdims=True) + EPSILON)
    normal = offset * inverse
    return (normal * gain + bias, normal, inverse)


def norm_backward(grad, gain, normal, inverse):
    scaled = grad * gain
    first = jnp.mean(scaled, axis=1, keepdims=True)
    second = jnp.mean(scaled * normal, axis=1, keepdims=True)
    result = inverse * (scaled - first - normal * second)
    return (result, jnp.sum(grad * normal, axis=0), jnp.sum(grad, axis=0))


def causal_mask(length):
    positions = jnp.arange(length)
    return positions[None, :] <= positions[:, None]


def attention_forward(queries, keys, values):
    factor = HEAD ** (-0.5)

    def one_sequence(pieces):
        seq_q, seq_k, seq_v = pieces
        scores = (
            jnp.einsum("qhd,khd->hqk", seq_q, seq_k, preferred_element_type=jnp.float32) * factor
        )
        scores = jnp.where(causal_mask(seq_q.shape[0])[None], scores, -1e30)
        summit = jnp.max(scores, axis=-1, keepdims=True)
        expos = jnp.exp(scores - summit)
        total = jnp.sum(expos, axis=-1, keepdims=True)
        probs = (expos / total).astype(jnp.bfloat16)
        output = jnp.einsum("hqk,khd->qhd", probs, seq_v, preferred_element_type=jnp.float32)
        return (output, summit[..., 0] + jnp.log(total[..., 0]))

    return lax.map(one_sequence, (queries, keys, values))


def attention_backward(queries, keys, values, grad_out, log_sums):
    factor = HEAD ** (-0.5)

    def one_sequence(pieces):
        seq_q, seq_k, seq_v, seq_g, seq_l = pieces
        scores = (
            jnp.einsum("qhd,khd->hqk", seq_q, seq_k, preferred_element_type=jnp.float32) * factor
        )
        scores = jnp.where(causal_mask(seq_q.shape[0])[None], scores, -1e30)
        probs = jnp.exp(scores - seq_l[..., None])
        grad_v = jnp.einsum(
            "hqk,qhd->khd", probs.astype(jnp.bfloat16), seq_g, preferred_element_type=jnp.float32
        )
        grad_p = jnp.einsum("qhd,khd->hqk", seq_g, seq_v, preferred_element_type=jnp.float32)
        inner = jnp.sum(grad_p * probs, axis=-1, keepdims=True)
        grad_s = (probs * (grad_p - inner)).astype(jnp.bfloat16)
        grad_q = (
            jnp.einsum("hqk,khd->qhd", grad_s, seq_k, preferred_element_type=jnp.float32) * factor
        )
        grad_k = (
            jnp.einsum("hqk,qhd->khd", grad_s, seq_q, preferred_element_type=jnp.float32) * factor
        )
        return (grad_q, grad_k, grad_v)

    return lax.map(one_sequence, (queries, keys, values, grad_out, log_sums))


def body(
    block_input, norm_gains, row_biases, w_qkv, qv_bias, w_out, w_up, up_bias, w_down, cotangent
):
    head_cols = w_qkv.shape[2]
    square = lax.axis_size("row") == lax.axis_size("col")
    heads_axis, split_axis = ("row", "col") if square else ("col", "row")
    qv_bias, up_bias = flip(qv_bias), flip(up_bias)
    inputs, cot = to_tokens(block_input, cotangent, 0)
    inputs = inputs.astype(jnp.float32)
    vectors = swap(jnp.concatenate([norm_gains, row_biases], axis=0), "row", True, 1)
    vectors = jnp.concatenate([vectors[r] for r in range(vectors.shape[0])], axis=1)
    gains, biases = vectors[:2], vectors[2:]
    qkv_weight = gather_async(flip(w_qkv.reshape(w_qkv.shape[0], -1)), split_axis)
    rest = gather_async(flip(jnp.concatenate([w_out.T, w_up, w_down], axis=1)), split_axis)
    width = w_up.shape[1]
    out_t = rest[:, :head_cols]
    up = rest[:, head_cols : head_cols + width]
    down = rest[:, head_cols + width :]

    normed_one, normal_one, inverse_one = norm_forward(inputs, gains[0], biases[0])
    source_one = gather(normed_one.astype(jnp.bfloat16), heads_axis, 2)
    qkv_sum = multiply(source_one, qkv_weight, False)
    rows_here = qkv_sum.shape[0]
    qkv_sum = qkv_sum.reshape(rows_here, 3, head_cols)
    shape_four = (rows_here // LENGTH, LENGTH, head_cols // HEAD, HEAD)
    queries = (qkv_sum[:, 0] + qv_bias[0]).astype(jnp.bfloat16).reshape(shape_four)
    keys_all = qkv_sum[:, 1].astype(jnp.bfloat16).reshape(shape_four)
    values_all = (qkv_sum[:, 2] + qv_bias[1]).astype(jnp.bfloat16).reshape(shape_four)
    attended, log_sums = attention_forward(queries, keys_all, values_all)
    attended_low = attended.reshape(rows_here, head_cols).astype(jnp.bfloat16)
    middle = inputs + scatter_sum(multiply(attended_low, out_t, True), heads_axis, 3) + biases[2]
    normed_two, normal_two, inverse_two = norm_forward(middle, gains[1], biases[1])
    source_two = gather(normed_two.astype(jnp.bfloat16), heads_axis, 4)
    cot_all = gather_async(cot, heads_axis)
    before = multiply(source_two, up, False) + up_bias
    hidden_low = gelu_tanh(before).astype(jnp.bfloat16)
    grad_hidden = multiply(cot_all, down, False)
    grad_before = jax.vjp(gelu_tanh, before)[1](grad_hidden)[0].astype(jnp.bfloat16)
    grad_normed_two = scatter_sum(multiply(grad_before, up, True), heads_axis, 5)
    output = middle + scatter_sum_async(multiply(hidden_low, down, True), heads_axis) + biases[3]
    grad_w_down = contract_tokens(cot_all, hidden_low)
    grad_up_bias = jnp.sum(grad_before.astype(jnp.float32), axis=0)
    grad_w_up = contract_tokens(source_two, grad_before)
    grad_out = cot.astype(jnp.float32)
    back_two, gain_two, shift_two = norm_backward(
        grad_normed_two, gains[1], normal_two, inverse_two
    )
    grad_middle = grad_out + back_two
    grad_middle_low = grad_middle.astype(jnp.bfloat16)
    grad_out_bias = jnp.sum(grad_middle_low.astype(jnp.float32), axis=0)
    grad_down_bias = jnp.sum(grad_out, axis=0)
    grad_middle_all = gather(grad_middle_low, heads_axis, 6)
    grad_att_low = multiply(grad_middle_all, out_t, False).astype(jnp.bfloat16).reshape(shape_four)
    grad_w_out_t = contract_tokens(grad_middle_all, attended_low)
    grad_q, grad_k, grad_v = attention_backward(
        queries, keys_all, values_all, grad_att_low, log_sums
    )
    grad_q = grad_q.reshape(rows_here, head_cols).astype(jnp.bfloat16)
    grad_k = grad_k.reshape(rows_here, head_cols).astype(jnp.bfloat16)
    grad_v = grad_v.reshape(rows_here, head_cols).astype(jnp.bfloat16)
    grad_qkv_low = jnp.concatenate([grad_q, grad_k, grad_v], axis=1)
    grad_qv = jnp.stack(
        [jnp.sum(grad_q.astype(jnp.float32), axis=0), jnp.sum(grad_v.astype(jnp.float32), axis=0)]
    )
    grad_normed_one = scatter_sum(multiply(grad_qkv_low, qkv_weight, True), heads_axis, 7)
    grad_w_qkv = contract_tokens(source_one, grad_qkv_low)
    back_one, gain_one, shift_one = norm_backward(
        grad_normed_one, gains[0], normal_one, inverse_one
    )
    grad_input = grad_middle + back_one

    mlp_sum = scatter_sum_async(jnp.concatenate([grad_w_up, grad_w_down], axis=1), split_axis)
    mlp_sum = flip(lax.psum(mlp_sum.astype(jnp.bfloat16), "dp")).astype(jnp.float32)
    att_sum = scatter_sum(jnp.concatenate([grad_w_qkv, grad_w_out_t], axis=1), split_axis, 8)
    att_sum = jnp.sum(
        swap(flip(att_sum.astype(jnp.bfloat16)), "dp", True, 9).astype(jnp.float32), axis=0
    )
    sum_up = mlp_sum[:, :width]
    sum_down = mlp_sum[:, width:]
    sum_qkv = att_sum[:, : 3 * head_cols].reshape(w_qkv.shape)
    sum_out = att_sum[:, 3 * head_cols :].T
    features = gains.shape[1]
    longest = max(features, width, 2 * head_cols)
    small = [gain_one, gain_two, shift_one, shift_two, grad_out_bias, grad_down_bias]
    small = small + [grad_up_bias, grad_qv.reshape(-1)]
    small = jnp.stack([jnp.pad(row, (0, longest - row.shape[0])) for row in small])
    small = jnp.sum(swap(small, "dp", True, 10), axis=0)
    small = jnp.sum(swap(small, split_axis, True, 11), axis=0)
    projected = flip(small[6:])
    sum_upb = projected[0, :width]
    sum_qv = projected[1, : 2 * head_cols].reshape(2, head_cols)
    share = norm_gains.shape[1]
    small = jnp.sum(swap(small[:6], heads_axis, True, 12), axis=0)
    small = lax.dynamic_slice_in_dim(small, lax.axis_index("row") * share, share, axis=1)
    output_t, grad_input_t = to_features(
        output.astype(jnp.bfloat16), grad_input.astype(jnp.bfloat16), 13
    )
    return (
        output_t,
        grad_input_t,
        small[:2],
        small[2:],
        sum_qkv,
        sum_qv,
        sum_out,
        sum_up,
        sum_upb,
        sum_down,
    )


MESH = pl.DeviceIdType.MESH
BIG = 60 * 1024 * 1024


def send(axis_name, peer, source, target, send_sem, recv_sem):
    copy = pltpu.make_async_remote_copy(
        src_ref=source,
        dst_ref=target,
        send_sem=send_sem,
        recv_sem=recv_sem,
        device_id={axis_name: peer},
        device_id_type=MESH,
    )
    copy.start()
    return copy


def keep(source, target, sem):
    copy = pltpu.make_async_copy(source, target, sem)
    copy.start()
    return copy


def others(axis_name):
    count = lax.axis_size(axis_name)
    me = lax.axis_index(axis_name)
    return me, [lax.rem(me + step, count) for step in range(1, count)]


def meet():
    barrier = pltpu.get_barrier_semaphore()
    total = 0
    for name in ("row", "col", "dp"):
        _, peers = others(name)
        for peer in peers:
            pl.semaphore_signal(barrier, inc=1, device_id={name: peer}, device_id_type=MESH)
        total += len(peers)
    pl.semaphore_wait(barrier, total)


def rows_of(index, size):
    return pl.ds(pl.multiple_of(index * size, size), size)


def left_t(weight, acts):
    return lax.dot_general(weight, acts, (((0,), (0,)), ((), ())), preferred_element_type=jnp.float32)


def right_t(left, right):
    return lax.dot_general(left, right, (((1,), (1,)), ((), ())), preferred_element_type=jnp.float32)


def plain(left, right):
    return jnp.dot(left, right, preferred_element_type=jnp.float32)


def lane_sums(values):
    ones = jnp.ones((8, values.shape[1]), jnp.float32)
    return lax.dot_general(
        ones,
        values,
        (((1,), (1,)), ((), ())),
        precision=lax.Precision.HIGHEST,
        preferred_element_type=jnp.float32,
    )


def spread_weight(stage, own_ref, full_ref, buf, piece, sems):
    half = own_ref.shape[0] // 2
    core = lax.axis_index("dp")
    row, row_peers = others("row")
    col, col_peers = others("col")
    other = 1 - core
    z_send, z_recv, p_send, p_recv, c_send, c_recv = (sem.at[piece] for sem in sems)
    slots = buf.at[piece]
    size = 2 * half

    def rows_at(index, which):
        return pl.ds(pl.multiple_of(index * size + which * half, half), half)

    if stage == 0:
        mine = own_ref.at[pl.ds(pl.multiple_of(core * half, half), half)]
        copies = [keep(mine, slots.at[col], z_recv.at[col])]
        for step, peer in enumerate(col_peers):
            copies.append(send("col", peer, mine, slots.at[col], z_send.at[step], z_recv.at[col]))
        return copies
    if stage == 1:
        place = rows_at(row, core)
        copies = [keep(slots.at[row], full_ref.at[place], p_recv.at[row])]
        for step, peer in enumerate(row_peers):
            copies.append(
                send("row", peer, slots.at[peer], full_ref.at[place], p_send.at[step], p_recv.at[row])
            )
        return copies
    copies = []
    for index in range(len(row_peers) + 1):
        place = rows_at(index, core)
        copies.append(
            send("dp", other, full_ref.at[place], full_ref.at[place], c_send.at[index], c_recv.at[index])
        )
    return copies


def wait_recv_all(block, sems, count):
    for index in range(count):
        pltpu.make_async_copy(block, block, sems.at[index]).wait()


def crossings():
    row = lax.axis_index("row")
    near = row + 1 - 2 * lax.rem(row, 2)
    side = lax.rem(row + 2, 4)
    return row, near, side, 3 - row


def gather_one(source, spot, send_sem, recv_sem):
    row, near, side, _ = crossings()
    return [
        send("row", near, source, spot(row), send_sem.at[0], recv_sem.at[0]),
        send("row", side, source, spot(row), send_sem.at[1], recv_sem.at[1]),
    ]


def gather_two(copies, half_spot, send_sem, recv_sem):
    row, near, side, _ = crossings()
    copies[0].wait_recv()
    first = half_spot(near, 0)
    copies.append(send("row", side, first, first, send_sem.at[2], recv_sem.at[2]))
    copies[1].wait_recv()
    second = half_spot(side, 1)
    copies.append(send("row", near, second, second, send_sem.at[3], recv_sem.at[3]))


def gather_end(copies):
    copies[2].wait_recv()
    copies[3].wait_recv()


def reduce_one(part, got, send_sem, recv_sem):
    _, near, side, far = crossings()
    moves = ((near, near, 0), (near, far, 0), (side, side, 1), (side, far, 1))
    order = (1, 0, 3, 2)
    copies = [None] * 4
    for index in order:
        peer, block, half = moves[index]
        copies[index] = send(
            "row", peer, part(block, half), got.at[index], send_sem.at[index], recv_sem.at[index]
        )
    return copies


def reduce_two(copies, part, got, middle, send_sem, recv_sem):
    _, near, side, _ = crossings()
    for slot, index, peer, half in ((0, 1, side, 0), (1, 3, near, 1)):
        copies[index].wait_recv()
        total = part(peer, half)[...].astype(jnp.float32) + got[index].astype(jnp.float32)
        middle[slot] = total.astype(jnp.bfloat16)
        copies.append(
            send("row", peer, middle.at[slot], got.at[4 + slot], send_sem.at[4 + slot], recv_sem.at[4 + slot])
        )


def reduce_end(copies, part, got):
    row = lax.axis_index("row")
    for index in (0, 2, 4, 5):
        copies[index].wait_recv()
    halves = []
    for half, one, two in ((0, 0, 4), (1, 2, 5)):
        halves.append(
            part(row, half)[...].astype(jnp.float32)
            + got[one].astype(jnp.float32)
            + got[two].astype(jnp.float32)
        )
    return jnp.concatenate(halves, axis=0)


def sent(*groups):
    for copies in groups:
        for copy in copies:
            copy.wait_send()


def enter_kernel(
    seqs,
    x_ref,
    c_ref,
    gains_ref,
    biases_ref,
    tip_ref,
    upb_ref,
    wq_ref,
    wo_ref,
    wu_ref,
    wd_ref,
    x_all,
    c_all,
    wa_all,
    wu_all,
    wd_all,
    ln_ref,
    qkv_ref,
    att_ref,
    lse_ref,
    stat_ref,
    x1_ref,
    l2_ref,
    vcol_ref,
    tcol_ref,
    wa_ref,
    vec_own,
    tip_own,
    vec_all,
    tip_all,
    zbuf,
    part,
    got,
    middle_buf,
    x_send,
    x_recv,
    c_send,
    c_recv,
    v_send,
    v_recv,
    t_send,
    t_recv,
    z_send,
    z_recv,
    p_send,
    p_recv,
    d_send,
    d_recv,
    r_send,
    r_recv,
    a_send,
    a_recv,
):
    share = x_ref.shape[0]
    length = x_ref.shape[1] // seqs
    width = x_all.shape[0]
    row, row_peers = others("row")
    col, col_peers = others("col")
    rows = len(row_peers) + 1
    head_cols = wo_ref.shape[0]
    heads = head_cols // HEAD
    piece = length // rows
    sems = (z_send, z_recv, p_send, p_recv, d_send, d_recv)
    slab = rows_of(row, share)
    for index in range(3):
        wa_ref[:, index * head_cols : (index + 1) * head_cols] = wq_ref[index]
    wa_ref[:, 3 * head_cols :] = wo_ref[...].T
    vec_own[...] = jnp.zeros_like(vec_own)
    vec_own[0:2, :share] = gains_ref[...]
    vec_own[2:6, :share] = biases_ref[...]
    tip_own[...] = jnp.zeros_like(tip_own)
    tip_own[0:2, :head_cols] = tip_ref[...]
    lanes = tip_own.shape[1]
    for index in range(upb_ref.shape[1] // lanes):
        tip_own[2 + index : 3 + index, :] = upb_ref[:, index * lanes : (index + 1) * lanes]
    meet()
    keep(vec_own, vec_all.at[row], v_recv.at[row])
    keep(tip_own, tip_all.at[col], t_recv.at[col])
    z_copies = [spread_weight(0, wa_ref, wa_all, zbuf, 0, sems)]
    vec_copies = [
        send("row", peer, vec_own, vec_all.at[row], v_send.at[step], v_recv.at[row])
        for step, peer in enumerate(row_peers)
    ]
    tip_copies = [
        send("col", peer, tip_own, tip_all.at[col], t_send.at[step], t_recv.at[col])
        for step, peer in enumerate(col_peers)
    ]

    def slab_spot(ref, at):
        return lambda index: ref.at[rows_of(index, share), at]

    def slab_half(ref, at):
        step = share // 2
        return lambda index, half: ref.at[
            pl.ds(pl.multiple_of(index * share + half * step, step), step), at
        ]

    spans = [pl.ds(seq * length, length) for seq in range(seqs)]
    x_copies = [
        gather_one(x_ref.at[:, at], slab_spot(x_all, at), x_send.at[seq], x_recv.at[seq])
        for seq, at in enumerate(spans)
    ]
    x_all[slab, :] = x_ref[...]
    c_all[slab, :] = c_ref[...]
    wait_recv_all(vec_all.at[0], v_recv, rows)
    for index in range(rows):
        flipped = vec_all[index].T
        vcol_ref[index * share : (index + 1) * share, :] = flipped[:share]
    wait_recv_all(tip_all.at[0], t_recv, len(col_peers) + 1)
    tip = tip_all[row].T
    bias_q, bias_v = tip[:head_cols, 0:1], tip[:head_cols, 1:2]
    for index in range(tcol_ref.shape[0] // lanes):
        tcol_ref[index * lanes : (index + 1) * lanes, :] = jnp.broadcast_to(
            tip[:, 2 + index : 3 + index], (lanes, 8)
        )
    wait_recv_all(zbuf.at[0, 0], z_recv.at[0], len(col_peers) + 1)
    p_copies = [spread_weight(1, wa_ref, wa_all, zbuf, 0, sems)]
    z_copies.append(spread_weight(0, wu_ref, wu_all, zbuf, 1, sems))
    z_copies.append(spread_weight(0, wd_ref, wd_all, zbuf, 2, sems))
    for seq, at in enumerate(spans):
        gather_two(x_copies[seq], slab_half(x_all, at), x_send.at[seq], x_recv.at[seq])
    chunk = length // 2

    def first_norm(step, carry):
        cols = pl.ds(pl.multiple_of(step * chunk, chunk), chunk)
        values = x_all[:, cols].astype(jnp.float32)
        center = jnp.mean(values, axis=0, keepdims=True)
        offset = values - center
        inverse = lax.rsqrt(jnp.mean(offset * offset, axis=0, keepdims=True) + EPSILON)
        normed = offset * inverse * vcol_ref[:, 0:1] + vcol_ref[:, 2:3]
        ln_ref[:, cols] = normed.astype(jnp.bfloat16)
        stat_ref[0:1, cols] = center
        stat_ref[1:2, cols] = inverse
        return carry

    gather_end(x_copies[0])
    lax.fori_loop(0, 2, first_norm, 0)
    wait_recv_all(zbuf.at[0, 0], p_recv.at[0], rows)
    d_copies = [spread_weight(2, wa_ref, wa_all, zbuf, 0, sems)]
    c_copies = [
        gather_one(c_ref.at[:, at], slab_spot(c_all, at), c_send.at[seq], c_recv.at[seq])
        for seq, at in enumerate(spans)
    ]
    for copy in d_copies[0]:
        copy.wait_recv()

    def project(step, carry):
        cols = pl.ds(pl.multiple_of(step * chunk, chunk), chunk)
        acts = ln_ref[:, cols]
        mixed = left_t(wa_all[:, : 3 * head_cols], acts)
        qkv_ref[:head_cols, cols] = ((mixed[:head_cols] + bias_q) * HEAD**-0.5).astype(jnp.bfloat16)
        qkv_ref[head_cols : 2 * head_cols, cols] = mixed[head_cols : 2 * head_cols].astype(jnp.bfloat16)
        qkv_ref[2 * head_cols :, cols] = (mixed[2 * head_cols :] + bias_v).astype(jnp.bfloat16)
        return carry

    def attend(seq):
        def one(head, carry):
            at = pl.multiple_of(head * HEAD, HEAD)
            for part_q in range(2):
                cols = pl.ds(seq * length + part_q * chunk, chunk)
                keys = (part_q + 1) * chunk
                span = pl.ds(seq * length, keys)
                queries = qkv_ref[pl.ds(at, HEAD), cols]
                scores = left_t(qkv_ref[pl.ds(at + head_cols, HEAD), span], queries)
                key_at = lax.broadcasted_iota(jnp.int32, (keys, chunk), 0)
                query_at = lax.broadcasted_iota(jnp.int32, (keys, chunk), 1) + part_q * chunk
                scores = jnp.where(key_at <= query_at, scores, -1e30)
                summit = jnp.max(scores, axis=0, keepdims=True)
                expos = jnp.exp(scores - summit)
                total = jnp.sum(expos, axis=0, keepdims=True)
                mixed = plain(qkv_ref[pl.ds(at + 2 * head_cols, HEAD), span], expos.astype(jnp.bfloat16))
                att_ref[pl.ds(at, HEAD), cols] = (mixed / total).astype(jnp.bfloat16)
                lse_ref[seq * heads + head, :, pl.ds(part_q * chunk, chunk)] = jnp.broadcast_to(
                    summit + jnp.log(total), (8, chunk)
                )
            return carry

        lax.fori_loop(0, heads, one, 0)

    step_rows = width // 2

    def part_of(seq):
        return lambda index, half: part.at[seq, index, half * step_rows : (half + 1) * step_rows]

    def own_at(seq):
        return lambda index: l2_ref.at[:, pl.ds(pl.multiple_of(seq * length + index * piece, piece), piece)]

    def own_half(seq):
        return lambda index, half: l2_ref.at[
            half * step_rows : (half + 1) * step_rows,
            pl.ds(pl.multiple_of(seq * length + index * piece, piece), piece),
        ]

    out_copies = []
    weights = ((wu_ref, wu_all), (wd_ref, wd_all))
    for seq in range(seqs):
        lax.fori_loop(2 * seq, 2 * seq + 2, project, 0)
        attend(seq)
        mixed = plain(wa_all[:, 3 * head_cols :], att_ref[:, seq * length : (seq + 1) * length])
        for index in range(rows):
            part[seq, index] = mixed[:, index * piece : (index + 1) * piece].astype(jnp.bfloat16)
        out_copies.append(reduce_one(part_of(seq), got.at[seq], r_send.at[seq], r_recv.at[seq]))
        if seq == 0:
            gather_end(x_copies[1])
            lax.fori_loop(2, 4, first_norm, 0)
    reduce_two(out_copies[0], part_of(0), got.at[0], middle_buf.at[0], r_send.at[0], r_recv.at[0])
    for index, (own, full) in enumerate(weights):
        wait_recv_all(zbuf.at[0, 0], z_recv.at[1 + index], len(col_peers) + 1)
        p_copies.append(spread_weight(1, own, full, zbuf, 1 + index, sems))
    reduce_two(out_copies[1], part_of(1), got.at[1], middle_buf.at[1], r_send.at[1], r_recv.at[1])
    gather_two(c_copies[0], slab_half(c_all, spans[0]), c_send.at[0], c_recv.at[0])
    gather_two(c_copies[1], slab_half(c_all, spans[1]), c_send.at[1], c_recv.at[1])
    gather_copies = []
    for seq in range(seqs):
        total = reduce_end(out_copies[seq], part_of(seq), got.at[seq])
        own = pl.ds(pl.multiple_of(seq * length + row * piece, piece), piece)
        middle = x_all[:, own].astype(jnp.float32) + total + vcol_ref[:, 4:5]
        x1_ref[:, seq * piece : (seq + 1) * piece] = middle
        center = jnp.mean(middle, axis=0, keepdims=True)
        offset = middle - center
        inverse = lax.rsqrt(jnp.mean(offset * offset, axis=0, keepdims=True) + EPSILON)
        l2_ref[:, own] = (offset * inverse * vcol_ref[:, 1:2] + vcol_ref[:, 3:4]).astype(jnp.bfloat16)
        gather_copies.append(
            gather_one(own_at(seq)(row), own_at(seq), a_send.at[seq], a_recv.at[seq])
        )
    for seq in range(seqs):
        gather_two(gather_copies[seq], own_half(seq), a_send.at[seq], a_recv.at[seq])
    for index, (own, full) in enumerate(weights):
        wait_recv_all(zbuf.at[0, 0], p_recv.at[1 + index], rows)
        d_copies.append(spread_weight(2, own, full, zbuf, 1 + index, sems))
    for copies in gather_copies + c_copies:
        gather_end(copies)
    for copies in d_copies[1:]:
        for copy in copies:
            copy.wait_recv()
    sent(vec_copies, tip_copies, *c_copies, *x_copies, *out_copies, *gather_copies, *d_copies)
    sent(*[copies[1:] for copies in z_copies + p_copies])


def dma(*shape):
    return pltpu.SemaphoreType.DMA(shape)


def enter(x, cot, gains, biases, tip, upb, wq, wo, wu, wd):
    share, tokens = x.shape
    rows, cols = lax.axis_size("row"), lax.axis_size("col")
    width = share * rows
    head_cols = wo.shape[0]
    mixed = 3 * head_cols + share
    seqs = tokens // LENGTH
    heads = head_cols // HEAD
    piece = LENGTH // rows
    lanes = -(-share // 128) * 128
    tips = -(-(2 + upb.shape[1] // lanes) // 8) * 8
    low, full = jnp.bfloat16, jnp.float32
    shapes = [
        ((width, tokens), low),
        ((width, tokens), low),
        ((width, mixed), low),
        ((width, wu.shape[1]), low),
        ((width, wd.shape[1]), low),
        ((width, tokens), low),
        ((3 * head_cols, tokens), low),
        ((head_cols, tokens), low),
        ((seqs * heads, 8, LENGTH), full),
        ((8, tokens), full),
        ((width, seqs * piece), full),
        ((width, tokens), low),
        ((width, 8), full),
        ((wu.shape[1], 8), full),
    ]
    return pl.pallas_call(
        functools.partial(enter_kernel, seqs),
        out_shape=[jax.ShapeDtypeStruct(*shape) for shape in shapes],
        in_specs=[pl.BlockSpec(memory_space=pltpu.VMEM)] * 10,
        out_specs=[pl.BlockSpec(memory_space=pltpu.VMEM)] * len(shapes),
        scratch_shapes=[
            pltpu.VMEM((share, mixed), low),
            pltpu.VMEM((8, lanes), full),
            pltpu.VMEM((tips, lanes), full),
            pltpu.VMEM((rows, 8, lanes), full),
            pltpu.VMEM((cols, tips, lanes), full),
            pltpu.VMEM((3, cols, share // 2, mixed), low),
            pltpu.VMEM((seqs, rows, width, piece), low),
            pltpu.VMEM((seqs, 6, width // 2, piece), low),
            pltpu.VMEM((seqs, 2, width // 2, piece), low),
            dma(seqs, 4),
            dma(seqs, 4),
            dma(seqs, 4),
            dma(seqs, 4),
            dma(rows - 1),
            dma(rows),
            dma(cols - 1),
            dma(cols),
            dma(3, cols - 1),
            dma(3, cols),
            dma(3, rows - 1),
            dma(3, rows),
            dma(3, rows),
            dma(3, rows),
            dma(seqs, 6),
            dma(seqs, 6),
            dma(seqs, 4),
            dma(seqs, 4),
        ],
        compiler_params=pltpu.CompilerParams(
            collective_id=0, has_side_effects=True, vmem_limit_bytes=BIG
        ),
    )(x, cot, gains, biases, tip, upb, wq, wo, wu, wd)


def mlp_kernel(
    seqs,
    l2_ref,
    c_ref,
    x1_ref,
    wu_ref,
    wd_ref,
    vcol_ref,
    tcol_ref,
    gx_ref,
    y_ref,
    du_ref,
    dd_ref,
    small_ref,
    up_ref,
    wu_t,
    wd_t,
    hid,
    gra,
    x1_wide,
    part,
    got,
    middle_buf,
    r_send,
    r_recv,
    a_send,
    a_recv,
):
    width, tokens = l2_ref.shape
    length = tokens // seqs
    row, row_peers = others("row")
    rows = len(row_peers) + 1
    piece = length // rows
    chunk = length // 2
    barrier = pltpu.get_barrier_semaphore()
    for peer in row_peers:
        pl.semaphore_signal(barrier, inc=1, device_id={"row": peer}, device_id_type=MESH)
    wu_t[...] = wu_ref[...].T
    wd_t[...] = wd_ref[...].T
    pieces = chunk // piece

    def forward(step, carry):
        cols = pl.ds(pl.multiple_of(step * chunk, chunk), chunk)
        before = plain(wu_t[...], l2_ref[:, cols]) + tcol_ref[:, 0:1]
        square = before * before
        tanh = jnp.tanh(GELU_COEF * (before + 0.044715 * before * square))
        hid[:, cols] = (0.5 * before * (1.0 + tanh)).astype(jnp.bfloat16)
        slope = 0.5 * (1.0 + tanh) + 0.5 * before * (1.0 - tanh * tanh) * (
            GELU_COEF * (1.0 + 3.0 * 0.044715 * square)
        )
        grad = (plain(wd_t[...], c_ref[:, cols]) * slope).astype(jnp.bfloat16)
        gra[:, cols] = grad
        back = plain(wu_ref[...], grad)
        for index in range(pieces):
            part[step * pieces + index] = back[:, index * piece : (index + 1) * piece].astype(
                jnp.bfloat16
            )
        return carry

    step_rows = width // 2

    def part_of(seq):
        return lambda index, half: part.at[
            seq * rows + index, half * step_rows : (half + 1) * step_rows
        ]

    def own_at(seq):
        return lambda index: gx_ref.at[:, pl.ds(pl.multiple_of(seq * length + index * piece, piece), piece)]

    def own_half(seq):
        return lambda index, half: gx_ref.at[
            half * step_rows : (half + 1) * step_rows,
            pl.ds(pl.multiple_of(seq * length + index * piece, piece), piece),
        ]

    out_copies = []
    for seq in range(seqs):
        lax.fori_loop(2 * seq, 2 * seq + 2, forward, 0)
        if seq == 0:
            pl.semaphore_wait(barrier, rows - 1)
        out_copies.append(reduce_one(part_of(seq), got.at[seq], r_send.at[seq], r_recv.at[seq]))
    x1_wide[...] = jnp.zeros_like(x1_wide)
    for seq in range(seqs):
        own = pl.ds(pl.multiple_of(seq * length + row * piece, piece), piece)
        x1_wide[:, own] = x1_ref[:, seq * piece : (seq + 1) * piece] + vcol_ref[:, 5:6]

    def finish(step, carry):
        cols = pl.ds(pl.multiple_of(step * chunk, chunk), chunk)
        y_ref[:, cols] = (plain(wd_ref[...], hid[:, cols]) + x1_wide[:, cols]).astype(jnp.bfloat16)
        return carry

    block = width // 4

    def up_weight(step, carry):
        place = pl.ds(pl.multiple_of(step * block, block), block)
        du_ref[place, :] = right_t(l2_ref[place, :], gra[...]).astype(jnp.bfloat16)
        return carry

    def down_weight(step, carry):
        place = pl.ds(pl.multiple_of(step * block, block), block)
        dd_ref[place, :] = right_t(c_ref[place, :], hid[...]).astype(jnp.bfloat16)
        return carry

    reduce_two(out_copies[0], part_of(0), got.at[0], middle_buf.at[0], r_send.at[0], r_recv.at[0])
    lax.fori_loop(0, 2 * seqs, finish, 0)
    reduce_two(out_copies[1], part_of(1), got.at[1], middle_buf.at[1], r_send.at[1], r_recv.at[1])
    gather_copies = []
    sums = [0.0] * 4
    for seq in range(seqs):
        own = pl.ds(pl.multiple_of(seq * length + row * piece, piece), piece)
        grad = reduce_end(out_copies[seq], part_of(seq), got.at[seq])
        middle = x1_ref[:, seq * piece : (seq + 1) * piece]
        center = jnp.mean(middle, axis=0, keepdims=True)
        offset = middle - center
        inverse = lax.rsqrt(jnp.mean(offset * offset, axis=0, keepdims=True) + EPSILON)
        normal = offset * inverse
        scaled = grad * vcol_ref[:, 1:2]
        first = jnp.mean(scaled, axis=0, keepdims=True)
        second = jnp.mean(scaled * normal, axis=0, keepdims=True)
        outer = c_ref[:, own].astype(jnp.float32)
        result = (outer + inverse * (scaled - first - normal * second)).astype(jnp.bfloat16)
        gx_ref[:, own] = result
        gather_copies.append(
            gather_one(own_at(seq)(row), own_at(seq), a_send.at[seq], a_recv.at[seq])
        )
        terms = (grad * normal, grad, result.astype(jnp.float32), outer)
        sums = [old + new for old, new in zip(sums, terms)]
    lax.fori_loop(0, 4, up_weight, 0)
    for seq in range(seqs):
        gather_two(gather_copies[seq], own_half(seq), a_send.at[seq], a_recv.at[seq])
    lax.fori_loop(0, 4, down_weight, 0)
    small_ref[...] = jnp.zeros_like(small_ref)
    for index in range(4):
        small_ref[index : index + 1, :] = lane_sums(sums[index])[0:1]
    up_ref[...] = right_t(jnp.ones((8, tokens), jnp.bfloat16), gra[...])
    for copies in gather_copies:
        gather_end(copies)
    sent(*out_copies, *gather_copies)


def mlp(l2, cot, x1, wu, wd, vcol, tcol):
    width, tokens = l2.shape
    rows = lax.axis_size("row")
    seqs = tokens // LENGTH
    piece = LENGTH // rows
    hidden = wu.shape[1]
    low, full = jnp.bfloat16, jnp.float32
    shapes = [
        ((width, tokens), low),
        ((width, tokens), low),
        ((width, hidden), low),
        ((width, hidden), low),
        ((8, width), full),
        ((8, hidden), full),
    ]
    return pl.pallas_call(
        functools.partial(mlp_kernel, seqs),
        out_shape=[jax.ShapeDtypeStruct(*shape) for shape in shapes],
        in_specs=[pl.BlockSpec(memory_space=pltpu.VMEM)] * 7,
        out_specs=[pl.BlockSpec(memory_space=pltpu.VMEM)] * len(shapes),
        scratch_shapes=[
            pltpu.VMEM((hidden, width), low),
            pltpu.VMEM((hidden, width), low),
            pltpu.VMEM((hidden, tokens), low),
            pltpu.VMEM((hidden, tokens), low),
            pltpu.VMEM((width, tokens), full),
            pltpu.VMEM((seqs * rows, width, piece), low),
            pltpu.VMEM((seqs, 6, width // 2, piece), low),
            pltpu.VMEM((seqs, 2, width // 2, piece), low),
            dma(seqs, 6),
            dma(seqs, 6),
            dma(seqs, 4),
            dma(seqs, 4),
        ],
        compiler_params=pltpu.CompilerParams(
            collective_id=1, has_side_effects=True, vmem_limit_bytes=BIG
        ),
    )(l2, cot, x1, wu, wd, vcol, tcol)


def leave_kernel(
    seqs,
    x_ref,
    gx_ref,
    y_ref,
    wa_ref,
    qkv_ref,
    att_ref,
    lse_ref,
    ln_ref,
    stat_ref,
    vcol_ref,
    small_ref,
    up_ref,
    du_ref,
    dd_ref,
    out_ref,
    gin_ref,
    gains_ref,
    biases_ref,
    gq_ref,
    qv_ref,
    go_ref,
    gu_ref,
    upb_ref,
    gd_ref,
    y_got,
    y_middle,
    back,
    mixed_grad,
    head_grad,
    got,
    middle_buf,
    ga_ref,
    stat_own,
    stat_all,
    da_ref,
    pair,
    summed,
    plane,
    line,
    small_all,
    tip_own,
    tip_all,
    a_own,
    a_all,
    b_all,
    a_sum,
    b_sum,
    a_pair,
    b_pair,
    y_send,
    y_recv,
    r_send,
    r_recv,
    s_send,
    s_recv,
    g_send,
    g_recv,
    p_send,
    p_recv,
    z_send,
    z_recv,
    f_send,
    f_recv,
    m_send,
    m_recv,
    t_send,
    t_recv,
    n_send,
    n_recv,
    e_send,
    e_recv,
):
    share, tokens = x_ref.shape
    length = tokens // seqs
    row, row_peers = others("row")
    col, col_peers = others("col")
    core = lax.axis_index("dp")
    twin = 1 - core
    rows, cols = len(row_peers) + 1, len(col_peers) + 1
    width = gx_ref.shape[0]
    head_cols = att_ref.shape[0]
    heads = head_cols // HEAD
    chunk = length // 2
    half = share // 2
    slab = rows_of(row, share)
    grads = (du_ref, dd_ref, da_ref)
    finals = (gu_ref, gd_ref, ga_ref)
    meet()
    step_rows = share // 2

    def half_rows(index, half):
        return pl.ds(pl.multiple_of(index * share + half * step_rows, step_rows), step_rows)

    def part_of(seq):
        return lambda index, half: back.at[half_rows(index, half), pl.ds(seq * length, length)]

    def y_part(index, half):
        return y_ref.at[half_rows(index, half)]

    def pair_start(piece):
        copies = []
        for index in range(rows):
            place = pl.ds(pl.multiple_of(index * share + twin * half, half), half)
            copies.append(
                send(
                    "dp",
                    twin,
                    grads[piece].at[place],
                    pair.at[piece, index],
                    g_send.at[piece, index],
                    g_recv.at[piece, index],
                )
            )
        return copies

    def pair_finish(piece, copies):
        for copy in copies:
            copy.wait_recv()
        for index in range(rows):
            place = pl.ds(pl.multiple_of(index * share + core * half, half), half)
            total = grads[piece][place, :].astype(jnp.float32) + pair[piece, index].astype(jnp.float32)
            summed[piece, index] = total.astype(jnp.bfloat16)
        keep(summed.at[piece, row], plane.at[piece, row], p_recv.at[piece, row])
        return [
            send(
                "row",
                peer,
                summed.at[piece, peer],
                plane.at[piece, row],
                p_send.at[piece, step],
                p_recv.at[piece, row],
            )
            for step, peer in enumerate(row_peers)
        ]

    def line_start(piece):
        wait_recv_all(plane.at[0, 0], p_recv.at[piece], rows)
        keep(plane.at[piece, col], line.at[piece, col], z_recv.at[piece, col])
        return [
            send(
                "col",
                peer,
                plane.at[piece, peer],
                line.at[piece, col],
                z_send.at[piece, step],
                z_recv.at[piece, col],
            )
            for step, peer in enumerate(col_peers)
        ]

    def line_finish(piece):
        wait_recv_all(line.at[0, 0], z_recv.at[piece], cols)
        total = line[piece, 0].astype(jnp.float32)
        for index in range(1, cols):
            total = total + line[piece, index].astype(jnp.float32)
        place = pl.ds(pl.multiple_of(core * half, half), half)
        finals[piece][place, :] = total
        return send(
            "dp", twin, finals[piece].at[place], finals[piece].at[place], f_send.at[piece], f_recv.at[piece]
        )

    pair_copies = [pair_start(0), pair_start(1)]

    def head_side(step, carry):
        at = pl.ds(pl.multiple_of(step * chunk, chunk), chunk)
        mixed_grad[:, at] = left_t(wa_ref[:, 3 * head_cols :], gx_ref[:, at]).astype(jnp.bfloat16)
        return carry

    def attend(seq):
        def one(head, carry):
            at = pl.multiple_of(head * HEAD, HEAD)
            key_rows = pl.ds(at + head_cols, HEAD)
            value_rows = pl.ds(at + 2 * head_cols, HEAD)
            kept = []
            for part_q in range(2):
                here = pl.ds(seq * length + part_q * chunk, chunk)
                keys = (part_q + 1) * chunk
                span = pl.ds(seq * length, keys)
                queries = qkv_ref[pl.ds(at, HEAD), here]
                key = qkv_ref[key_rows, span]
                outer = mixed_grad[pl.ds(at, HEAD), here]
                scores = left_t(key, queries)
                key_at = lax.broadcasted_iota(jnp.int32, (keys, chunk), 0)
                query_at = lax.broadcasted_iota(jnp.int32, (keys, chunk), 1) + part_q * chunk
                shift = lse_ref[seq * heads + head, 0:1, pl.ds(part_q * chunk, chunk)]
                probs = jnp.exp(jnp.where(key_at <= query_at, scores - shift, -1e30))
                delta = jnp.sum(
                    outer.astype(jnp.float32) * att_ref[pl.ds(at, HEAD), here].astype(jnp.float32),
                    axis=0,
                    keepdims=True,
                )
                inner = left_t(qkv_ref[value_rows, span], outer)
                slope = (probs * (inner - delta)).astype(jnp.bfloat16)
                head_grad[pl.ds(at, HEAD), here] = (plain(key, slope) * HEAD**-0.5).astype(jnp.bfloat16)
                kept.append((right_t(queries, slope), right_t(outer, probs.astype(jnp.bfloat16))))
            early, late = pl.ds(seq * length, chunk), pl.ds(seq * length + chunk, chunk)
            for rows_at, index in ((key_rows, 0), (value_rows, 1)):
                second = kept[1][index]
                head_grad[rows_at, early] = (second[:, :chunk] + kept[0][index]).astype(jnp.bfloat16)
                head_grad[rows_at, late] = second[:, chunk:].astype(jnp.bfloat16)
            return carry

        lax.fori_loop(0, heads, one, 0)

    def backward(step, carry):
        at = pl.ds(pl.multiple_of(step * chunk, chunk), chunk)
        back[:, at] = plain(wa_ref[:, : 3 * head_cols], head_grad[:, at]).astype(jnp.bfloat16)
        return carry

    out_copies = []
    p_copies, z_copies = [], []
    for seq in range(seqs):
        lax.fori_loop(2 * seq, 2 * seq + 2, head_side, 0)
        if seq == 0:
            for piece in range(2):
                p_copies.append(pair_finish(piece, pair_copies[piece]))
        attend(seq)
        lax.fori_loop(2 * seq, 2 * seq + 2, backward, 0)
        out_copies.append(reduce_one(part_of(seq), got.at[seq], r_send.at[seq], r_recv.at[seq]))
    z_copies.append(line_start(0))
    z_copies.append(line_start(1))
    reduce_two(out_copies[0], part_of(0), got.at[0], middle_buf.at[0], r_send.at[0], r_recv.at[0])
    block = width // 4

    def weight(step, carry):
        place = pl.ds(pl.multiple_of(step * block, block), block)
        da_ref[place, : 3 * head_cols] = right_t(ln_ref[place, :], head_grad[...]).astype(jnp.bfloat16)
        da_ref[place, 3 * head_cols :] = right_t(gx_ref[place, :], att_ref[...]).astype(jnp.bfloat16)
        return carry

    lax.fori_loop(0, 4, weight, 0)
    pair_copies.append(pair_start(2))
    reduce_two(out_copies[1], part_of(1), got.at[1], middle_buf.at[1], r_send.at[1], r_recv.at[1])
    p_copies.append(pair_finish(2, pair_copies[2]))
    tip_own[...] = jnp.zeros_like(tip_own)
    tip_own[:, : up_ref.shape[1]] = up_ref[...]
    tip_own[:, up_ref.shape[1] : up_ref.shape[1] + 3 * head_cols] = right_t(
        jnp.ones((8, tokens), jnp.bfloat16), head_grad[...]
    )
    keep(small_ref, small_all.at[row], m_recv.at[row])
    keep(tip_own, tip_all.at[row], t_recv.at[row])
    m_copies = [
        send("row", peer, small_ref, small_all.at[row], m_send.at[step], m_recv.at[row])
        for step, peer in enumerate(row_peers)
    ] + [
        send("row", peer, tip_own, tip_all.at[row], t_send.at[step], t_recv.at[row])
        for step, peer in enumerate(row_peers)
    ]
    gain = vcol_ref[slab, 0:1]
    a_own[...] = jnp.zeros_like(a_own)
    stat_own[...] = jnp.zeros_like(stat_own)
    scale_sum, shift_sum = 0.0, 0.0
    saved = []
    for seq in range(seqs):
        at = pl.ds(seq * length, length)
        grad = reduce_end(out_copies[seq], part_of(seq), got.at[seq])
        normal = (x_ref[:, at].astype(jnp.float32) - stat_ref[0:1, at]) * stat_ref[1:2, at]
        scaled = grad * gain
        stat_own[0:1, at] = jnp.sum(scaled, axis=0, keepdims=True)
        stat_own[1:2, at] = jnp.sum(scaled * normal, axis=0, keepdims=True)
        saved.append((scaled, normal))
        scale_sum = scale_sum + grad * normal
        shift_sum = shift_sum + grad
    keep(stat_own, stat_all.at[row], s_recv.at[row])
    s_copies = [
        send("row", peer, stat_own, stat_all.at[row], s_send.at[step], s_recv.at[row])
        for step, peer in enumerate(row_peers)
    ]
    y_copies = reduce_one(y_part, y_got, y_send, y_recv)
    z_copies.append(line_start(2))
    wait_recv_all(small_ref, m_recv, rows)
    wait_recv_all(tip_own, t_recv, rows)
    total = small_all[0]
    for index in range(1, rows):
        total = total + small_all[index]
    a_own[:, :width] = total
    a_own[0:1, width : width + share] = lane_sums(scale_sum)[0:1]
    a_own[1:2, width : width + share] = lane_sums(shift_sum)[0:1]
    keep(a_own, a_all.at[col], n_recv.at[0, col])
    keep(tip_all.at[col], b_all.at[col], n_recv.at[1, col])
    n_copies = [
        send("col", peer, a_own, a_all.at[col], n_send.at[0, step], n_recv.at[0, col])
        for step, peer in enumerate(col_peers)
    ] + [
        send("col", peer, tip_all.at[peer], b_all.at[col], n_send.at[1, step], n_recv.at[1, col])
        for step, peer in enumerate(col_peers)
    ]
    wait_recv_all(stat_own, s_recv, rows)
    total = stat_all[0]
    for index in range(1, rows):
        total = total + stat_all[index]
    total = total * (1.0 / width)
    for seq in range(seqs):
        at = pl.ds(seq * length, length)
        scaled, normal = saved[seq]
        first, second = (
            total[0:1, seq * length : (seq + 1) * length],
            total[1:2, seq * length : (seq + 1) * length],
        )
        result = stat_ref[1:2, at] * (scaled - first - normal * second)
        gin_ref[:, at] = (gx_ref[slab, at].astype(jnp.float32) + result).astype(jnp.bfloat16)
    f_copies = [line_finish(0), line_finish(1)]
    wait_recv_all(a_own, n_recv.at[0], cols)
    wait_recv_all(tip_own, n_recv.at[1], cols)
    first, second = a_all[0], b_all[0]
    for index in range(1, cols):
        first, second = first + a_all[index], second + b_all[index]
    a_sum[...] = first
    b_sum[...] = second
    e_copies = [
        send("dp", twin, a_sum, a_pair, e_send.at[0], e_recv.at[0]),
        send("dp", twin, b_sum, b_pair, e_send.at[1], e_recv.at[1]),
    ]
    reduce_two(y_copies, y_part, y_got, y_middle, y_send, y_recv)
    for copy in e_copies:
        copy.wait_recv()
    a_total = a_sum[...] + a_pair[...]
    b_total = b_sum[...] + b_pair[...]
    wide = jnp.zeros((8, share), jnp.float32)
    for index in range(rows):
        wide = wide + jnp.where(row == index, a_total[:, index * share : (index + 1) * share], 0.0)
    near = a_total[:, width : width + share]
    gains_ref[0:1, :] = near[0:1]
    gains_ref[1:2, :] = wide[0:1]
    biases_ref[0:1, :] = near[1:2]
    biases_ref[1:4, :] = wide[1:4]
    hidden = up_ref.shape[1]
    upb_ref[...] = b_total[0:1, :hidden]
    qv_ref[0:1, :] = b_total[0:1, hidden : hidden + head_cols]
    qv_ref[1:2, :] = b_total[0:1, hidden + 2 * head_cols : hidden + 3 * head_cols]
    f_copies.append(line_finish(2))
    out_ref[...] = reduce_end(y_copies, y_part, y_got).astype(jnp.bfloat16)
    for copy in f_copies:
        copy.wait_recv()
    for index in range(3):
        gq_ref[index] = ga_ref[:, index * head_cols : (index + 1) * head_cols]
    go_ref[...] = ga_ref[:, 3 * head_cols :].T
    sent(y_copies, m_copies, n_copies, s_copies, e_copies, f_copies)
    sent(*out_copies, *pair_copies, *p_copies, *z_copies)


def leave(x, gx, y, wa, qkv, att, lse, ln, stat, vcol, small, up, du, dd):
    share, tokens = x.shape
    rows, cols = lax.axis_size("row"), lax.axis_size("col")
    width = gx.shape[0]
    head_cols = att.shape[0]
    seqs = tokens // LENGTH
    half = share // 2
    low, full = jnp.bfloat16, jnp.float32
    a_lanes = -(-(width + share) // 128) * 128
    b_lanes = -(-(up.shape[1] + 3 * head_cols) // 128) * 128
    shapes = [
        ((share, tokens), low),
        ((share, tokens), low),
        ((2, share), full),
        ((4, share), full),
        ((3, share, head_cols), full),
        ((2, head_cols), full),
        ((head_cols, share), full),
        ((share, du.shape[1]), full),
        ((1, up.shape[1]), full),
        ((share, dd.shape[1]), full),
    ]
    return pl.pallas_call(
        functools.partial(leave_kernel, seqs),
        out_shape=[jax.ShapeDtypeStruct(*shape) for shape in shapes],
        in_specs=[pl.BlockSpec(memory_space=pltpu.VMEM)] * 14,
        out_specs=[pl.BlockSpec(memory_space=pltpu.VMEM)] * len(shapes),
        scratch_shapes=[
            pltpu.VMEM((6, half, tokens), low),
            pltpu.VMEM((2, half, tokens), low),
            pltpu.VMEM((width, tokens), low),
            pltpu.VMEM((head_cols, tokens), low),
            pltpu.VMEM((3 * head_cols, tokens), low),
            pltpu.VMEM((seqs, 6, half, LENGTH), low),
            pltpu.VMEM((seqs, 2, half, LENGTH), low),
            pltpu.VMEM((share, wa.shape[1]), full),
            pltpu.VMEM((8, tokens), full),
            pltpu.VMEM((rows, 8, tokens), full),
            pltpu.VMEM((width, wa.shape[1]), low),
            pltpu.VMEM((3, rows, half, wa.shape[1]), low),
            pltpu.VMEM((3, rows, half, wa.shape[1]), low),
            pltpu.VMEM((3, rows, half, wa.shape[1]), low),
            pltpu.VMEM((3, cols, half, wa.shape[1]), low),
            pltpu.VMEM((rows, 8, width), full),
            pltpu.VMEM((8, b_lanes), full),
            pltpu.VMEM((rows, 8, b_lanes), full),
            pltpu.VMEM((8, a_lanes), full),
            pltpu.VMEM((cols, 8, a_lanes), full),
            pltpu.VMEM((cols, 8, b_lanes), full),
            pltpu.VMEM((8, a_lanes), full),
            pltpu.VMEM((8, b_lanes), full),
            pltpu.VMEM((8, a_lanes), full),
            pltpu.VMEM((8, b_lanes), full),
            dma(6),
            dma(6),
            dma(seqs, 6),
            dma(seqs, 6),
            dma(rows - 1),
            dma(rows),
            dma(3, rows),
            dma(3, rows),
            dma(3, rows - 1),
            dma(3, rows),
            dma(3, cols - 1),
            dma(3, cols),
            dma(3),
            dma(3),
            dma(rows - 1),
            dma(rows),
            dma(rows - 1),
            dma(rows),
            dma(2, cols - 1),
            dma(2, cols),
            dma(2),
            dma(2),
        ],
        compiler_params=pltpu.CompilerParams(
            collective_id=2, has_side_effects=True, vmem_limit_bytes=BIG
        ),
    )(x, gx, y, wa, qkv, att, lse, ln, stat, vcol, small, up, du, dd)


def square_body(
    block_input, norm_gains, row_biases, w_qkv, qv_bias, w_out, w_up, up_bias, w_down, cotangent
):
    (x_all, c_all, wa_all, wu_all, wd_all, ln, qkv, att, lse, stat, x1, l2, vcol, tcol) = enter(
        block_input,
        cotangent,
        norm_gains,
        row_biases,
        qv_bias,
        up_bias.reshape(1, -1),
        w_qkv.transpose(1, 0, 2),
        w_out,
        w_up,
        w_down,
    )
    gx, y, du, dd, small, up = mlp(l2, c_all, x1, wu_all, wd_all, vcol, tcol)
    out, gin, gains, biases, gq, qv, go, gu, upb, gd = leave(
        block_input, gx, y, wa_all, qkv, att, lse, ln, stat, vcol, small, up, du, dd
    )
    return (out, gin, gains, biases, gq.transpose(1, 0, 2), qv, go, gu, upb.reshape(-1), gd)


def fits(mesh):
    sizes = mesh.shape
    return sizes["row"] == 4 and sizes["col"] == 4 and sizes["dp"] == 2


def solution(mesh):
    in_specs = (
        P("row", ("dp", "col")),
        P(None, "row"),
        P(None, "row"),
        P("row", None, "col"),
        P(None, "col"),
        P("col", "row"),
        P("row", "col"),
        P("col"),
        P("row", "col"),
        P("row", ("dp", "col")),
    )
    out_specs = (
        P("row", ("dp", "col")),
        P("row", ("dp", "col")),
        P(None, "row"),
        P(None, "row"),
        P("row", None, "col"),
        P(None, "col"),
        P("col", "row"),
        P("row", "col"),
        P("col"),
        P("row", "col"),
    )
    chosen = square_body if fits(mesh) else body
    return jax.shard_map(chosen, mesh=mesh, in_specs=in_specs, out_specs=out_specs, check_vma=False)
```

```python
import functools

import jax
import jax.numpy as jnp
from jax import lax
from jax.experimental import pallas as pl
from jax.experimental.pallas import tpu as pltpu
from jax.sharding import PartitionSpec as P

D = 768
HEAD = 64
LENGTH = 512


EPSILON = 1e-05
GELU_COEF = 0.7978845608028654


def gelu_tanh(values):
    return (
        0.5 * values * (1.0 + jnp.tanh(GELU_COEF * (values + 0.044715 * values * values * values)))
    )


def multiply(rows, weight, flipped):
    if flipped:
        return lax.dot_general(
            rows, weight, (((1,), (1,)), ((), ())), preferred_element_type=jnp.float32
        )
    return jnp.dot(rows, weight, preferred_element_type=jnp.float32)


def contract_tokens(left, right):
    return lax.dot_general(
        left, right, (((0,), (0,)), ((), ())), preferred_element_type=jnp.float32
    )


def swap_kernel(axis_name, count, shared, x_ref, o_ref, send_sem, recv_sem, own_sem):
    me = lax.axis_index(axis_name)
    barrier = pltpu.get_barrier_semaphore()
    peers = [lax.rem(me + step, count) for step in range(1, count)]
    for peer in peers:
        pl.semaphore_signal(
            barrier, inc=1, device_id={axis_name: peer}, device_id_type=pl.DeviceIdType.MESH
        )
    own = pltpu.make_async_copy(x_ref if shared else x_ref.at[me], o_ref.at[me], own_sem)
    own.start()
    pl.semaphore_wait(barrier, count - 1)
    copies = []
    for slot, peer in enumerate(peers):
        copy = pltpu.make_async_remote_copy(
            src_ref=x_ref if shared else x_ref.at[peer],
            dst_ref=o_ref.at[me],
            send_sem=send_sem.at[slot],
            recv_sem=recv_sem.at[slot],
            device_id={axis_name: peer},
            device_id_type=pl.DeviceIdType.MESH,
        )
        copy.start()
        copies.append(copy)
    own.wait()
    for copy in copies:
        copy.wait()


def swap(values, axis_name, shared, ident):
    count = lax.axis_size(axis_name)
    block = values.shape if shared else values.shape[1:]
    moved = values.size * values.dtype.itemsize
    return pl.pallas_call(
        functools.partial(swap_kernel, axis_name, count, shared),
        out_shape=jax.ShapeDtypeStruct((count, *block), values.dtype),
        in_specs=[pl.BlockSpec(memory_space=pltpu.VMEM)],
        out_specs=pl.BlockSpec(memory_space=pltpu.VMEM),
        scratch_shapes=[
            pltpu.SemaphoreType.DMA((count - 1,)),
            pltpu.SemaphoreType.DMA((count - 1,)),
            pltpu.SemaphoreType.DMA,
        ],
        compiler_params=pltpu.CompilerParams(collective_id=ident, has_side_effects=True),
        cost_estimate=pl.CostEstimate(
            flops=0, bytes_accessed=(20 if not shared else 60) * moved, transcendentals=0
        ),
    )(values)


def gather_async(local, axis_name):
    return lax.all_gather(local, axis_name, axis=0, tiled=True)


def scatter_sum_async(partial, axis_name):
    return lax.psum_scatter(
        partial.astype(jnp.bfloat16), axis_name, scatter_dimension=0, tiled=True
    ).astype(jnp.float32)


def gather(local, axis_name, ident):
    return swap(local, axis_name, True, ident).reshape(-1, *local.shape[1:])


def scatter_sum(partial, axis_name, ident):
    count = lax.axis_size(axis_name)
    pieces = partial.astype(jnp.bfloat16).reshape(count, -1, *partial.shape[1:])
    return jnp.sum(swap(pieces, axis_name, False, ident).astype(jnp.float32), axis=0)


def to_tokens(first, second, ident):
    rows, cols = lax.axis_size("row"), lax.axis_size("col")
    share = first.shape[0]
    block = jnp.concatenate([first.T, second.T], axis=1).reshape(rows, -1, 2 * share)
    block = swap(block, "row", False, ident)
    if rows != cols:
        moves = [(r * cols + c, c * rows + r) for r in range(rows) for c in range(cols)]
        block = lax.ppermute(block, ("row", "col"), moves)
    first = jnp.concatenate([block[r, :, :share] for r in range(rows)], axis=1)
    second = jnp.concatenate([block[r, :, share:] for r in range(rows)], axis=1)
    return first, second


def to_features(first, second, ident):
    rows, cols = lax.axis_size("row"), lax.axis_size("col")
    share = first.shape[1] // rows
    block = jnp.stack(
        [
            jnp.concatenate(
                [first[:, r * share : (r + 1) * share], second[:, r * share : (r + 1) * share]], axis=1
            )
            for r in range(rows)
        ]
    )
    if rows != cols:
        moves = [(c * rows + r, r * cols + c) for r in range(rows) for c in range(cols)]
        block = lax.ppermute(block, ("row", "col"), moves)
    block = swap(block, "row", False, ident).reshape(-1, 2 * share)
    return block[:, :share].T, block[:, share:].T


def flip(block):
    rows, cols = lax.axis_size("row"), lax.axis_size("col")
    if rows != cols:
        return block
    moves = [(r * cols + c, c * rows + r) for r in range(rows) for c in range(cols)]
    return lax.ppermute(block, ("row", "col"), moves)


def norm_forward(values, gain, bias):
    center = jnp.mean(values, axis=1, keepdims=True)
    offset = values - center
    inverse = lax.rsqrt(jnp.mean(offset * offset, axis=1, keepdims=True) + EPSILON)
    normal = offset * inverse
    return (normal * gain + bias, normal, inverse)


def norm_backward(grad, gain, normal, inverse):
    scaled = grad * gain
    first = jnp.mean(scaled, axis=1, keepdims=True)
    second = jnp.mean(scaled * normal, axis=1, keepdims=True)
    result = inverse * (scaled - first - normal * second)
    return (result, jnp.sum(grad * normal, axis=0), jnp.sum(grad, axis=0))


def causal_mask(length):
    positions = jnp.arange(length)
    return positions[None, :] <= positions[:, None]


def attention_forward(queries, keys, values):
    factor = HEAD ** (-0.5)

    def one_sequence(pieces):
        seq_q, seq_k, seq_v = pieces
        scores = (
            jnp.einsum("qhd,khd->hqk", seq_q, seq_k, preferred_element_type=jnp.float32) * factor
        )
        scores = jnp.where(causal_mask(seq_q.shape[0])[None], scores, -1e30)
        summit = jnp.max(scores, axis=-1, keepdims=True)
        expos = jnp.exp(scores - summit)
        total = jnp.sum(expos, axis=-1, keepdims=True)
        probs = (expos / total).astype(jnp.bfloat16)
        output = jnp.einsum("hqk,khd->qhd", probs, seq_v, preferred_element_type=jnp.float32)
        return (output, summit[..., 0] + jnp.log(total[..., 0]))

    return lax.map(one_sequence, (queries, keys, values))


def attention_backward(queries, keys, values, grad_out, log_sums):
    factor = HEAD ** (-0.5)

    def one_sequence(pieces):
        seq_q, seq_k, seq_v, seq_g, seq_l = pieces
        scores = (
            jnp.einsum("qhd,khd->hqk", seq_q, seq_k, preferred_element_type=jnp.float32) * factor
        )
        scores = jnp.where(causal_mask(seq_q.shape[0])[None], scores, -1e30)
        probs = jnp.exp(scores - seq_l[..., None])
        grad_v = jnp.einsum(
            "hqk,qhd->khd", probs.astype(jnp.bfloat16), seq_g, preferred_element_type=jnp.float32
        )
        grad_p = jnp.einsum("qhd,khd->hqk", seq_g, seq_v, preferred_element_type=jnp.float32)
        inner = jnp.sum(grad_p * probs, axis=-1, keepdims=True)
        grad_s = (probs * (grad_p - inner)).astype(jnp.bfloat16)
        grad_q = (
            jnp.einsum("hqk,khd->qhd", grad_s, seq_k, preferred_element_type=jnp.float32) * factor
        )
        grad_k = (
            jnp.einsum("hqk,qhd->khd", grad_s, seq_q, preferred_element_type=jnp.float32) * factor
        )
        return (grad_q, grad_k, grad_v)

    return lax.map(one_sequence, (queries, keys, values, grad_out, log_sums))


def body(
    block_input, norm_gains, row_biases, w_qkv, qv_bias, w_out, w_up, up_bias, w_down, cotangent
):
    head_cols = w_qkv.shape[2]
    square = lax.axis_size("row") == lax.axis_size("col")
    heads_axis, split_axis = ("row", "col") if square else ("col", "row")
    qv_bias, up_bias = flip(qv_bias), flip(up_bias)
    inputs, cot = to_tokens(block_input, cotangent, 0)
    inputs = inputs.astype(jnp.float32)
    vectors = swap(jnp.concatenate([norm_gains, row_biases], axis=0), "row", True, 1)
    vectors = jnp.concatenate([vectors[r] for r in range(vectors.shape[0])], axis=1)
    gains, biases = vectors[:2], vectors[2:]
    qkv_weight = gather_async(flip(w_qkv.reshape(w_qkv.shape[0], -1)), split_axis)
    rest = gather_async(flip(jnp.concatenate([w_out.T, w_up, w_down], axis=1)), split_axis)
    width = w_up.shape[1]
    out_t = rest[:, :head_cols]
    up = rest[:, head_cols : head_cols + width]
    down = rest[:, head_cols + width :]

    normed_one, normal_one, inverse_one = norm_forward(inputs, gains[0], biases[0])
    source_one = gather(normed_one.astype(jnp.bfloat16), heads_axis, 2)
    qkv_sum = multiply(source_one, qkv_weight, False)
    rows_here = qkv_sum.shape[0]
    qkv_sum = qkv_sum.reshape(rows_here, 3, head_cols)
    shape_four = (rows_here // LENGTH, LENGTH, head_cols // HEAD, HEAD)
    queries = (qkv_sum[:, 0] + qv_bias[0]).astype(jnp.bfloat16).reshape(shape_four)
    keys_all = qkv_sum[:, 1].astype(jnp.bfloat16).reshape(shape_four)
    values_all = (qkv_sum[:, 2] + qv_bias[1]).astype(jnp.bfloat16).reshape(shape_four)
    attended, log_sums = attention_forward(queries, keys_all, values_all)
    attended_low = attended.reshape(rows_here, head_cols).astype(jnp.bfloat16)
    middle = inputs + scatter_sum(multiply(attended_low, out_t, True), heads_axis, 3) + biases[2]
    normed_two, normal_two, inverse_two = norm_forward(middle, gains[1], biases[1])
    source_two = gather(normed_two.astype(jnp.bfloat16), heads_axis, 4)
    cot_all = gather_async(cot, heads_axis)
    before = multiply(source_two, up, False) + up_bias
    hidden_low = gelu_tanh(before).astype(jnp.bfloat16)
    grad_hidden = multiply(cot_all, down, False)
    grad_before = jax.vjp(gelu_tanh, before)[1](grad_hidden)[0].astype(jnp.bfloat16)
    grad_normed_two = scatter_sum(multiply(grad_before, up, True), heads_axis, 5)
    output = middle + scatter_sum_async(multiply(hidden_low, down, True), heads_axis) + biases[3]
    grad_w_down = contract_tokens(cot_all, hidden_low)
    grad_up_bias = jnp.sum(grad_before.astype(jnp.float32), axis=0)
    grad_w_up = contract_tokens(source_two, grad_before)
    grad_out = cot.astype(jnp.float32)
    back_two, gain_two, shift_two = norm_backward(
        grad_normed_two, gains[1], normal_two, inverse_two
    )
    grad_middle = grad_out + back_two
    grad_middle_low = grad_middle.astype(jnp.bfloat16)
    grad_out_bias = jnp.sum(grad_middle_low.astype(jnp.float32), axis=0)
    grad_down_bias = jnp.sum(grad_out, axis=0)
    grad_middle_all = gather(grad_middle_low, heads_axis, 6)
    grad_att_low = multiply(grad_middle_all, out_t, False).astype(jnp.bfloat16).reshape(shape_four)
    grad_w_out_t = contract_tokens(grad_middle_all, attended_low)
    grad_q, grad_k, grad_v = attention_backward(
        queries, keys_all, values_all, grad_att_low, log_sums
    )
    grad_q = grad_q.reshape(rows_here, head_cols).astype(jnp.bfloat16)
    grad_k = grad_k.reshape(rows_here, head_cols).astype(jnp.bfloat16)
    grad_v = grad_v.reshape(rows_here, head_cols).astype(jnp.bfloat16)
    grad_qkv_low = jnp.concatenate([grad_q, grad_k, grad_v], axis=1)
    grad_qv = jnp.stack(
        [jnp.sum(grad_q.astype(jnp.float32), axis=0), jnp.sum(grad_v.astype(jnp.float32), axis=0)]
    )
    grad_normed_one = scatter_sum(multiply(grad_qkv_low, qkv_weight, True), heads_axis, 7)
    grad_w_qkv = contract_tokens(source_one, grad_qkv_low)
    back_one, gain_one, shift_one = norm_backward(
        grad_normed_one, gains[0], normal_one, inverse_one
    )
    grad_input = grad_middle + back_one

    mlp_sum = scatter_sum_async(jnp.concatenate([grad_w_up, grad_w_down], axis=1), split_axis)
    mlp_sum = flip(lax.psum(mlp_sum.astype(jnp.bfloat16), "dp")).astype(jnp.float32)
    att_sum = scatter_sum(jnp.concatenate([grad_w_qkv, grad_w_out_t], axis=1), split_axis, 8)
    att_sum = jnp.sum(
        swap(flip(att_sum.astype(jnp.bfloat16)), "dp", True, 9).astype(jnp.float32), axis=0
    )
    sum_up = mlp_sum[:, :width]
    sum_down = mlp_sum[:, width:]
    sum_qkv = att_sum[:, : 3 * head_cols].reshape(w_qkv.shape)
    sum_out = att_sum[:, 3 * head_cols :].T
    features = gains.shape[1]
    longest = max(features, width, 2 * head_cols)
    small = [gain_one, gain_two, shift_one, shift_two, grad_out_bias, grad_down_bias]
    small = small + [grad_up_bias, grad_qv.reshape(-1)]
    small = jnp.stack([jnp.pad(row, (0, longest - row.shape[0])) for row in small])
    small = jnp.sum(swap(small, "dp", True, 10), axis=0)
    small = jnp.sum(swap(small, split_axis, True, 11), axis=0)
    projected = flip(small[6:])
    sum_upb = projected[0, :width]
    sum_qv = projected[1, : 2 * head_cols].reshape(2, head_cols)
    share = norm_gains.shape[1]
    small = jnp.sum(swap(small[:6], heads_axis, True, 12), axis=0)
    small = lax.dynamic_slice_in_dim(small, lax.axis_index("row") * share, share, axis=1)
    output_t, grad_input_t = to_features(
        output.astype(jnp.bfloat16), grad_input.astype(jnp.bfloat16), 13
    )
    return (
        output_t,
        grad_input_t,
        small[:2],
        small[2:],
        sum_qkv,
        sum_qv,
        sum_out,
        sum_up,
        sum_upb,
        sum_down,
    )


MESH = pl.DeviceIdType.MESH
BIG = 63 * 1024 * 1024


def send(axis_name, peer, source, target, send_sem, recv_sem):
    copy = pltpu.make_async_remote_copy(
        src_ref=source,
        dst_ref=target,
        send_sem=send_sem,
        recv_sem=recv_sem,
        device_id={axis_name: peer},
        device_id_type=MESH,
    )
    copy.start()
    return copy


def keep(source, target, sem):
    copy = pltpu.make_async_copy(source, target, sem)
    copy.start()
    return copy


def others(axis_name):
    count = lax.axis_size(axis_name)
    me = lax.axis_index(axis_name)
    return me, [lax.rem(me + step, count) for step in range(1, count)]


def meet():
    barrier = pltpu.get_barrier_semaphore()
    total = 0
    for name in ("row", "col", "dp"):
        _, peers = others(name)
        for peer in peers:
            pl.semaphore_signal(barrier, inc=1, device_id={name: peer}, device_id_type=MESH)
        total += len(peers)
    pl.semaphore_wait(barrier, total)


def rows_of(index, size):
    return pl.ds(pl.multiple_of(index * size, size), size)


def left_t(weight, acts):
    return lax.dot_general(weight, acts, (((0,), (0,)), ((), ())), preferred_element_type=jnp.float32)


def right_t(left, right):
    return lax.dot_general(left, right, (((1,), (1,)), ((), ())), preferred_element_type=jnp.float32)


def plain(left, right):
    return jnp.dot(left, right, preferred_element_type=jnp.float32)


def lane_sums(values):
    ones = jnp.ones((8, values.shape[1]), jnp.float32)
    return lax.dot_general(
        ones,
        values,
        (((1,), (1,)), ((), ())),
        precision=lax.Precision.HIGHEST,
        preferred_element_type=jnp.float32,
    )


def spread_weight(stage, own_ref, full_ref, buf, piece, sems):
    half = own_ref.shape[0] // 2
    core = lax.axis_index("dp")
    row, row_peers = others("row")
    col, col_peers = others("col")
    other = 1 - core
    z_send, z_recv, p_send, p_recv, c_send, c_recv = (sem.at[piece] for sem in sems)
    slots = buf.at[piece]
    size = 2 * half

    def rows_at(index, which):
        return pl.ds(pl.multiple_of(index * size + which * half, half), half)

    if stage == 0:
        mine = own_ref.at[pl.ds(pl.multiple_of(core * half, half), half)]
        copies = [keep(mine, slots.at[col], z_recv.at[col])]
        for step, peer in enumerate(col_peers):
            copies.append(send("col", peer, mine, slots.at[col], z_send.at[step], z_recv.at[col]))
        return copies
    if stage == 1:
        place = rows_at(row, core)
        copies = [keep(slots.at[row], full_ref.at[place], p_recv.at[row])]
        for step, peer in enumerate(row_peers):
            copies.append(
                send("row", peer, slots.at[peer], full_ref.at[place], p_send.at[step], p_recv.at[row])
            )
        return copies
    copies = []
    for index in range(len(row_peers) + 1):
        place = rows_at(index, core)
        copies.append(
            send("dp", other, full_ref.at[place], full_ref.at[place], c_send.at[index], c_recv.at[index])
        )
    return copies


def wait_recv_all(block, sems, count):
    for index in range(count):
        pltpu.make_async_copy(block, block, sems.at[index]).wait()


def crossings():
    row = lax.axis_index("row")
    near = row + 1 - 2 * lax.rem(row, 2)
    side = lax.rem(row + 2, 4)
    return row, near, side, 3 - row


def gather_one(source, spot, send_sem, recv_sem):
    row, near, side, _ = crossings()
    return [
        send("row", near, source, spot(row), send_sem.at[0], recv_sem.at[0]),
        send("row", side, source, spot(row), send_sem.at[1], recv_sem.at[1]),
    ]


def gather_two(copies, half_spot, send_sem, recv_sem):
    row, near, side, _ = crossings()
    copies[0].wait_recv()
    first = half_spot(near, 0)
    copies.append(send("row", side, first, first, send_sem.at[2], recv_sem.at[2]))
    copies[1].wait_recv()
    second = half_spot(side, 1)
    copies.append(send("row", near, second, second, send_sem.at[3], recv_sem.at[3]))


def gather_end(copies):
    copies[2].wait_recv()
    copies[3].wait_recv()


def reduce_one(part, got, send_sem, recv_sem):
    _, near, side, far = crossings()
    moves = ((near, near, 0), (near, far, 0), (side, side, 1), (side, far, 1))
    order = (1, 0, 3, 2)
    copies = [None] * 4
    for index in order:
        peer, block, half = moves[index]
        copies[index] = send(
            "row", peer, part(block, half), got.at[index], send_sem.at[index], recv_sem.at[index]
        )
    return copies


def reduce_two(copies, part, got, middle, send_sem, recv_sem):
    _, near, side, _ = crossings()
    for slot, index, peer, half in ((0, 1, side, 0), (1, 3, near, 1)):
        copies[index].wait_recv()
        total = part(peer, half)[...].astype(jnp.float32) + got[index].astype(jnp.float32)
        middle[slot] = total.astype(jnp.bfloat16)
        copies.append(
            send("row", peer, middle.at[slot], got.at[4 + slot], send_sem.at[4 + slot], recv_sem.at[4 + slot])
        )


def reduce_end(copies, part, got):
    row = lax.axis_index("row")
    for index in (0, 2, 4, 5):
        copies[index].wait_recv()
    halves = []
    for half, one, two in ((0, 0, 4), (1, 2, 5)):
        halves.append(
            part(row, half)[...].astype(jnp.float32)
            + got[one].astype(jnp.float32)
            + got[two].astype(jnp.float32)
        )
    return jnp.concatenate(halves, axis=0)


def sent(*groups):
    for copies in groups:
        for copy in copies:
            copy.wait_send()


def block_kernel(names, seqs, *refs):
    r = dict(zip(names, refs))
    x_ref, c_ref = r["x"], r["c"]
    x_all, c_all, ln_ref, qkv_ref, att_ref = r["x_all"], r["c_all"], r["ln"], r["qkv"], r["att"]
    wa_all, wu_all, wd_all = r["wa_all"], r["wu_all"], r["wd_all"]
    lse_ref, stat_ref, x1_ref, l2_ref, gx_ref = r["lse"], r["stat"], r["x1"], r["l2"], r["gx"]
    vcol_ref, tcol_ref, zbuf = r["vcol"], r["tcol"], r["zbuf"]
    hid, gra, y_ref, head_grad, mixed_grad, back = (
        r["hid"],
        r["gra"],
        r["y"],
        r["head_grad"],
        r["mixed_grad"],
        r["back"],
    )
    low, full = jnp.bfloat16, jnp.float32
    share, tokens = x_ref.shape
    length = tokens // seqs
    width = x_all.shape[0]
    row, row_peers = others("row")
    col, col_peers = others("col")
    core = lax.axis_index("dp")
    twin = 1 - core
    rows, cols = len(row_peers) + 1, len(col_peers) + 1
    head_cols = r["wo"].shape[0]
    heads = head_cols // HEAD
    hidden = wu_all.shape[1]
    piece = length // rows
    chunk = length // 2
    half = share // 2
    slab = rows_of(row, share)
    spans = [pl.ds(seq * length, length) for seq in range(seqs)]
    owns = [pl.ds(pl.multiple_of(seq * length + row * piece, piece), piece) for seq in range(seqs)]
    owned = [slice(seq * piece, (seq + 1) * piece) for seq in range(seqs)]

    def slab_spot(ref, at):
        return lambda index: ref.at[rows_of(index, share), at]

    def half_rows(index, side):
        return pl.ds(pl.multiple_of(index * share + side * half, half), half)

    def slab_half(ref, at):
        return lambda index, side: ref.at[half_rows(index, side), at]

    def token_spot(ref, seq):
        return lambda index: ref.at[:, pl.ds(pl.multiple_of(seq * length + index * piece, piece), piece)]

    def token_half(ref, seq):
        step = width // 2
        return lambda index, side: ref.at[
            side * step : (side + 1) * step,
            pl.ds(pl.multiple_of(seq * length + index * piece, piece), piece),
        ]

    def token_part(ref, seq):
        step = width // 2
        return lambda index, side: ref.at[seq * rows + index, side * step : (side + 1) * step]

    class Gather:
        def __init__(self, name, seq, source, spot, half_spot):
            self.sems = (r[name + "_send"].at[seq], r[name + "_recv"].at[seq])
            self.half_spot = half_spot
            self.copies = gather_one(source, spot, *self.sems)

        def two(self):
            gather_two(self.copies, self.half_spot, *self.sems)

        def end(self):
            gather_end(self.copies)

    class Reduce:
        def __init__(self, name, seq, part):
            self.sems = (r[name + "_send"].at[seq], r[name + "_recv"].at[seq])
            self.got, self.middle = r[name + "_got"].at[seq], r[name + "_middle"].at[seq]
            self.part = part
            self.copies = reduce_one(part, self.got, *self.sems)

        def two(self):
            reduce_two(self.copies, self.part, self.got, self.middle, *self.sems)

        def end(self):
            return reduce_end(self.copies, self.part, self.got)

    wa_ref, vec_own, tip_own = r["wa_own"], r["vec_own"], r["tip_own"]
    for index in range(3):
        wa_ref[:, index * head_cols : (index + 1) * head_cols] = r["wq"][index]
    wa_ref[:, 3 * head_cols :] = r["wo"][...].T
    vec_own[...] = jnp.zeros_like(vec_own)
    vec_own[0:2, :share] = r["gains"][...]
    vec_own[2:6, :share] = r["biases"][...]
    tip_own[...] = jnp.zeros_like(tip_own)
    tip_own[0:2, :head_cols] = r["qv_bias"][...]
    lanes = tip_own.shape[1]
    for index in range(hidden // lanes):
        tip_own[2 + index : 3 + index, :] = r["up_bias"][:, index * lanes : (index + 1) * lanes]
    weights = ((wa_ref, wa_all), (r["wu"], wu_all), (r["wd"], wd_all))
    weight_sems = tuple(r[name] for name in ("wz_send", "wz_recv", "wp_send", "wp_recv", "wc_send", "wc_recv"))

    def spread(stage, index):
        own, whole = weights[index]
        return spread_weight(stage, own, whole, zbuf, index, weight_sems)

    def arrived(stage, index):
        sems = weight_sems[2 * stage + 1].at[index]
        wait_recv_all(zbuf.at[0, 0], sems, (cols, rows, rows)[stage])

    meet()
    keep(vec_own, r["vec_all"].at[row], r["vec_recv"].at[row])
    keep(tip_own, r["tip_all"].at[col], r["tip_recv"].at[col])
    z_copies, p_copies, d_copies = [spread(0, 0)], [], []
    small_copies = [
        send("row", peer, vec_own, r["vec_all"].at[row], r["vec_send"].at[step], r["vec_recv"].at[row])
        for step, peer in enumerate(row_peers)
    ] + [
        send("col", peer, tip_own, r["tip_all"].at[col], r["tip_send"].at[step], r["tip_recv"].at[col])
        for step, peer in enumerate(col_peers)
    ]
    xs = [
        Gather("x", seq, x_ref.at[:, at], slab_spot(x_all, at), slab_half(x_all, at))
        for seq, at in enumerate(spans)
    ]
    x_all[slab, :] = x_ref[...]
    c_all[slab, :] = c_ref[...]
    wait_recv_all(vec_own, r["vec_recv"], rows)
    for index in range(rows):
        flipped = r["vec_all"][index].T
        vcol_ref[index * share : (index + 1) * share, :] = flipped[:share]
    wait_recv_all(tip_own, r["tip_recv"], cols)
    tip = r["tip_all"][row].T
    bias_q, bias_v = tip[:head_cols, 0:1], tip[:head_cols, 1:2]
    for index in range(hidden // lanes):
        tcol_ref[index * lanes : (index + 1) * lanes, :] = jnp.broadcast_to(
            tip[:, 2 + index : 3 + index], (lanes, 8)
        )
    arrived(0, 0)
    p_copies.append(spread(1, 0))
    z_copies += [spread(0, 1), spread(0, 2)]
    for gather in xs:
        gather.two()
    cots = [
        Gather("c", seq, c_ref.at[:, at], slab_spot(c_all, at), slab_half(c_all, at))
        for seq, at in enumerate(spans)
    ]

    def first_norm(step, carry):
        at = pl.ds(pl.multiple_of(step * chunk, chunk), chunk)
        values = x_all[:, at].astype(full)
        center = jnp.mean(values, axis=0, keepdims=True)
        offset = values - center
        inverse = lax.rsqrt(jnp.mean(offset * offset, axis=0, keepdims=True) + EPSILON)
        ln_ref[:, at] = (offset * inverse * vcol_ref[:, 0:1] + vcol_ref[:, 2:3]).astype(low)
        stat_ref[0:1, at] = center
        stat_ref[1:2, at] = inverse
        return carry

    def project(step, carry):
        at = pl.ds(pl.multiple_of(step * chunk, chunk), chunk)
        mixed = left_t(wa_all[:, : 3 * head_cols], ln_ref[:, at])
        qkv_ref[:head_cols, at] = ((mixed[:head_cols] + bias_q) * HEAD**-0.5).astype(low)
        qkv_ref[head_cols : 2 * head_cols, at] = mixed[head_cols : 2 * head_cols].astype(low)
        qkv_ref[2 * head_cols :, at] = (mixed[2 * head_cols :] + bias_v).astype(low)
        return carry

    def causal(part_q):
        keys = (part_q + 1) * chunk
        key_at = lax.broadcasted_iota(jnp.int32, (keys, chunk), 0)
        return key_at <= lax.broadcasted_iota(jnp.int32, (keys, chunk), 1) + part_q * chunk

    def attend(seq):
        def one(head, carry):
            at = pl.multiple_of(head * HEAD, HEAD)
            for part_q in range(2):
                here = pl.ds(seq * length + part_q * chunk, chunk)
                span = pl.ds(seq * length, (part_q + 1) * chunk)
                scores = left_t(qkv_ref[pl.ds(at + head_cols, HEAD), span], qkv_ref[pl.ds(at, HEAD), here])
                scores = jnp.where(causal(part_q), scores, -1e30)
                summit = jnp.max(scores, axis=0, keepdims=True)
                expos = jnp.exp(scores - summit)
                total = jnp.sum(expos, axis=0, keepdims=True)
                mixed = plain(qkv_ref[pl.ds(at + 2 * head_cols, HEAD), span], expos.astype(low))
                att_ref[pl.ds(at, HEAD), here] = (mixed / total).astype(low)
                lse_ref[seq * heads + head, :, pl.ds(part_q * chunk, chunk)] = jnp.broadcast_to(
                    summit + jnp.log(total), (8, chunk)
                )
            return carry

        lax.fori_loop(0, heads, one, 0)

    xs[0].end()
    lax.fori_loop(0, 2, first_norm, 0)
    arrived(1, 0)
    d_copies.append(spread(2, 0))
    arrived(2, 0)
    outs = []
    for seq in range(seqs):
        lax.fori_loop(2 * seq, 2 * seq + 2, project, 0)
        attend(seq)
        mixed = plain(wa_all[:, 3 * head_cols :], att_ref[:, seq * length : (seq + 1) * length])
        for index in range(rows):
            r["o_part"][seq * rows + index] = mixed[:, index * piece : (index + 1) * piece].astype(low)
        outs.append(Reduce("o", seq, token_part(r["o_part"], seq)))
        if seq == 0:
            xs[1].end()
            lax.fori_loop(2, 4, first_norm, 0)
            arrived(0, 1)
            p_copies.append(spread(1, 1))
    outs[0].two()
    arrived(0, 2)
    p_copies.append(spread(1, 2))
    outs[1].two()
    for gather in cots:
        gather.two()
    l2s = []
    for seq in range(seqs):
        middle = x_all[:, owns[seq]].astype(full) + outs[seq].end() + vcol_ref[:, 4:5]
        x1_ref[:, owned[seq]] = middle
        center = jnp.mean(middle, axis=0, keepdims=True)
        offset = middle - center
        inverse = lax.rsqrt(jnp.mean(offset * offset, axis=0, keepdims=True) + EPSILON)
        l2_ref[:, owns[seq]] = (offset * inverse * vcol_ref[:, 1:2] + vcol_ref[:, 3:4]).astype(low)
        spot = token_spot(l2_ref, seq)
        l2s.append(Gather("l", seq, spot(row), spot, token_half(l2_ref, seq)))
    arrived(1, 1)
    d_copies.append(spread(2, 1))
    l2s[0].two()
    arrived(1, 2)
    d_copies.append(spread(2, 2))
    l2s[1].two()

    wu_t, wd_t, g_part = r["wu_t"], r["wd_t"], r["g_part"]
    arrived(2, 1)
    wu_t[...] = wu_all[...].T
    arrived(2, 2)
    wd_t[...] = wd_all[...].T
    pieces = chunk // piece

    def forward(step, carry):
        at = pl.ds(pl.multiple_of(step * chunk, chunk), chunk)
        before = plain(wu_t[...], l2_ref[:, at]) + tcol_ref[:, 0:1]
        square = before * before
        tanh = jnp.tanh(GELU_COEF * (before + 0.044715 * before * square))
        hid[:, at] = (0.5 * before * (1.0 + tanh)).astype(low)
        slope = 0.5 * (1.0 + tanh) + 0.5 * before * (1.0 - tanh * tanh) * (
            GELU_COEF * (1.0 + 3.0 * 0.044715 * square)
        )
        grad = (plain(wd_t[...], c_all[:, at]) * slope).astype(low)
        gra[:, at] = grad
        backs = plain(wu_all[...], grad)
        for index in range(pieces):
            g_part[step * pieces + index] = backs[:, index * piece : (index + 1) * piece].astype(low)
        return carry

    def finish(step, carry):
        at = pl.ds(pl.multiple_of(step * chunk, chunk), chunk)
        y_ref[:, at] = plain(wd_all[...], hid[:, at]).astype(low)
        return carry

    block = width // 4

    def up_weight(step, carry):
        place = pl.ds(pl.multiple_of(step * block, block), block)
        r["du"][place, :] = right_t(l2_ref[place, :], gra[...]).astype(low)
        return carry

    def down_weight(step, carry):
        place = pl.ds(pl.multiple_of(step * block, block), block)
        r["dd"][place, :] = right_t(c_all[place, :], hid[...]).astype(low)
        return carry

    grads = (r["du"], r["dd"], r["da"])
    finals = (r["gu"], r["gd"], r["ga"])
    pair, summed, plane, line = r["pair"], r["summed"], r["plane"], r["line"]

    def pair_start(index):
        return [
            send(
                "dp",
                twin,
                grads[index].at[half_rows(block_row, twin)],
                pair.at[index, block_row],
                r["pair_send"].at[index, block_row],
                r["pair_recv"].at[index, block_row],
            )
            for block_row in range(rows)
        ]

    def pair_finish(index, copies):
        for copy in copies:
            copy.wait_recv()
        for block_row in range(rows):
            mine = grads[index][half_rows(block_row, core), :].astype(full)
            summed[index, block_row] = (mine + pair[index, block_row].astype(full)).astype(low)
        keep(summed.at[index, row], plane.at[index, row], r["plane_recv"].at[index, row])
        return [
            send(
                "row",
                peer,
                summed.at[index, peer],
                plane.at[index, row],
                r["plane_send"].at[index, step],
                r["plane_recv"].at[index, row],
            )
            for step, peer in enumerate(row_peers)
        ]

    def line_start(index):
        wait_recv_all(plane.at[0, 0], r["plane_recv"].at[index], rows)
        keep(plane.at[index, col], line.at[index, col], r["line_recv"].at[index, col])
        return [
            send(
                "col",
                peer,
                plane.at[index, peer],
                line.at[index, col],
                r["line_send"].at[index, step],
                r["line_recv"].at[index, col],
            )
            for step, peer in enumerate(col_peers)
        ]

    def line_finish(index):
        wait_recv_all(line.at[0, 0], r["line_recv"].at[index], cols)
        total = line[index, 0].astype(full)
        for other in range(1, cols):
            total = total + line[index, other].astype(full)
        place = pl.ds(pl.multiple_of(core * half, half), half)
        finals[index][place, :] = total
        return send(
            "dp",
            twin,
            finals[index].at[place],
            finals[index].at[place],
            r["final_send"].at[index],
            r["final_recv"].at[index],
        )

    pair_copies, plane_copies, line_copies = [], [], []
    gls = []
    for seq in range(seqs):
        l2s[seq].end()
        cots[seq].end()
        lax.fori_loop(2 * seq, 2 * seq + 2, forward, 0)
        gls.append(Reduce("g", seq, token_part(g_part, seq)))
    lax.fori_loop(0, 4, up_weight, 0)
    pair_copies.append(pair_start(0))
    gls[0].two()
    lax.fori_loop(0, 4, down_weight, 0)
    pair_copies.append(pair_start(1))
    gls[1].two()
    gxs = []
    sums = [0.0] * 4
    for seq in range(seqs):
        grad = gls[seq].end()
        middle = x1_ref[:, owned[seq]]
        center = jnp.mean(middle, axis=0, keepdims=True)
        offset = middle - center
        inverse = lax.rsqrt(jnp.mean(offset * offset, axis=0, keepdims=True) + EPSILON)
        normal = offset * inverse
        scaled = grad * vcol_ref[:, 1:2]
        first = jnp.mean(scaled, axis=0, keepdims=True)
        second = jnp.mean(scaled * normal, axis=0, keepdims=True)
        outer = c_all[:, owns[seq]].astype(full)
        result = (outer + inverse * (scaled - first - normal * second)).astype(low)
        gx_ref[:, owns[seq]] = result
        spot = token_spot(gx_ref, seq)
        gxs.append(Gather("gx", seq, spot(row), spot, token_half(gx_ref, seq)))
        terms = (grad * normal, grad, result.astype(full), outer)
        sums = [old + new for old, new in zip(sums, terms)]
    small_ref = r["small"]
    small_ref[...] = jnp.zeros_like(small_ref)
    for index in range(4):
        small_ref[index : index + 1, :] = lane_sums(sums[index])[0:1]
    gxs[0].two()
    plane_copies.append(pair_finish(0, pair_copies[0]))
    gxs[1].two()
    plane_copies.append(pair_finish(1, pair_copies[1]))
    lax.fori_loop(0, 2 * seqs, finish, 0)
    for seq in range(seqs):
        y_own = plain(wd_all[...], hid[:, owns[seq]]) + x1_ref[:, owned[seq]] + vcol_ref[:, 5:6]
        y_ref[:, owns[seq]] = y_own.astype(low)

    def head_side(step, carry):
        at = pl.ds(pl.multiple_of(step * chunk, chunk), chunk)
        mixed_grad[:, at] = left_t(wa_all[:, 3 * head_cols :], gx_ref[:, at]).astype(low)
        return carry

    def attend_back(seq):
        def one(head, carry):
            at = pl.multiple_of(head * HEAD, HEAD)
            key_rows = pl.ds(at + head_cols, HEAD)
            value_rows = pl.ds(at + 2 * head_cols, HEAD)
            kept = []
            for part_q in range(2):
                here = pl.ds(seq * length + part_q * chunk, chunk)
                span = pl.ds(seq * length, (part_q + 1) * chunk)
                queries = qkv_ref[pl.ds(at, HEAD), here]
                key = qkv_ref[key_rows, span]
                outer = mixed_grad[pl.ds(at, HEAD), here]
                shift = lse_ref[seq * heads + head, 0:1, pl.ds(part_q * chunk, chunk)]
                probs = jnp.exp(jnp.where(causal(part_q), left_t(key, queries) - shift, -1e30))
                delta = jnp.sum(
                    outer.astype(full) * att_ref[pl.ds(at, HEAD), here].astype(full), axis=0, keepdims=True
                )
                slope = (probs * (left_t(qkv_ref[value_rows, span], outer) - delta)).astype(low)
                head_grad[pl.ds(at, HEAD), here] = (plain(key, slope) * HEAD**-0.5).astype(low)
                kept.append((right_t(queries, slope), right_t(outer, probs.astype(low))))
            early, late = pl.ds(seq * length, chunk), pl.ds(seq * length + chunk, chunk)
            for place, index in ((key_rows, 0), (value_rows, 1)):
                second = kept[1][index]
                head_grad[place, early] = (second[:, :chunk] + kept[0][index]).astype(low)
                head_grad[place, late] = second[:, chunk:].astype(low)
            return carry

        lax.fori_loop(0, heads, one, 0)

    def backward(step, carry):
        at = pl.ds(pl.multiple_of(step * chunk, chunk), chunk)
        back[:, at] = plain(wa_all[:, : 3 * head_cols], head_grad[:, at]).astype(low)
        return carry

    def mixed_weight(step, carry):
        place = pl.ds(pl.multiple_of(step * block, block), block)
        r["da"][place, : 3 * head_cols] = right_t(ln_ref[place, :], head_grad[...]).astype(low)
        r["da"][place, 3 * head_cols :] = right_t(gx_ref[place, :], att_ref[...]).astype(low)
        return carry

    ones = []
    for seq in range(seqs):
        gxs[seq].end()
        lax.fori_loop(2 * seq, 2 * seq + 2, head_side, 0)
        attend_back(seq)
        lax.fori_loop(2 * seq, 2 * seq + 2, backward, 0)
        ones.append(Reduce("n", seq, slab_half(back, spans[seq])))
        if seq == 0:
            line_copies += [line_start(0), line_start(1)]
    ones[0].two()
    lax.fori_loop(0, 4, mixed_weight, 0)
    pair_copies.append(pair_start(2))
    ones[1].two()
    plane_copies.append(pair_finish(2, pair_copies[2]))

    tail_own, tail_all, a_own, a_all, b_all = r["tail_own"], r["tail_all"], r["a_own"], r["a_all"], r["b_all"]
    tail_own[...] = jnp.zeros_like(tail_own)
    count = jnp.ones((8, tokens), low)
    tail_own[:, :hidden] = right_t(count, gra[...])
    tail_own[:, hidden : hidden + 3 * head_cols] = right_t(count, head_grad[...])
    keep(small_ref, r["small_all"].at[row], r["s_recv"].at[0, row])
    keep(tail_own, tail_all.at[row], r["s_recv"].at[1, row])
    for step, peer in enumerate(row_peers):
        small_copies += [
            send(
                "row", peer, small_ref, r["small_all"].at[row], r["s_send"].at[0, step], r["s_recv"].at[0, row]
            ),
            send("row", peer, tail_own, tail_all.at[row], r["s_send"].at[1, step], r["s_recv"].at[1, row]),
        ]
    stat_own, stat_all = r["stat_own"], r["stat_all"]
    gain = vcol_ref[slab, 0:1]
    a_own[...] = jnp.zeros_like(a_own)
    stat_own[...] = jnp.zeros_like(stat_own)
    scale_sum, shift_sum = 0.0, 0.0
    saved = []
    for seq, at in enumerate(spans):
        grad = ones[seq].end()
        normal = (x_ref[:, at].astype(full) - stat_ref[0:1, at]) * stat_ref[1:2, at]
        scaled = grad * gain
        stat_own[0:1, at] = jnp.sum(scaled, axis=0, keepdims=True)
        stat_own[1:2, at] = jnp.sum(scaled * normal, axis=0, keepdims=True)
        saved.append((scaled, normal))
        scale_sum = scale_sum + grad * normal
        shift_sum = shift_sum + grad
    keep(stat_own, stat_all.at[row], r["s_recv"].at[2, row])
    for step, peer in enumerate(row_peers):
        small_copies.append(
            send("row", peer, stat_own, stat_all.at[row], r["s_send"].at[2, step], r["s_recv"].at[2, row])
        )
    ys = Reduce("y", 0, slab_half(y_ref, pl.ds(0, tokens)))
    line_copies.append(line_start(2))
    wait_recv_all(small_ref, r["s_recv"].at[0], rows)
    wait_recv_all(tail_own, r["s_recv"].at[1], rows)
    total = r["small_all"][0]
    for index in range(1, rows):
        total = total + r["small_all"][index]
    a_own[:, :width] = total
    a_own[0:1, width : width + share] = lane_sums(scale_sum)[0:1]
    a_own[1:2, width : width + share] = lane_sums(shift_sum)[0:1]
    keep(a_own, a_all.at[col], r["t_recv"].at[0, col])
    keep(tail_all.at[col], b_all.at[col], r["t_recv"].at[1, col])
    for step, peer in enumerate(col_peers):
        small_copies += [
            send("col", peer, a_own, a_all.at[col], r["t_send"].at[0, step], r["t_recv"].at[0, col]),
            send("col", peer, tail_all.at[peer], b_all.at[col], r["t_send"].at[1, step], r["t_recv"].at[1, col]),
        ]
    wait_recv_all(stat_own, r["s_recv"].at[2], rows)
    total = stat_all[0]
    for index in range(1, rows):
        total = total + stat_all[index]
    total = total * (1.0 / width)
    for seq, at in enumerate(spans):
        scaled, normal = saved[seq]
        here = slice(seq * length, (seq + 1) * length)
        result = stat_ref[1:2, at] * (scaled - total[0:1, here] - normal * total[1:2, here])
        r["gin"][:, at] = (gx_ref[slab, at].astype(full) + result).astype(low)
    final_copies = [line_finish(0), line_finish(1)]
    wait_recv_all(a_own, r["t_recv"].at[0], cols)
    wait_recv_all(tail_own, r["t_recv"].at[1], cols)
    first, second = a_all[0], b_all[0]
    for index in range(1, cols):
        first, second = first + a_all[index], second + b_all[index]
    r["a_sum"][...] = first
    r["b_sum"][...] = second
    twin_copies = [
        send("dp", twin, r["a_sum"], r["a_pair"], r["u_send"].at[0], r["u_recv"].at[0]),
        send("dp", twin, r["b_sum"], r["b_pair"], r["u_send"].at[1], r["u_recv"].at[1]),
    ]
    ys.two()
    for copy in twin_copies:
        copy.wait_recv()
    a_total = r["a_sum"][...] + r["a_pair"][...]
    b_total = r["b_sum"][...] + r["b_pair"][...]
    wide = jnp.zeros((8, share), full)
    for index in range(rows):
        wide = wide + jnp.where(row == index, a_total[:, index * share : (index + 1) * share], 0.0)
    near = a_total[:, width : width + share]
    r["g_gains"][0:1, :] = near[0:1]
    r["g_gains"][1:2, :] = wide[0:1]
    r["g_biases"][0:1, :] = near[1:2]
    r["g_biases"][1:4, :] = wide[1:4]
    r["g_up_bias"][...] = b_total[0, :hidden]
    r["g_qv"][0:1, :] = b_total[0:1, hidden : hidden + head_cols]
    r["g_qv"][1:2, :] = b_total[0:1, hidden + 2 * head_cols : hidden + 3 * head_cols]
    final_copies.append(line_finish(2))
    r["out"][...] = ys.end().astype(low)
    for copy in final_copies:
        copy.wait_recv()
    for index in range(3):
        r["g_wq"][index] = r["ga"][:, index * head_cols : (index + 1) * head_cols]
    r["g_wo"][...] = r["ga"][:, 3 * head_cols :].T
    sent(small_copies, twin_copies, final_copies, *pair_copies, *plane_copies, *line_copies, *d_copies)
    sent(*[copies[1:] for copies in z_copies + p_copies])
    sent(*[move.copies for move in xs + cots + outs + l2s + gls + gxs + ones + [ys]])


def settle_kernel(count, *refs):
    for index in range(count):
        refs[count + index][...] = refs[index][...]


def settle(arrays):
    count = len(arrays)
    return pl.pallas_call(
        functools.partial(settle_kernel, count),
        out_shape=[jax.ShapeDtypeStruct(array.shape, array.dtype) for array in arrays],
        in_specs=[pl.BlockSpec(memory_space=pltpu.VMEM)] * count,
        out_specs=[pl.BlockSpec(memory_space=pltpu.VMEM)] * count,
    )(*arrays)


def square_body(
    block_input, norm_gains, row_biases, w_qkv, qv_bias, w_out, w_up, up_bias, w_down, cotangent
):
    low, full = jnp.bfloat16, jnp.float32
    share, tokens = block_input.shape
    rows, cols = lax.axis_size("row"), lax.axis_size("col")
    width = share * rows
    head_cols = w_out.shape[0]
    mixed = 3 * head_cols + share
    hidden = w_up.shape[1]
    seqs = tokens // LENGTH
    heads = head_cols // HEAD
    piece = LENGTH // rows
    half = share // 2
    lanes = -(-share // 128) * 128
    tips = -(-(2 + hidden // lanes) // 8) * 8
    a_lanes = -(-(width + share) // 128) * 128
    b_lanes = -(-(hidden + 3 * head_cols) // 128) * 128
    inputs = {
        "x": block_input,
        "c": cotangent,
        "gains": norm_gains,
        "biases": row_biases,
        "qv_bias": qv_bias,
        "up_bias": up_bias.reshape(1, -1),
        "wq": w_qkv.transpose(1, 0, 2),
        "wo": w_out,
        "wu": w_up,
        "wd": w_down,
    }
    outputs = {
        "out": ((share, tokens), low),
        "gin": ((share, tokens), low),
        "g_gains": ((2, share), full),
        "g_biases": ((4, share), full),
        "g_wq": ((3, share, head_cols), full),
        "g_qv": ((2, head_cols), full),
        "g_wo": ((head_cols, share), full),
        "gu": ((share, hidden), full),
        "g_up_bias": ((hidden,), full),
        "gd": ((share, hidden), full),
    }
    token_got, token_middle = (seqs, 6, width // 2, piece), (seqs, 2, width // 2, piece)
    buffers = {
        "x_all": ((width, tokens), low),
        "c_all": ((width, tokens), low),
        "wa_all": ((width, mixed), low),
        "wu_all": ((width, hidden), low),
        "wd_all": ((width, hidden), low),
        "ln": ((width, tokens), low),
        "qkv": ((3 * head_cols, tokens), low),
        "att": ((head_cols, tokens), low),
        "lse": ((seqs * heads, 8, LENGTH), full),
        "stat": ((8, tokens), full),
        "x1": ((width, seqs * piece), full),
        "l2": ((width, tokens), low),
        "gx": ((width, tokens), low),
        "vcol": ((width, 8), full),
        "tcol": ((hidden, 8), full),
        "wa_own": ((share, mixed), low),
        "vec_own": ((8, lanes), full),
        "tip_own": ((tips, lanes), full),
        "vec_all": ((rows, 8, lanes), full),
        "tip_all": ((cols, tips, lanes), full),
        "zbuf": ((3, cols, half, mixed), low),
        "o_part": ((seqs * rows, width, piece), low),
        "o_got": (token_got, low),
        "o_middle": (token_middle, low),
        "wu_t": ((hidden, width), low),
        "wd_t": ((hidden, width), low),
        "hid": ((hidden, tokens), low),
        "gra": ((hidden, tokens), low),
        "g_part": ((seqs * rows, width, piece), low),
        "g_got": (token_got, low),
        "g_middle": (token_middle, low),
        "y": ((width, tokens), low),
        "y_got": ((1, 6, half, tokens), low),
        "y_middle": ((1, 2, half, tokens), low),
        "du": ((width, hidden), low),
        "dd": ((width, hidden), low),
        "da": ((width, mixed), low),
        "small": ((8, width), full),
        "mixed_grad": ((head_cols, tokens), low),
        "head_grad": ((3 * head_cols, tokens), low),
        "back": ((width, tokens), low),
        "n_got": ((seqs, 6, half, LENGTH), low),
        "n_middle": ((seqs, 2, half, LENGTH), low),
        "ga": ((share, mixed), full),
        "stat_own": ((8, tokens), full),
        "stat_all": ((rows, 8, tokens), full),
        "pair": ((3, rows, half, mixed), low),
        "summed": ((3, rows, half, mixed), low),
        "plane": ((3, rows, half, mixed), low),
        "line": ((3, cols, half, mixed), low),
        "small_all": ((rows, 8, width), full),
        "tail_own": ((8, b_lanes), full),
        "tail_all": ((rows, 8, b_lanes), full),
        "a_own": ((8, a_lanes), full),
        "a_all": ((cols, 8, a_lanes), full),
        "b_all": ((cols, 8, b_lanes), full),
        "a_sum": ((8, a_lanes), full),
        "b_sum": ((8, b_lanes), full),
        "a_pair": ((8, a_lanes), full),
        "b_pair": ((8, b_lanes), full),
    }
    arrivals = {
        "x": ((seqs, 4), (seqs, 4)),
        "c": ((seqs, 4), (seqs, 4)),
        "l": ((seqs, 4), (seqs, 4)),
        "gx": ((seqs, 4), (seqs, 4)),
        "o": ((seqs, 6), (seqs, 6)),
        "g": ((seqs, 6), (seqs, 6)),
        "n": ((seqs, 6), (seqs, 6)),
        "y": ((1, 6), (1, 6)),
        "vec": ((rows - 1,), (rows,)),
        "tip": ((cols - 1,), (cols,)),
        "wz": ((3, cols - 1), (3, cols)),
        "wp": ((3, rows - 1), (3, rows)),
        "wc": ((3, rows), (3, rows)),
        "pair": ((3, rows), (3, rows)),
        "plane": ((3, rows - 1), (3, rows)),
        "line": ((3, cols - 1), (3, cols)),
        "final": ((3,), (3,)),
        "s": ((3, rows - 1), (3, rows)),
        "t": ((2, cols - 1), (2, cols)),
        "u": ((2,), (2,)),
    }
    names = list(inputs) + list(outputs) + list(buffers)
    scratch = [pltpu.VMEM(*shape) for shape in buffers.values()]
    for name, (sends, receives) in arrivals.items():
        names += [name + "_send", name + "_recv"]
        scratch += [pltpu.SemaphoreType.DMA(sends), pltpu.SemaphoreType.DMA(receives)]
    results = pl.pallas_call(
        functools.partial(block_kernel, names, seqs),
        out_shape=[jax.ShapeDtypeStruct(*shape) for shape in outputs.values()],
        in_specs=[pl.BlockSpec(memory_space=pltpu.VMEM)] * len(inputs),
        out_specs=[pl.BlockSpec(memory_space=pltpu.VMEM)] * len(outputs),
        scratch_shapes=scratch,
        compiler_params=pltpu.CompilerParams(
            collective_id=0, has_side_effects=True, vmem_limit_bytes=BIG
        ),
    )(*inputs.values())
    results = dict(zip(outputs, settle(results)))
    results["g_wq"] = results["g_wq"].transpose(1, 0, 2)
    return tuple(results.values())


def fits(mesh):
    sizes = mesh.shape
    return sizes["row"] == 4 and sizes["col"] == 4 and sizes["dp"] == 2


def solution(mesh):
    in_specs = (
        P("row", ("dp", "col")),
        P(None, "row"),
        P(None, "row"),
        P("row", None, "col"),
        P(None, "col"),
        P("col", "row"),
        P("row", "col"),
        P("col"),
        P("row", "col"),
        P("row", ("dp", "col")),
    )
    out_specs = (
        P("row", ("dp", "col")),
        P("row", ("dp", "col")),
        P(None, "row"),
        P(None, "row"),
        P("row", None, "col"),
        P(None, "col"),
        P("col", "row"),
        P("row", "col"),
        P("col"),
        P("row", "col"),
    )
    chosen = square_body if fits(mesh) else body
    return jax.shard_map(chosen, mesh=mesh, in_specs=in_specs, out_specs=out_specs, check_vma=False)
```

```python
import functools
import types

import jax
import jax.numpy as jnp
from jax import lax
from jax.experimental import pallas as pl
from jax.experimental.pallas import tpu as pltpu
from jax.sharding import PartitionSpec as P

D = 768
HEAD = 64
LENGTH = 512


EPSILON = 1e-05
GELU_COEF = 0.7978845608028654


def gelu_tanh(values):
    return (
        0.5 * values * (1.0 + jnp.tanh(GELU_COEF * (values + 0.044715 * values * values * values)))
    )


def multiply(rows, weight, flipped):
    if flipped:
        return lax.dot_general(
            rows, weight, (((1,), (1,)), ((), ())), preferred_element_type=jnp.float32
        )
    return jnp.dot(rows, weight, preferred_element_type=jnp.float32)


def contract_tokens(left, right):
    return lax.dot_general(
        left, right, (((0,), (0,)), ((), ())), preferred_element_type=jnp.float32
    )


def swap_kernel(axis_name, count, shared, x_ref, o_ref, send_sem, recv_sem, own_sem):
    me = lax.axis_index(axis_name)
    barrier = pltpu.get_barrier_semaphore()
    peers = [lax.rem(me + step, count) for step in range(1, count)]
    for peer in peers:
        pl.semaphore_signal(
            barrier, inc=1, device_id={axis_name: peer}, device_id_type=pl.DeviceIdType.MESH
        )
    own = pltpu.make_async_copy(x_ref if shared else x_ref.at[me], o_ref.at[me], own_sem)
    own.start()
    pl.semaphore_wait(barrier, count - 1)
    copies = []
    for slot, peer in enumerate(peers):
        copy = pltpu.make_async_remote_copy(
            src_ref=x_ref if shared else x_ref.at[peer],
            dst_ref=o_ref.at[me],
            send_sem=send_sem.at[slot],
            recv_sem=recv_sem.at[slot],
            device_id={axis_name: peer},
            device_id_type=pl.DeviceIdType.MESH,
        )
        copy.start()
        copies.append(copy)
    own.wait()
    for copy in copies:
        copy.wait()


def swap(values, axis_name, shared, ident):
    count = lax.axis_size(axis_name)
    block = values.shape if shared else values.shape[1:]
    moved = values.size * values.dtype.itemsize
    return pl.pallas_call(
        functools.partial(swap_kernel, axis_name, count, shared),
        out_shape=jax.ShapeDtypeStruct((count, *block), values.dtype),
        in_specs=[pl.BlockSpec(memory_space=pltpu.VMEM)],
        out_specs=pl.BlockSpec(memory_space=pltpu.VMEM),
        scratch_shapes=[
            pltpu.SemaphoreType.DMA((count - 1,)),
            pltpu.SemaphoreType.DMA((count - 1,)),
            pltpu.SemaphoreType.DMA,
        ],
        compiler_params=pltpu.CompilerParams(collective_id=ident, has_side_effects=True),
        cost_estimate=pl.CostEstimate(
            flops=0, bytes_accessed=(20 if not shared else 60) * moved, transcendentals=0
        ),
    )(values)


def gather_async(local, axis_name):
    return lax.all_gather(local, axis_name, axis=0, tiled=True)


def scatter_sum_async(partial, axis_name):
    return lax.psum_scatter(
        partial.astype(jnp.bfloat16), axis_name, scatter_dimension=0, tiled=True
    ).astype(jnp.float32)


def gather(local, axis_name, ident):
    return swap(local, axis_name, True, ident).reshape(-1, *local.shape[1:])


def scatter_sum(partial, axis_name, ident):
    count = lax.axis_size(axis_name)
    pieces = partial.astype(jnp.bfloat16).reshape(count, -1, *partial.shape[1:])
    return jnp.sum(swap(pieces, axis_name, False, ident).astype(jnp.float32), axis=0)


def to_tokens(first, second, ident):
    rows, cols = lax.axis_size("row"), lax.axis_size("col")
    share = first.shape[0]
    block = jnp.concatenate([first.T, second.T], axis=1).reshape(rows, -1, 2 * share)
    block = swap(block, "row", False, ident)
    if rows != cols:
        moves = [(r * cols + c, c * rows + r) for r in range(rows) for c in range(cols)]
        block = lax.ppermute(block, ("row", "col"), moves)
    first = jnp.concatenate([block[r, :, :share] for r in range(rows)], axis=1)
    second = jnp.concatenate([block[r, :, share:] for r in range(rows)], axis=1)
    return first, second


def to_features(first, second, ident):
    rows, cols = lax.axis_size("row"), lax.axis_size("col")
    share = first.shape[1] // rows
    block = jnp.stack(
        [
            jnp.concatenate(
                [first[:, r * share : (r + 1) * share], second[:, r * share : (r + 1) * share]], axis=1
            )
            for r in range(rows)
        ]
    )
    if rows != cols:
        moves = [(c * rows + r, r * cols + c) for r in range(rows) for c in range(cols)]
        block = lax.ppermute(block, ("row", "col"), moves)
    block = swap(block, "row", False, ident).reshape(-1, 2 * share)
    return block[:, :share].T, block[:, share:].T


def flip(block):
    rows, cols = lax.axis_size("row"), lax.axis_size("col")
    if rows != cols:
        return block
    moves = [(r * cols + c, c * rows + r) for r in range(rows) for c in range(cols)]
    return lax.ppermute(block, ("row", "col"), moves)


def norm_forward(values, gain, bias):
    center = jnp.mean(values, axis=1, keepdims=True)
    offset = values - center
    inverse = lax.rsqrt(jnp.mean(offset * offset, axis=1, keepdims=True) + EPSILON)
    normal = offset * inverse
    return (normal * gain + bias, normal, inverse)


def norm_backward(grad, gain, normal, inverse):
    scaled = grad * gain
    first = jnp.mean(scaled, axis=1, keepdims=True)
    second = jnp.mean(scaled * normal, axis=1, keepdims=True)
    result = inverse * (scaled - first - normal * second)
    return (result, jnp.sum(grad * normal, axis=0), jnp.sum(grad, axis=0))


def causal_mask(length):
    positions = jnp.arange(length)
    return positions[None, :] <= positions[:, None]


def attention_forward(queries, keys, values):
    factor = HEAD ** (-0.5)

    def one_sequence(pieces):
        seq_q, seq_k, seq_v = pieces
        scores = (
            jnp.einsum("qhd,khd->hqk", seq_q, seq_k, preferred_element_type=jnp.float32) * factor
        )
        scores = jnp.where(causal_mask(seq_q.shape[0])[None], scores, -1e30)
        summit = jnp.max(scores, axis=-1, keepdims=True)
        expos = jnp.exp(scores - summit)
        total = jnp.sum(expos, axis=-1, keepdims=True)
        probs = (expos / total).astype(jnp.bfloat16)
        output = jnp.einsum("hqk,khd->qhd", probs, seq_v, preferred_element_type=jnp.float32)
        return (output, summit[..., 0] + jnp.log(total[..., 0]))

    return lax.map(one_sequence, (queries, keys, values))


def attention_backward(queries, keys, values, grad_out, log_sums):
    factor = HEAD ** (-0.5)

    def one_sequence(pieces):
        seq_q, seq_k, seq_v, seq_g, seq_l = pieces
        scores = (
            jnp.einsum("qhd,khd->hqk", seq_q, seq_k, preferred_element_type=jnp.float32) * factor
        )
        scores = jnp.where(causal_mask(seq_q.shape[0])[None], scores, -1e30)
        probs = jnp.exp(scores - seq_l[..., None])
        grad_v = jnp.einsum(
            "hqk,qhd->khd", probs.astype(jnp.bfloat16), seq_g, preferred_element_type=jnp.float32
        )
        grad_p = jnp.einsum("qhd,khd->hqk", seq_g, seq_v, preferred_element_type=jnp.float32)
        inner = jnp.sum(grad_p * probs, axis=-1, keepdims=True)
        grad_s = (probs * (grad_p - inner)).astype(jnp.bfloat16)
        grad_q = (
            jnp.einsum("hqk,khd->qhd", grad_s, seq_k, preferred_element_type=jnp.float32) * factor
        )
        grad_k = (
            jnp.einsum("hqk,qhd->khd", grad_s, seq_q, preferred_element_type=jnp.float32) * factor
        )
        return (grad_q, grad_k, grad_v)

    return lax.map(one_sequence, (queries, keys, values, grad_out, log_sums))


def body(
    block_input, norm_gains, row_biases, w_qkv, qv_bias, w_out, w_up, up_bias, w_down, cotangent
):
    head_cols = w_qkv.shape[2]
    square = lax.axis_size("row") == lax.axis_size("col")
    heads_axis, split_axis = ("row", "col") if square else ("col", "row")
    qv_bias, up_bias = flip(qv_bias), flip(up_bias)
    inputs, cot = to_tokens(block_input, cotangent, 0)
    inputs = inputs.astype(jnp.float32)
    vectors = swap(jnp.concatenate([norm_gains, row_biases], axis=0), "row", True, 1)
    vectors = jnp.concatenate([vectors[r] for r in range(vectors.shape[0])], axis=1)
    gains, biases = vectors[:2], vectors[2:]
    qkv_weight = gather_async(flip(w_qkv.reshape(w_qkv.shape[0], -1)), split_axis)
    rest = gather_async(flip(jnp.concatenate([w_out.T, w_up, w_down], axis=1)), split_axis)
    width = w_up.shape[1]
    out_t = rest[:, :head_cols]
    up = rest[:, head_cols : head_cols + width]
    down = rest[:, head_cols + width :]

    normed_one, normal_one, inverse_one = norm_forward(inputs, gains[0], biases[0])
    source_one = gather(normed_one.astype(jnp.bfloat16), heads_axis, 2)
    qkv_sum = multiply(source_one, qkv_weight, False)
    rows_here = qkv_sum.shape[0]
    qkv_sum = qkv_sum.reshape(rows_here, 3, head_cols)
    shape_four = (rows_here // LENGTH, LENGTH, head_cols // HEAD, HEAD)
    queries = (qkv_sum[:, 0] + qv_bias[0]).astype(jnp.bfloat16).reshape(shape_four)
    keys_all = qkv_sum[:, 1].astype(jnp.bfloat16).reshape(shape_four)
    values_all = (qkv_sum[:, 2] + qv_bias[1]).astype(jnp.bfloat16).reshape(shape_four)
    attended, log_sums = attention_forward(queries, keys_all, values_all)
    attended_low = attended.reshape(rows_here, head_cols).astype(jnp.bfloat16)
    middle = inputs + scatter_sum(multiply(attended_low, out_t, True), heads_axis, 3) + biases[2]
    normed_two, normal_two, inverse_two = norm_forward(middle, gains[1], biases[1])
    source_two = gather(normed_two.astype(jnp.bfloat16), heads_axis, 4)
    cot_all = gather_async(cot, heads_axis)
    before = multiply(source_two, up, False) + up_bias
    hidden_low = gelu_tanh(before).astype(jnp.bfloat16)
    grad_hidden = multiply(cot_all, down, False)
    grad_before = jax.vjp(gelu_tanh, before)[1](grad_hidden)[0].astype(jnp.bfloat16)
    grad_normed_two = scatter_sum(multiply(grad_before, up, True), heads_axis, 5)
    output = middle + scatter_sum_async(multiply(hidden_low, down, True), heads_axis) + biases[3]
    grad_w_down = contract_tokens(cot_all, hidden_low)
    grad_up_bias = jnp.sum(grad_before.astype(jnp.float32), axis=0)
    grad_w_up = contract_tokens(source_two, grad_before)
    grad_out = cot.astype(jnp.float32)
    back_two, gain_two, shift_two = norm_backward(
        grad_normed_two, gains[1], normal_two, inverse_two
    )
    grad_middle = grad_out + back_two
    grad_middle_low = grad_middle.astype(jnp.bfloat16)
    grad_out_bias = jnp.sum(grad_middle_low.astype(jnp.float32), axis=0)
    grad_down_bias = jnp.sum(grad_out, axis=0)
    grad_middle_all = gather(grad_middle_low, heads_axis, 6)
    grad_att_low = multiply(grad_middle_all, out_t, False).astype(jnp.bfloat16).reshape(shape_four)
    grad_w_out_t = contract_tokens(grad_middle_all, attended_low)
    grad_q, grad_k, grad_v = attention_backward(
        queries, keys_all, values_all, grad_att_low, log_sums
    )
    grad_q = grad_q.reshape(rows_here, head_cols).astype(jnp.bfloat16)
    grad_k = grad_k.reshape(rows_here, head_cols).astype(jnp.bfloat16)
    grad_v = grad_v.reshape(rows_here, head_cols).astype(jnp.bfloat16)
    grad_qkv_low = jnp.concatenate([grad_q, grad_k, grad_v], axis=1)
    grad_qv = jnp.stack(
        [jnp.sum(grad_q.astype(jnp.float32), axis=0), jnp.sum(grad_v.astype(jnp.float32), axis=0)]
    )
    grad_normed_one = scatter_sum(multiply(grad_qkv_low, qkv_weight, True), heads_axis, 7)
    grad_w_qkv = contract_tokens(source_one, grad_qkv_low)
    back_one, gain_one, shift_one = norm_backward(
        grad_normed_one, gains[0], normal_one, inverse_one
    )
    grad_input = grad_middle + back_one

    mlp_sum = scatter_sum_async(jnp.concatenate([grad_w_up, grad_w_down], axis=1), split_axis)
    mlp_sum = flip(lax.psum(mlp_sum.astype(jnp.bfloat16), "dp")).astype(jnp.float32)
    att_sum = scatter_sum(jnp.concatenate([grad_w_qkv, grad_w_out_t], axis=1), split_axis, 8)
    att_sum = jnp.sum(
        swap(flip(att_sum.astype(jnp.bfloat16)), "dp", True, 9).astype(jnp.float32), axis=0
    )
    sum_up = mlp_sum[:, :width]
    sum_down = mlp_sum[:, width:]
    sum_qkv = att_sum[:, : 3 * head_cols].reshape(w_qkv.shape)
    sum_out = att_sum[:, 3 * head_cols :].T
    features = gains.shape[1]
    longest = max(features, width, 2 * head_cols)
    small = [gain_one, gain_two, shift_one, shift_two, grad_out_bias, grad_down_bias]
    small = small + [grad_up_bias, grad_qv.reshape(-1)]
    small = jnp.stack([jnp.pad(row, (0, longest - row.shape[0])) for row in small])
    small = jnp.sum(swap(small, "dp", True, 10), axis=0)
    small = jnp.sum(swap(small, split_axis, True, 11), axis=0)
    projected = flip(small[6:])
    sum_upb = projected[0, :width]
    sum_qv = projected[1, : 2 * head_cols].reshape(2, head_cols)
    share = norm_gains.shape[1]
    small = jnp.sum(swap(small[:6], heads_axis, True, 12), axis=0)
    small = lax.dynamic_slice_in_dim(small, lax.axis_index("row") * share, share, axis=1)
    output_t, grad_input_t = to_features(
        output.astype(jnp.bfloat16), grad_input.astype(jnp.bfloat16), 13
    )
    return (
        output_t,
        grad_input_t,
        small[:2],
        small[2:],
        sum_qkv,
        sum_qv,
        sum_out,
        sum_up,
        sum_upb,
        sum_down,
    )


MESH = pl.DeviceIdType.MESH
BIG = 63 * 1024 * 1024


def remote(target_id, source, target, send_sem, recv_sem):
    copy = pltpu.make_async_remote_copy(
        src_ref=source,
        dst_ref=target,
        send_sem=send_sem,
        recv_sem=recv_sem,
        device_id=target_id,
        device_id_type=MESH,
    )
    copy.start()
    return copy


def keep(source, target, sem):
    copy = pltpu.make_async_copy(source, target, sem)
    copy.start()
    return copy


def send(axis_name, peer, source, target, send_sem, recv_sem):
    return remote({axis_name: peer}, source, target, send_sem, recv_sem)


def place():
    core, row = lax.axis_index("dp"), lax.axis_index("row")
    home, level = lax.rem(row, 2), row // 2
    return core, 1 - core, home, level, 2 * core + home


def others(axis_name):
    count = lax.axis_size(axis_name)
    me = lax.axis_index(axis_name)
    return me, [lax.rem(me + step, count) for step in range(1, count)]


def meet(extra):
    barrier = pltpu.get_barrier_semaphore()
    pl.semaphore_signal(barrier, inc=1, device_id=extra, device_id_type=MESH)
    total = 1
    for name in ("row", "col", "dp"):
        _, peers = others(name)
        for peer in peers:
            pl.semaphore_signal(barrier, inc=1, device_id={name: peer}, device_id_type=MESH)
        total += len(peers)
    pl.semaphore_wait(barrier, total)


def rows_of(index, size):
    return pl.ds(pl.multiple_of(index * size, size), size)


def left_t(weight, acts):
    return lax.dot_general(weight, acts, (((0,), (0,)), ((), ())), preferred_element_type=jnp.float32)


def right_t(left, right):
    return lax.dot_general(left, right, (((1,), (1,)), ((), ())), preferred_element_type=jnp.float32)


def plain(left, right):
    return jnp.dot(left, right, preferred_element_type=jnp.float32)


def lane_sums(values):
    ones = jnp.ones((8, values.shape[1]), jnp.float32)
    return lax.dot_general(
        ones,
        values,
        (((1,), (1,)), ((), ())),
        precision=lax.Precision.HIGHEST,
        preferred_element_type=jnp.float32,
    )


def wait_recv_all(block, sems, count):
    for index in range(count):
        pltpu.make_async_copy(block, block, sems.at[index]).wait()


def crossings():
    core, twin, home, _, me = place()
    row = lax.axis_index("row")
    near = me + 1 - 2 * home
    side = 2 * twin + home
    return me, near, side, 3 - me, {"row": row + 1 - 2 * home}, {"dp": twin}


def gather_one(source, spot, send_sem, recv_sem):
    me, _, _, _, near_id, side_id = crossings()
    return [
        remote(near_id, source, spot(me), send_sem.at[0], recv_sem.at[0]),
        remote(side_id, source, spot(me), send_sem.at[1], recv_sem.at[1]),
    ]


def gather_two(copies, spot, send_sem, recv_sem):
    _, near, _, _, _, side_id = crossings()
    copies[0].wait_recv()
    copies.append(remote(side_id, spot(near), spot(near), send_sem.at[2], recv_sem.at[2]))


def gather_end(copies):
    copies[1].wait_recv()
    copies[2].wait_recv()


def reduce_one(part, got, send_sem, recv_sem):
    _, _, side, far, _, side_id = crossings()
    moves = ((1, far), (0, side))
    copies = [None, None]
    for slot, block in moves:
        copies[slot] = remote(side_id, part(block), got.at[slot], send_sem.at[slot], recv_sem.at[slot])
    return copies


def reduce_two(copies, part, got, middle, send_sem, recv_sem):
    _, near, _, _, near_id, _ = crossings()
    copies[1].wait_recv()
    middle[...] = (part(near)[...].astype(jnp.float32) + got[1].astype(jnp.float32)).astype(jnp.bfloat16)
    copies.append(remote(near_id, middle, got.at[2], send_sem.at[2], recv_sem.at[2]))


def reduce_end(copies, part, got):
    me = crossings()[0]
    copies[0].wait_recv()
    copies[2].wait_recv()
    total = part(me)[...].astype(jnp.float32) + got[0].astype(jnp.float32)
    return total + got[2].astype(jnp.float32)


def sent(*groups):
    for copies in groups:
        for copy in copies:
            copy.wait_send()


def block_kernel(names, seqs, *refs):
    count = len(refs) - 2 * len(names[1])
    arrays = dict(zip(names[0], refs[:count]))
    r = types.SimpleNamespace(**arrays)
    out_sems = types.SimpleNamespace(**dict(zip(names[1], refs[count::2])))
    in_sems = types.SimpleNamespace(**dict(zip(names[1], refs[count + 1 :: 2])))
    x_ref, c_ref = r.x, r.c
    x_all, c_all, ln_ref, qkv_ref, att_ref = r.x_all, r.c_all, r.ln, r.qkv, r.att
    wa_all, wu_all, wd_all = r.wa_all, r.wu_all, r.wd_all
    lse_ref, stat_ref, x1_ref, l2_ref, gx_ref = r.lse, r.stat, r.x1, r.l2, r.gx
    vcol_ref, tcol_ref = r.vcol, r.tcol
    hid, gra, y_ref, head_grad, mixed_grad, back = r.hid, r.gra, r.y, r.head_grad, r.mixed_grad, r.back
    low, full = jnp.bfloat16, jnp.float32
    share, tokens = x_ref.shape
    length = tokens // seqs
    width = x_all.shape[0]
    row, row_peers = others("row")
    col, col_peers = others("col")
    core, twin, home, level, me = place()
    near_row, over_row = row + 1 - 2 * home, lax.rem(row + 2, 4)
    swap_id = {"dp": twin, "row": over_row}
    stays = core == level
    rows, cols = len(row_peers) + 1, len(col_peers) + 1
    head_cols = r.wo.shape[0]
    heads = head_cols // HEAD
    hidden = wu_all.shape[1]
    piece = length // rows
    chunk = length // 2
    half = share // 2
    slab = rows_of(me, share)
    spans = [pl.ds(seq * length, length) for seq in range(seqs)]
    owns = [pl.ds(pl.multiple_of(seq * length + me * piece, piece), piece) for seq in range(seqs)]
    owned = [slice(seq * piece, (seq + 1) * piece) for seq in range(seqs)]

    def slab_spot(ref, at):
        return lambda index: ref.at[rows_of(index, share), at]

    def half_rows(index, side):
        return pl.ds(pl.multiple_of(index * share + side * half, half), half)

    def token_spot(ref, seq):
        return lambda index: ref.at[:, pl.ds(pl.multiple_of(seq * length + index * piece, piece), piece)]

    def token_part(ref, seq):
        return lambda index: ref.at[seq * rows + index]

    class Gather:
        def __init__(self, sends, receives, seq, source, spot):
            self.sems = (sends.at[seq], receives.at[seq])
            self.spot = spot
            self.copies = gather_one(source, spot, *self.sems)

        def two(self):
            gather_two(self.copies, self.spot, *self.sems)

        def end(self):
            gather_end(self.copies)

    class Reduce:
        def __init__(self, sends, receives, got, middle, seq, part):
            self.sems = (sends.at[seq], receives.at[seq])
            self.got, self.middle = got.at[seq], middle.at[seq]
            self.part = part
            self.copies = reduce_one(part, self.got, *self.sems)

        def two(self):
            reduce_two(self.copies, self.part, self.got, self.middle, *self.sems)

        def end(self):
            return reduce_end(self.copies, self.part, self.got)

    def swap(source, target, send_sem, recv_sem):
        @pl.when(stays)
        def _():
            keep(source, target, recv_sem)

        @pl.when(jnp.logical_not(stays))
        def _():
            remote(swap_id, source, target, send_sem, recv_sem)

    def swap_sent(source, send_sem):
        @pl.when(jnp.logical_not(stays))
        def _():
            pltpu.make_async_copy(source, source, send_sem).wait()

    def landed(block, sem):
        pltpu.make_async_copy(block, block, sem).wait()

    wa_ref, vec_own, tip_own = r.wa_own, r.vec_own, r.tip_own
    for index in range(3):
        wa_ref[:, index * head_cols : (index + 1) * head_cols] = r.wq[index]
    wa_ref[:, 3 * head_cols :] = r.wo[...].T
    vec_own[...] = jnp.zeros_like(vec_own)
    vec_own[0:2, :share] = r.gains[...]
    vec_own[2:6, :share] = r.biases[...]
    tip_own[...] = jnp.zeros_like(tip_own)
    tip_own[0:2, :head_cols] = r.qv_bias[...]
    lanes = tip_own.shape[1]
    for index in range(hidden // lanes):
        tip_own[2 + index : 3 + index, :] = r.up_bias[:, index * lanes : (index + 1) * lanes]
    weights = ((wa_ref, wa_all), (r.wu, wu_all), (r.wd, wd_all))
    zbuf, relay = r.zbuf, r.relay
    near_id, over_id, twin_id = {"row": near_row}, {"row": over_row}, {"dp": twin}
    weight_copies = []

    def spread(index):
        own, _ = weights[index]
        mine = own.at[pl.ds(pl.multiple_of(core * half, half), half)]
        keep(mine, zbuf.at[index, col], in_sems.wz.at[index, col])
        for step, peer in enumerate(col_peers):
            weight_copies.append(
                send("col", peer, mine, zbuf.at[index, col], out_sems.wz.at[index, step], in_sems.wz.at[index, col])
            )

    def weight_move(index, slot, target_id, source, target):
        weight_copies.append(
            remote(target_id, source, target, out_sems.wm.at[index, slot], in_sems.wm.at[index, slot])
        )

    def weight_one(index):
        _, whole = weights[index]
        wait_recv_all(zbuf.at[0, 0], in_sems.wz.at[index], cols)
        here = whole.at[half_rows(row, core)]
        away = 1 - home
        weight_move(index, 0, near_id, zbuf.at[index, away + 2 * core], here)
        weight_move(index, 1, near_id, zbuf.at[index, away + 2 * twin], relay.at[index, 0])
        weight_move(index, 2, over_id, zbuf.at[index, home + 2 * core], here)
        weight_move(index, 3, over_id, zbuf.at[index, home + 2 * twin], relay.at[index, 1])
        weight_move(index, 6, twin_id, zbuf.at[index, home + 2 * twin], here)
        keep(zbuf.at[index, home + 2 * core], here, in_sems.wl.at[index])

    def weight_two(index):
        _, whole = weights[index]
        block = zbuf.at[0, 0]
        there = whole.at[half_rows(near_row, core)]
        landed(block, in_sems.wm.at[index, 0])
        weight_move(index, 4, over_id, there, there)
        landed(block, in_sems.wm.at[index, 1])
        weight_move(index, 5, over_id, relay.at[index, 0], relay.at[index, 2])
        weight_move(index, 7, twin_id, relay.at[index, 0], there)

    def weight_three(index):
        _, whole = weights[index]
        block = zbuf.at[0, 0]
        landed(block, in_sems.wm.at[index, 3])
        weight_move(index, 8, twin_id, relay.at[index, 1], whole.at[half_rows(over_row, core)])
        landed(block, in_sems.wm.at[index, 5])
        weight_move(index, 9, twin_id, relay.at[index, 2], whole.at[half_rows(3 - row, core)])

    def weight_end(index):
        block = zbuf.at[0, 0]
        landed(block, in_sems.wl.at[index])
        for slot in (2, 4, 6, 7, 8, 9):
            landed(block, in_sems.wm.at[index, slot])

    meet(swap_id)
    spread(0)
    x_own, c_own = r.x_own, r.c_own
    for seq, at in enumerate(spans):
        swap(x_ref.at[:, at], x_own.at[:, at], out_sems.xs.at[seq], in_sems.xs.at[seq])
    keep(vec_own, r.vec_all.at[row], in_sems.vec.at[row])
    keep(tip_own, r.tip_all.at[col], in_sems.tip.at[col])
    small_copies = [
        send("row", peer, vec_own, r.vec_all.at[row], out_sems.vec.at[step], in_sems.vec.at[row])
        for step, peer in enumerate(row_peers)
    ] + [
        send("col", peer, tip_own, r.tip_all.at[col], out_sems.tip.at[step], in_sems.tip.at[col])
        for step, peer in enumerate(col_peers)
    ]
    xs, cots = [], []
    for seq, at in enumerate(spans):
        landed(x_ref.at[:, at], in_sems.xs.at[seq])
        xs.append(Gather(out_sems.x, in_sems.x, seq, x_own.at[:, at], slab_spot(x_all, at)))
    swap(c_ref, c_own, out_sems.cs.at[0], in_sems.cs.at[0])
    x_all[slab, :] = x_own[...]
    wait_recv_all(vec_own, in_sems.vec, rows)
    for index in range(rows):
        flipped = r.vec_all[index].T
        vcol_ref[index * share : (index + 1) * share, :] = flipped[:share]
    wait_recv_all(tip_own, in_sems.tip, cols)
    tip = r.tip_all[me].T
    bias_q, bias_v = tip[:head_cols, 0:1], tip[:head_cols, 1:2]
    for index in range(hidden // lanes):
        tcol_ref[index * lanes : (index + 1) * lanes, :] = jnp.broadcast_to(
            tip[:, 2 + index : 3 + index], (lanes, 8)
        )
    xs[0].two()
    weight_one(0)
    spread(1)
    xs[1].two()

    def first_norm(step, carry):
        at = pl.ds(pl.multiple_of(step * chunk, chunk), chunk)
        values = x_all[:, at].astype(full)
        center = jnp.mean(values, axis=0, keepdims=True)
        offset = values - center
        inverse = lax.rsqrt(jnp.mean(offset * offset, axis=0, keepdims=True) + EPSILON)
        ln_ref[:, at] = (offset * inverse * vcol_ref[:, 0:1] + vcol_ref[:, 2:3]).astype(low)
        stat_ref[0:1, at] = center
        stat_ref[1:2, at] = inverse
        return carry

    def project(step, carry):
        at = pl.ds(pl.multiple_of(step * chunk, chunk), chunk)
        mixed = left_t(wa_all[:, : 3 * head_cols], ln_ref[:, at])
        qkv_ref[:head_cols, at] = ((mixed[:head_cols] + bias_q) * HEAD**-0.5).astype(low)
        qkv_ref[head_cols : 2 * head_cols, at] = mixed[head_cols : 2 * head_cols].astype(low)
        qkv_ref[2 * head_cols :, at] = (mixed[2 * head_cols :] + bias_v).astype(low)
        return carry

    def causal(part_q):
        keys = (part_q + 1) * chunk
        key_at = lax.broadcasted_iota(jnp.int32, (keys, chunk), 0)
        return key_at <= lax.broadcasted_iota(jnp.int32, (keys, chunk), 1) + part_q * chunk

    def attend(seq, between):
        for head in range(heads):
            at = head * HEAD
            for part_q in range(2):
                here = pl.ds(seq * length + part_q * chunk, chunk)
                span = pl.ds(seq * length, (part_q + 1) * chunk)
                scores = left_t(qkv_ref[pl.ds(at + head_cols, HEAD), span], qkv_ref[pl.ds(at, HEAD), here])
                scores = jnp.where(causal(part_q), scores, -1e30)
                summit = jnp.max(scores, axis=0, keepdims=True)
                expos = jnp.exp(scores - summit)
                total = jnp.sum(expos, axis=0, keepdims=True)
                mixed = plain(qkv_ref[pl.ds(at + 2 * head_cols, HEAD), span], expos.astype(low))
                att_ref[pl.ds(at, HEAD), here] = (mixed / total).astype(low)
                lse_ref[seq * heads + head, :, pl.ds(part_q * chunk, chunk)] = jnp.broadcast_to(
                    summit + jnp.log(total), (8, chunk)
                )
            for step in between.get(head, ()):
                step()

    xs[0].end()
    lax.fori_loop(0, 2, first_norm, 0)
    weight_two(0)
    xs[1].end()
    lax.fori_loop(2, 4, first_norm, 0)
    landed(c_ref, in_sems.cs.at[0])
    for seq, at in enumerate(spans):
        cots.append(Gather(out_sems.c, in_sems.c, seq, c_own.at[:, at], slab_spot(c_all, at)))
    c_all[slab, :] = c_own[...]
    weight_one(1)
    spread(2)
    weight_three(0)
    weight_end(0)
    outs = []
    between = [
        {1: [lambda: weight_two(1)], 2: [gather.two for gather in cots]},
        {0: [lambda: weight_one(2)], 1: [lambda: weight_three(1)]},
    ]
    for seq in range(seqs):
        lax.fori_loop(2 * seq, 2 * seq + 2, project, 0)
        if seq == 1:
            outs[0].two()
        attend(seq, between[seq])
        mixed = plain(wa_all[:, 3 * head_cols :], att_ref[:, seq * length : (seq + 1) * length])
        for index in range(rows):
            r.o_part[seq * rows + index] = mixed[:, index * piece : (index + 1) * piece].astype(low)
        outs.append(Reduce(out_sems.o, in_sems.o, r.o_got, r.o_middle, seq, token_part(r.o_part, seq)))
    l2s = []

    def second_norm(seq):
        middle = x_all[:, owns[seq]].astype(full) + outs[seq].end() + vcol_ref[:, 4:5]
        x1_ref[:, owned[seq]] = middle
        center = jnp.mean(middle, axis=0, keepdims=True)
        offset = middle - center
        inverse = lax.rsqrt(jnp.mean(offset * offset, axis=0, keepdims=True) + EPSILON)
        l2_ref[:, owns[seq]] = (offset * inverse * vcol_ref[:, 1:2] + vcol_ref[:, 3:4]).astype(low)
        spot = token_spot(l2_ref, seq)
        l2s.append(Gather(out_sems.l, in_sems.l, seq, spot(me), spot))

    second_norm(0)
    outs[1].two()
    weight_end(1)
    wu_t, wd_t, g_part = r.wu_t, r.wd_t, r.g_part
    wu_t[...] = wu_all[...].T
    weight_two(2)
    second_norm(1)

    pieces = chunk // piece

    def forward(step, carry):
        at = pl.ds(pl.multiple_of(step * chunk, chunk), chunk)
        before = plain(wu_t[...], l2_ref[:, at]) + tcol_ref[:, 0:1]
        square = before * before
        tanh = jnp.tanh(GELU_COEF * (before + 0.044715 * before * square))
        hid[:, at] = (0.5 * before * (1.0 + tanh)).astype(low)
        r.slope[:, at] = 0.5 * (1.0 + tanh) + 0.5 * before * (1.0 - tanh * tanh) * (
            GELU_COEF * (1.0 + 3.0 * 0.044715 * square)
        )
        return carry

    def returning(step, carry):
        at = pl.ds(pl.multiple_of(step * chunk, chunk), chunk)
        grad = (plain(wd_t[...], c_all[:, at]) * r.slope[:, at]).astype(low)
        gra[:, at] = grad
        backs = plain(wu_all[...], grad)
        for index in range(pieces):
            g_part[step * pieces + index] = backs[:, index * piece : (index + 1) * piece].astype(low)
        return carry

    def finish(step, carry):
        at = pl.ds(pl.multiple_of(step * chunk, chunk), chunk)
        y_ref[:, at] = plain(wd_all[...], hid[:, at]).astype(low)
        return carry

    block = width // 4

    def up_weight(step, carry):
        place = pl.ds(pl.multiple_of(step * block, block), block)
        r.du[place, :] = right_t(l2_ref[place, :], gra[...]).astype(low)
        return carry

    def down_weight(step, carry):
        place = pl.ds(pl.multiple_of(step * block, block), block)
        r.dd[place, :] = right_t(c_all[place, :], hid[...]).astype(low)
        return carry

    grads = (r.du, r.dd, r.da)
    finals = (r.gu, r.gd, r.ga)
    pair, over, aside, plane, line = r.pair, r.over, r.aside, r.plane, r.line
    grad_copies = []
    quarter = half // 2
    parts = ((0, 0, half), (1, 0, half), (2, 0, quarter), (2, quarter, quarter))
    grad_blocks = [pair.at[0, 0, 0:size] for _, _, size in parts]

    def part_rows(part, block_row, side):
        _, start, size = parts[part]
        return pl.ds(pl.multiple_of(block_row * share + side * half + start, size), size)

    def cutter(part):
        index, start, size = parts[part]
        return lambda ref, slot: ref.at[index, slot, start : start + size]

    def pair_start(part):
        index, start, size = parts[part]
        cut = cutter(part)
        for block_row in range(rows):
            grad_copies.append(
                remote(
                    twin_id,
                    grads[index].at[part_rows(part, block_row, twin)],
                    cut(pair, block_row),
                    out_sems.pair.at[part, block_row],
                    in_sems.pair.at[part, block_row],
                )
            )

    def pair_finish(part):
        index, start, size = parts[part]
        cut = cutter(part)
        wait_recv_all(grad_blocks[part], in_sems.pair.at[part], rows)
        for slot, block_row in enumerate((over_row, 3 - row)):
            moves = ((0, grads[index].at[part_rows(part, block_row, core)]), (1, cut(pair, block_row)))
            for which, source in moves:
                place_at = 2 * slot + which
                grad_copies.append(
                    remote(
                        over_id,
                        source,
                        cut(over, place_at),
                        out_sems.over.at[part, place_at],
                        in_sems.over.at[part, place_at],
                    )
                )

    def over_finish(part):
        index, start, size = parts[part]
        cut = cutter(part)
        for slot, block_row in ((1, near_row), (0, row)):
            for which, owner in ((0, core), (1, twin)):
                landed(grad_blocks[part], in_sems.over.at[part, 2 * slot + which])
                if which == 0:
                    mine = grads[index][part_rows(part, block_row, core), :].astype(full)
                else:
                    mine = cut(pair, block_row)[...].astype(full)
                total = (mine + cut(over, 2 * slot + which)[...].astype(full)).astype(low)
                if slot == 0:
                    cut(plane, home + 2 * owner)[...] = total
                else:
                    cut(aside, which)[...] = total
                    grad_copies.append(
                        remote(
                            near_id,
                            cut(aside, which),
                            cut(plane, home + 2 * owner),
                            out_sems.aside.at[part, which],
                            in_sems.aside.at[part, which],
                        )
                    )

    def line_start(part):
        index, start, size = parts[part]
        cut = cutter(part)
        wait_recv_all(grad_blocks[part], in_sems.aside.at[part], 2)
        keep(cut(plane, col), cut(line, col), in_sems.line.at[part, col])
        for step, peer in enumerate(col_peers):
            grad_copies.append(
                send(
                    "col",
                    peer,
                    cut(plane, peer),
                    cut(line, col),
                    out_sems.line.at[part, step],
                    in_sems.line.at[part, col],
                )
            )

    def line_finish(part):
        index, start, size = parts[part]
        cut = cutter(part)
        wait_recv_all(grad_blocks[part], in_sems.line.at[part], cols)
        total = cut(line, 0)[...].astype(full)
        for other in range(1, cols):
            total = total + cut(line, other)[...].astype(full)
        at = pl.ds(pl.multiple_of(core * half + start, size), size)
        finals[index][at, :] = total
        grad_copies.append(
            remote(
                twin_id,
                finals[index].at[at],
                finals[index].at[at],
                out_sems.final.at[part],
                in_sems.final.at[part],
            )
        )

    gls = []
    l2s[0].two()
    l2s[0].end()
    lax.fori_loop(0, 2, forward, 0)
    l2s[1].two()
    weight_three(2)
    l2s[1].end()
    lax.fori_loop(2, 4, forward, 0)
    weight_end(2)
    wd_t[...] = wd_all[...].T
    for seq in range(seqs):
        cots[seq].end()
        lax.fori_loop(2 * seq, 2 * seq + 2, returning, 0)
        gls.append(Reduce(out_sems.g, in_sems.g, r.g_got, r.g_middle, seq, token_part(g_part, seq)))
        if seq == 1:
            gls[0].two()
    lax.fori_loop(0, 4, up_weight, 0)
    pair_start(0)
    gls[1].two()
    lax.fori_loop(0, 4, down_weight, 0)
    pair_start(1)
    pair_finish(0)
    gxs = []
    sums = [0.0] * 4
    for seq in range(seqs):
        grad = gls[seq].end()
        middle = x1_ref[:, owned[seq]]
        center = jnp.mean(middle, axis=0, keepdims=True)
        offset = middle - center
        inverse = lax.rsqrt(jnp.mean(offset * offset, axis=0, keepdims=True) + EPSILON)
        normal = offset * inverse
        scaled = grad * vcol_ref[:, 1:2]
        first = jnp.mean(scaled, axis=0, keepdims=True)
        second = jnp.mean(scaled * normal, axis=0, keepdims=True)
        outer = c_all[:, owns[seq]].astype(full)
        result = (outer + inverse * (scaled - first - normal * second)).astype(low)
        gx_ref[:, owns[seq]] = result
        spot = token_spot(gx_ref, seq)
        gxs.append(Gather(out_sems.gx, in_sems.gx, seq, spot(me), spot))
        terms = (grad * normal, grad, result.astype(full), outer)
        sums = [old + new for old, new in zip(sums, terms)]
    pack_own = r.pack_own
    pack_own[...] = jnp.zeros_like(pack_own)
    for index in range(4):
        pack_own[index : index + 1, :] = lane_sums(sums[index])[0:1]
    pair_finish(1)
    gxs[0].two()
    gxs[1].two()
    lax.fori_loop(0, 2 * seqs, finish, 0)
    for seq in range(seqs):
        y_own = plain(wd_all[...], hid[:, owns[seq]]) + x1_ref[:, owned[seq]] + vcol_ref[:, 5:6]
        y_ref[:, owns[seq]] = y_own.astype(low)

    def head_side(step, carry):
        at = pl.ds(pl.multiple_of(step * chunk, chunk), chunk)
        mixed_grad[:, at] = left_t(wa_all[:, 3 * head_cols :], gx_ref[:, at]).astype(low)
        return carry

    def attend_back(seq, between):
        for head in range(heads):
            at = head * HEAD
            key_rows = pl.ds(at + head_cols, HEAD)
            value_rows = pl.ds(at + 2 * head_cols, HEAD)
            kept = []
            for part_q in range(2):
                here = pl.ds(seq * length + part_q * chunk, chunk)
                span = pl.ds(seq * length, (part_q + 1) * chunk)
                queries = qkv_ref[pl.ds(at, HEAD), here]
                key = qkv_ref[key_rows, span]
                outer = mixed_grad[pl.ds(at, HEAD), here]
                shift = lse_ref[seq * heads + head, 0:1, pl.ds(part_q * chunk, chunk)]
                probs = jnp.exp(jnp.where(causal(part_q), left_t(key, queries) - shift, -1e30))
                delta = jnp.sum(
                    outer.astype(full) * att_ref[pl.ds(at, HEAD), here].astype(full), axis=0, keepdims=True
                )
                slope = (probs * (left_t(qkv_ref[value_rows, span], outer) - delta)).astype(low)
                head_grad[pl.ds(at, HEAD), here] = (plain(key, slope) * HEAD**-0.5).astype(low)
                kept.append((right_t(queries, slope), right_t(outer, probs.astype(low))))
            early, late = pl.ds(seq * length, chunk), pl.ds(seq * length + chunk, chunk)
            for place, index in ((key_rows, 0), (value_rows, 1)):
                second = kept[1][index]
                head_grad[place, early] = (second[:, :chunk] + kept[0][index]).astype(low)
                head_grad[place, late] = second[:, chunk:].astype(low)
            for step in between.get(head, ()):
                step()

    def backward(step, carry):
        at = pl.ds(pl.multiple_of(step * chunk, chunk), chunk)
        back[:, at] = plain(wa_all[:, : 3 * head_cols], head_grad[:, at]).astype(low)
        return carry

    def mixed_weight(step, carry):
        place = pl.ds(pl.multiple_of(step * block, block), block)
        r.da[place, : 3 * head_cols] = right_t(ln_ref[place, :], head_grad[...]).astype(low)
        r.da[place, 3 * head_cols :] = right_t(gx_ref[place, :], att_ref[...]).astype(low)
        return carry

    ones = []
    between = [
        {1: [lambda: over_finish(0)]},
        {0: [lambda: ones[0].two()], 1: [lambda: line_start(0)], 2: [lambda: over_finish(1)]},
    ]
    for seq in range(seqs):
        gxs[seq].end()
        lax.fori_loop(2 * seq, 2 * seq + 2, head_side, 0)
        attend_back(seq, between[seq])
        lax.fori_loop(2 * seq, 2 * seq + 2, backward, 0)
        ones.append(Reduce(out_sems.n, in_sems.n, r.n_got, r.n_middle, seq, slab_spot(back, spans[seq])))
    lax.fori_loop(0, 4, mixed_weight, 0)
    pair_start(2)
    pair_start(3)
    ones[1].two()
    line_start(1)
    pair_finish(2)

    count = jnp.ones((8, tokens), low)
    pack_own[6:7, :hidden] = right_t(count, gra[...])[0:1]
    pack_own[7:8, : 3 * head_cols] = right_t(count, head_grad[...])[0:1]
    stat_own, stat_side, stat_near, stat_sum = r.stat_own, r.stat_side, r.stat_near, r.stat_sum
    gain = vcol_ref[slab, 0:1]
    stat_own[...] = jnp.zeros_like(stat_own)
    scale_sum, shift_sum = 0.0, 0.0
    saved = []
    for seq, at in enumerate(spans):
        grad = ones[seq].end()
        normal = (x_own[:, at].astype(full) - stat_ref[0:1, at]) * stat_ref[1:2, at]
        scaled = grad * gain
        stat_own[0:1, at] = jnp.sum(scaled, axis=0, keepdims=True)
        stat_own[1:2, at] = jnp.sum(scaled * normal, axis=0, keepdims=True)
        saved.append((scaled, normal))
        scale_sum = scale_sum + grad * normal
        shift_sum = shift_sum + grad
    stat_copies = [remote(twin_id, stat_own, stat_side, out_sems.stat.at[0], in_sems.stat.at[0])]
    pack_own[4:5, :share] = lane_sums(scale_sum)[0:1]
    pack_own[5:6, :share] = lane_sums(shift_sum)[0:1]
    stat_copies[0].wait_recv()
    stat_sum[...] = stat_own[...] + stat_side[...]
    stat_copies.append(remote(near_id, stat_sum, stat_near, out_sems.stat.at[1], in_sems.stat.at[1]))
    pack_all, mid_own, mid_pair, blocks = r.pack_all, r.mid_own, r.mid_pair, r.blocks
    keep(pack_own, pack_all.at[row], in_sems.pack.at[row])
    small_copies += [
        send("row", peer, pack_own, pack_all.at[row], out_sems.pack.at[step], in_sems.pack.at[row])
        for step, peer in enumerate(row_peers)
    ]
    over_finish(2)
    pair_finish(3)
    ys = Reduce(out_sems.y, in_sems.y, r.y_got, r.y_middle, 0, slab_spot(y_ref, pl.ds(0, tokens)))
    stat_copies[1].wait_recv()
    total = (stat_sum[...] + stat_near[...]) * (1.0 / width)
    for seq, at in enumerate(spans):
        scaled, normal = saved[seq]
        here = slice(seq * length, (seq + 1) * length)
        result = stat_ref[1:2, at] * (scaled - total[0:1, here] - normal * total[1:2, here])
        r.gin_own[:, at] = (gx_ref[slab, at].astype(full) + result).astype(low)
    for seq, at in enumerate(spans):
        swap_sent(x_ref.at[:, at], out_sems.xs.at[seq])
    swap(r.gin_own, r.gin, out_sems.gs.at[0], in_sems.gs.at[0])
    wait_recv_all(pack_own, in_sems.pack, rows)
    total = pack_all[0, 0:4]
    for index in range(1, rows):
        total = total + pack_all[index, 0:4]
    mid_own[0, 4:8] = total
    for index in range(2):
        mid_own[index, 0:4] = pack_all[index, 4:8] + pack_all[2 + index, 4:8]
    mid_own[1, 4:8] = total
    small_copies.append(remote(twin_id, mid_own, mid_pair, out_sems.mid.at[0], in_sems.mid.at[0]))
    line_start(2)
    ys.two()
    landed(mid_own, in_sems.mid.at[0])
    total = mid_own[0, 4:8] + mid_pair[0, 4:8]
    for index in range(2):
        blocks[2 * core + index, 0:4] = mid_own[index, 0:4]
        blocks[2 * twin + index, 0:4] = mid_pair[index, 0:4]
    for index in range(rows):
        blocks[index, 4:8] = total
    a_all, b_all = r.a_all, r.b_all
    keep(blocks.at[row], a_all.at[col], in_sems.t.at[0, col])
    keep(blocks.at[col], b_all.at[col], in_sems.t.at[1, col])
    for step, peer in enumerate(col_peers):
        small_copies += [
            send("col", peer, blocks.at[row], a_all.at[col], out_sems.t.at[0, step], in_sems.t.at[0, col]),
            send("col", peer, blocks.at[peer], b_all.at[col], out_sems.t.at[1, step], in_sems.t.at[1, col]),
        ]
    over_finish(3)
    line_finish(0)
    line_finish(1)
    line_start(3)
    wait_recv_all(pack_own, in_sems.t.at[0], cols)
    wait_recv_all(pack_own, in_sems.t.at[1], cols)
    a_total, b_total = a_all[0], b_all[0]
    for index in range(1, cols):
        a_total, b_total = a_total + a_all[index], b_total + b_all[index]
    wide = jnp.zeros((4, share), full)
    for index in range(rows):
        wide = wide + jnp.where(row == index, a_total[4:8, index * share : (index + 1) * share], 0.0)
    r.g_gains[0:1, :] = a_total[0:1, :share]
    r.g_gains[1:2, :] = wide[0:1]
    r.g_biases[0:1, :] = a_total[1:2, :share]
    r.g_biases[1:4, :] = wide[1:4]
    r.g_up_bias[...] = b_total[2, :hidden]
    r.g_qv[0:1, :] = b_total[3:4, :head_cols]
    r.g_qv[1:2, :] = b_total[3:4, 2 * head_cols : 3 * head_cols]
    r.out_own[...] = ys.end().astype(low)
    swap_sent(c_ref, out_sems.cs.at[0])
    swap(r.out_own, r.out, out_sems.gs.at[1], in_sems.gs.at[1])
    line_finish(2)
    line_finish(3)
    for part, (index, _, size) in enumerate(parts):
        landed(finals[index].at[pl.ds(0, size)], in_sems.final.at[part])
    for index in range(3):
        r.g_wq[index] = r.ga[:, index * head_cols : (index + 1) * head_cols]
    r.g_wo[...] = r.ga[:, 3 * head_cols :].T
    landed(r.gin, in_sems.gs.at[0])
    landed(r.out, in_sems.gs.at[1])
    swap_sent(r.gin, out_sems.gs.at[0])
    swap_sent(r.out, out_sems.gs.at[1])
    sent(small_copies, stat_copies, weight_copies, grad_copies)
    sent(*[move.copies for move in xs + cots + outs + l2s + gls + gxs + ones + [ys]])


def settle_kernel(count, *refs):
    for index in range(count):
        refs[count + index][...] = refs[index][...]


def settle(arrays):
    count = len(arrays)
    return pl.pallas_call(
        functools.partial(settle_kernel, count),
        out_shape=[jax.ShapeDtypeStruct(array.shape, array.dtype) for array in arrays],
        in_specs=[pl.BlockSpec(memory_space=pltpu.VMEM)] * count,
        out_specs=[pl.BlockSpec(memory_space=pltpu.VMEM)] * count,
    )(*arrays)


def square_body(
    block_input, norm_gains, row_biases, w_qkv, qv_bias, w_out, w_up, up_bias, w_down, cotangent
):
    low, full = jnp.bfloat16, jnp.float32
    share, tokens = block_input.shape
    rows, cols = lax.axis_size("row"), lax.axis_size("col")
    width = share * rows
    head_cols = w_out.shape[0]
    mixed = 3 * head_cols + share
    hidden = w_up.shape[1]
    seqs = tokens // LENGTH
    heads = head_cols // HEAD
    piece = LENGTH // rows
    half = share // 2
    lanes = -(-share // 128) * 128
    tips = -(-(2 + hidden // lanes) // 8) * 8
    inputs = dict(
        x=block_input,
        c=cotangent,
        gains=norm_gains,
        biases=row_biases,
        qv_bias=qv_bias,
        up_bias=up_bias.reshape(1, -1),
        wq=w_qkv.transpose(1, 0, 2),
        wo=w_out,
        wu=w_up,
        wd=w_down,
    )
    outputs = dict(
        out=((share, tokens), low),
        gin=((share, tokens), low),
        g_gains=((2, share), full),
        g_biases=((4, share), full),
        g_wq=((3, share, head_cols), full),
        g_qv=((2, head_cols), full),
        g_wo=((head_cols, share), full),
        gu=((share, hidden), full),
        g_up_bias=((hidden,), full),
        gd=((share, hidden), full),
    )
    token_got, token_middle = (seqs, 3, width, piece), (seqs, width, piece)
    buffers = dict(
        x_all=((width, tokens), low),
        c_all=((width, tokens), low),
        wa_all=((width, mixed), low),
        wu_all=((width, hidden), low),
        wd_all=((width, hidden), low),
        ln=((width, tokens), low),
        qkv=((3 * head_cols, tokens), low),
        att=((head_cols, tokens), low),
        lse=((seqs * heads, 8, LENGTH), full),
        stat=((8, tokens), full),
        x1=((width, seqs * piece), full),
        l2=((width, tokens), low),
        gx=((width, tokens), low),
        vcol=((width, 8), full),
        tcol=((hidden, 8), full),
        wa_own=((share, mixed), low),
        vec_own=((8, lanes), full),
        tip_own=((tips, lanes), full),
        vec_all=((rows, 8, lanes), full),
        tip_all=((cols, tips, lanes), full),
        zbuf=((3, cols, half, mixed), low),
        relay=((3, 3, half, mixed), low),
        x_own=((share, tokens), low),
        c_own=((share, tokens), low),
        gin_own=((share, tokens), low),
        out_own=((share, tokens), low),
        o_part=((seqs * rows, width, piece), low),
        o_got=(token_got, low),
        o_middle=(token_middle, low),
        wu_t=((hidden, width), low),
        wd_t=((hidden, width), low),
        hid=((hidden, tokens), low),
        gra=((hidden, tokens), low),
        slope=((hidden, tokens), full),
        g_part=((seqs * rows, width, piece), low),
        g_got=(token_got, low),
        g_middle=(token_middle, low),
        y=((width, tokens), low),
        y_got=((1, 3, share, tokens), low),
        y_middle=((1, share, tokens), low),
        du=((width, hidden), low),
        dd=((width, hidden), low),
        da=((width, mixed), low),
        pack_own=((8, width), full),
        mixed_grad=((head_cols, tokens), low),
        head_grad=((3 * head_cols, tokens), low),
        back=((width, tokens), low),
        n_got=((seqs, 3, share, LENGTH), low),
        n_middle=((seqs, share, LENGTH), low),
        ga=((share, mixed), full),
        stat_own=((8, tokens), full),
        stat_side=((8, tokens), full),
        stat_near=((8, tokens), full),
        stat_sum=((8, tokens), full),
        pair=((3, rows, half, mixed), low),
        over=((3, 4, half, mixed), low),
        aside=((3, 2, half, mixed), low),
        plane=((3, cols, half, mixed), low),
        line=((3, cols, half, mixed), low),
        pack_all=((rows, 8, width), full),
        mid_own=((2, 8, width), full),
        mid_pair=((2, 8, width), full),
        blocks=((rows, 8, width), full),
        a_all=((cols, 8, width), full),
        b_all=((cols, 8, width), full),
    )
    arrivals = dict(
        x=((seqs, 3), (seqs, 3)),
        c=((seqs, 3), (seqs, 3)),
        l=((seqs, 3), (seqs, 3)),
        gx=((seqs, 3), (seqs, 3)),
        o=((seqs, 3), (seqs, 3)),
        g=((seqs, 3), (seqs, 3)),
        n=((seqs, 3), (seqs, 3)),
        y=((1, 3), (1, 3)),
        xs=((seqs,), (seqs,)),
        cs=((1,), (1,)),
        gs=((2,), (2,)),
        vec=((rows - 1,), (rows,)),
        tip=((cols - 1,), (cols,)),
        wz=((3, cols - 1), (3, cols)),
        wm=((3, 10), (3, 10)),
        wl=((3,), (3,)),
        pair=((4, rows), (4, rows)),
        over=((4, 4), (4, 4)),
        aside=((4, 2), (4, 2)),
        line=((4, cols - 1), (4, cols)),
        final=((4,), (4,)),
        stat=((2,), (2,)),
        pack=((rows - 1,), (rows,)),
        mid=((1,), (1,)),
        t=((2, cols - 1), (2, cols)),
    )
    names = (list(inputs) + list(outputs) + list(buffers), list(arrivals))
    scratch = [pltpu.VMEM(*shape) for shape in buffers.values()]
    for sends, receives in arrivals.values():
        scratch += [pltpu.SemaphoreType.DMA(sends), pltpu.SemaphoreType.DMA(receives)]
    results = pl.pallas_call(
        functools.partial(block_kernel, names, seqs),
        out_shape=[jax.ShapeDtypeStruct(*shape) for shape in outputs.values()],
        in_specs=[pl.BlockSpec(memory_space=pltpu.VMEM)] * len(inputs),
        out_specs=[pl.BlockSpec(memory_space=pltpu.VMEM)] * len(outputs),
        scratch_shapes=scratch,
        compiler_params=pltpu.CompilerParams(
            collective_id=0, has_side_effects=True, vmem_limit_bytes=BIG
        ),
    )(*inputs.values())
    out, gin, gains, biases, g_wq, g_qv, g_wo, gu, g_up_bias, gd = settle(results)
    return (out, gin, gains, biases, g_wq.transpose(1, 0, 2), g_qv, g_wo, gu, g_up_bias, gd)


def fits(mesh):
    sizes = mesh.shape
    return sizes["row"] == 4 and sizes["col"] == 4 and sizes["dp"] == 2


def solution(mesh):
    in_specs = (
        P("row", ("dp", "col")),
        P(None, "row"),
        P(None, "row"),
        P("row", None, "col"),
        P(None, "col"),
        P("col", "row"),
        P("row", "col"),
        P("col"),
        P("row", "col"),
        P("row", ("dp", "col")),
    )
    out_specs = (
        P("row", ("dp", "col")),
        P("row", ("dp", "col")),
        P(None, "row"),
        P(None, "row"),
        P("row", None, "col"),
        P(None, "col"),
        P("col", "row"),
        P("row", "col"),
        P("col"),
        P("row", "col"),
    )
    chosen = square_body if fits(mesh) else body
    return jax.shard_map(chosen, mesh=mesh, in_specs=in_specs, out_specs=out_specs, check_vma=False)
```

```python
import functools
import types

import jax
import jax.numpy as jnp
from jax import lax
from jax.experimental import pallas as pl
from jax.experimental.pallas import tpu as pltpu
from jax.sharding import PartitionSpec as P

D = 768
HEAD = 64
LENGTH = 512


EPSILON = 1e-05
GELU_COEF = 0.7978845608028654


def gelu_tanh(values):
    return (
        0.5 * values * (1.0 + jnp.tanh(GELU_COEF * (values + 0.044715 * values * values * values)))
    )


def multiply(rows, weight, flipped):
    if flipped:
        return lax.dot_general(
            rows, weight, (((1,), (1,)), ((), ())), preferred_element_type=jnp.float32
        )
    return jnp.dot(rows, weight, preferred_element_type=jnp.float32)


def contract_tokens(left, right):
    return lax.dot_general(
        left, right, (((0,), (0,)), ((), ())), preferred_element_type=jnp.float32
    )


def swap_kernel(axis_name, count, shared, x_ref, o_ref, send_sem, recv_sem, own_sem):
    me = lax.axis_index(axis_name)
    barrier = pltpu.get_barrier_semaphore()
    peers = [lax.rem(me + step, count) for step in range(1, count)]
    for peer in peers:
        pl.semaphore_signal(
            barrier, inc=1, device_id={axis_name: peer}, device_id_type=pl.DeviceIdType.MESH
        )
    own = pltpu.make_async_copy(x_ref if shared else x_ref.at[me], o_ref.at[me], own_sem)
    own.start()
    pl.semaphore_wait(barrier, count - 1)
    copies = []
    for slot, peer in enumerate(peers):
        copy = pltpu.make_async_remote_copy(
            src_ref=x_ref if shared else x_ref.at[peer],
            dst_ref=o_ref.at[me],
            send_sem=send_sem.at[slot],
            recv_sem=recv_sem.at[slot],
            device_id={axis_name: peer},
            device_id_type=pl.DeviceIdType.MESH,
        )
        copy.start()
        copies.append(copy)
    own.wait()
    for copy in copies:
        copy.wait()


def swap(values, axis_name, shared, ident):
    count = lax.axis_size(axis_name)
    block = values.shape if shared else values.shape[1:]
    moved = values.size * values.dtype.itemsize
    return pl.pallas_call(
        functools.partial(swap_kernel, axis_name, count, shared),
        out_shape=jax.ShapeDtypeStruct((count, *block), values.dtype),
        in_specs=[pl.BlockSpec(memory_space=pltpu.VMEM)],
        out_specs=pl.BlockSpec(memory_space=pltpu.VMEM),
        scratch_shapes=[
            pltpu.SemaphoreType.DMA((count - 1,)),
            pltpu.SemaphoreType.DMA((count - 1,)),
            pltpu.SemaphoreType.DMA,
        ],
        compiler_params=pltpu.CompilerParams(collective_id=ident, has_side_effects=True),
        cost_estimate=pl.CostEstimate(
            flops=0, bytes_accessed=(20 if not shared else 60) * moved, transcendentals=0
        ),
    )(values)


def gather_async(local, axis_name):
    return lax.all_gather(local, axis_name, axis=0, tiled=True)


def scatter_sum_async(partial, axis_name):
    return lax.psum_scatter(
        partial.astype(jnp.bfloat16), axis_name, scatter_dimension=0, tiled=True
    ).astype(jnp.float32)


def gather(local, axis_name, ident):
    return swap(local, axis_name, True, ident).reshape(-1, *local.shape[1:])


def scatter_sum(partial, axis_name, ident):
    count = lax.axis_size(axis_name)
    pieces = partial.astype(jnp.bfloat16).reshape(count, -1, *partial.shape[1:])
    return jnp.sum(swap(pieces, axis_name, False, ident).astype(jnp.float32), axis=0)


def to_tokens(first, second, ident):
    rows, cols = lax.axis_size("row"), lax.axis_size("col")
    share = first.shape[0]
    block = jnp.concatenate([first.T, second.T], axis=1).reshape(rows, -1, 2 * share)
    block = swap(block, "row", False, ident)
    if rows != cols:
        moves = [(r * cols + c, c * rows + r) for r in range(rows) for c in range(cols)]
        block = lax.ppermute(block, ("row", "col"), moves)
    first = jnp.concatenate([block[r, :, :share] for r in range(rows)], axis=1)
    second = jnp.concatenate([block[r, :, share:] for r in range(rows)], axis=1)
    return first, second


def to_features(first, second, ident):
    rows, cols = lax.axis_size("row"), lax.axis_size("col")
    share = first.shape[1] // rows
    block = jnp.stack(
        [
            jnp.concatenate(
                [first[:, r * share : (r + 1) * share], second[:, r * share : (r + 1) * share]], axis=1
            )
            for r in range(rows)
        ]
    )
    if rows != cols:
        moves = [(c * rows + r, r * cols + c) for r in range(rows) for c in range(cols)]
        block = lax.ppermute(block, ("row", "col"), moves)
    block = swap(block, "row", False, ident).reshape(-1, 2 * share)
    return block[:, :share].T, block[:, share:].T


def flip(block):
    rows, cols = lax.axis_size("row"), lax.axis_size("col")
    if rows != cols:
        return block
    moves = [(r * cols + c, c * rows + r) for r in range(rows) for c in range(cols)]
    return lax.ppermute(block, ("row", "col"), moves)


def norm_forward(values, gain, bias):
    center = jnp.mean(values, axis=1, keepdims=True)
    offset = values - center
    inverse = lax.rsqrt(jnp.mean(offset * offset, axis=1, keepdims=True) + EPSILON)
    normal = offset * inverse
    return (normal * gain + bias, normal, inverse)


def norm_backward(grad, gain, normal, inverse):
    scaled = grad * gain
    first = jnp.mean(scaled, axis=1, keepdims=True)
    second = jnp.mean(scaled * normal, axis=1, keepdims=True)
    result = inverse * (scaled - first - normal * second)
    return (result, jnp.sum(grad * normal, axis=0), jnp.sum(grad, axis=0))


def causal_mask(length):
    positions = jnp.arange(length)
    return positions[None, :] <= positions[:, None]


def attention_forward(queries, keys, values):
    factor = HEAD ** (-0.5)

    def one_sequence(pieces):
        seq_q, seq_k, seq_v = pieces
        scores = (
            jnp.einsum("qhd,khd->hqk", seq_q, seq_k, preferred_element_type=jnp.float32) * factor
        )
        scores = jnp.where(causal_mask(seq_q.shape[0])[None], scores, -1e30)
        summit = jnp.max(scores, axis=-1, keepdims=True)
        expos = jnp.exp(scores - summit)
        total = jnp.sum(expos, axis=-1, keepdims=True)
        probs = (expos / total).astype(jnp.bfloat16)
        output = jnp.einsum("hqk,khd->qhd", probs, seq_v, preferred_element_type=jnp.float32)
        return (output, summit[..., 0] + jnp.log(total[..., 0]))

    return lax.map(one_sequence, (queries, keys, values))


def attention_backward(queries, keys, values, grad_out, log_sums):
    factor = HEAD ** (-0.5)

    def one_sequence(pieces):
        seq_q, seq_k, seq_v, seq_g, seq_l = pieces
        scores = (
            jnp.einsum("qhd,khd->hqk", seq_q, seq_k, preferred_element_type=jnp.float32) * factor
        )
        scores = jnp.where(causal_mask(seq_q.shape[0])[None], scores, -1e30)
        probs = jnp.exp(scores - seq_l[..., None])
        grad_v = jnp.einsum(
            "hqk,qhd->khd", probs.astype(jnp.bfloat16), seq_g, preferred_element_type=jnp.float32
        )
        grad_p = jnp.einsum("qhd,khd->hqk", seq_g, seq_v, preferred_element_type=jnp.float32)
        inner = jnp.sum(grad_p * probs, axis=-1, keepdims=True)
        grad_s = (probs * (grad_p - inner)).astype(jnp.bfloat16)
        grad_q = (
            jnp.einsum("hqk,khd->qhd", grad_s, seq_k, preferred_element_type=jnp.float32) * factor
        )
        grad_k = (
            jnp.einsum("hqk,qhd->khd", grad_s, seq_q, preferred_element_type=jnp.float32) * factor
        )
        return (grad_q, grad_k, grad_v)

    return lax.map(one_sequence, (queries, keys, values, grad_out, log_sums))


def body(
    block_input, norm_gains, row_biases, w_qkv, qv_bias, w_out, w_up, up_bias, w_down, cotangent
):
    head_cols = w_qkv.shape[2]
    square = lax.axis_size("row") == lax.axis_size("col")
    heads_axis, split_axis = ("row", "col") if square else ("col", "row")
    qv_bias, up_bias = flip(qv_bias), flip(up_bias)
    inputs, cot = to_tokens(block_input, cotangent, 0)
    inputs = inputs.astype(jnp.float32)
    vectors = swap(jnp.concatenate([norm_gains, row_biases], axis=0), "row", True, 1)
    vectors = jnp.concatenate([vectors[r] for r in range(vectors.shape[0])], axis=1)
    gains, biases = vectors[:2], vectors[2:]
    qkv_weight = gather_async(flip(w_qkv.reshape(w_qkv.shape[0], -1)), split_axis)
    rest = gather_async(flip(jnp.concatenate([w_out.T, w_up, w_down], axis=1)), split_axis)
    width = w_up.shape[1]
    out_t = rest[:, :head_cols]
    up = rest[:, head_cols : head_cols + width]
    down = rest[:, head_cols + width :]

    normed_one, normal_one, inverse_one = norm_forward(inputs, gains[0], biases[0])
    source_one = gather(normed_one.astype(jnp.bfloat16), heads_axis, 2)
    qkv_sum = multiply(source_one, qkv_weight, False)
    rows_here = qkv_sum.shape[0]
    qkv_sum = qkv_sum.reshape(rows_here, 3, head_cols)
    shape_four = (rows_here // LENGTH, LENGTH, head_cols // HEAD, HEAD)
    queries = (qkv_sum[:, 0] + qv_bias[0]).astype(jnp.bfloat16).reshape(shape_four)
    keys_all = qkv_sum[:, 1].astype(jnp.bfloat16).reshape(shape_four)
    values_all = (qkv_sum[:, 2] + qv_bias[1]).astype(jnp.bfloat16).reshape(shape_four)
    attended, log_sums = attention_forward(queries, keys_all, values_all)
    attended_low = attended.reshape(rows_here, head_cols).astype(jnp.bfloat16)
    middle = inputs + scatter_sum(multiply(attended_low, out_t, True), heads_axis, 3) + biases[2]
    normed_two, normal_two, inverse_two = norm_forward(middle, gains[1], biases[1])
    source_two = gather(normed_two.astype(jnp.bfloat16), heads_axis, 4)
    cot_all = gather_async(cot, heads_axis)
    before = multiply(source_two, up, False) + up_bias
    hidden_low = gelu_tanh(before).astype(jnp.bfloat16)
    grad_hidden = multiply(cot_all, down, False)
    grad_before = jax.vjp(gelu_tanh, before)[1](grad_hidden)[0].astype(jnp.bfloat16)
    grad_normed_two = scatter_sum(multiply(grad_before, up, True), heads_axis, 5)
    output = middle + scatter_sum_async(multiply(hidden_low, down, True), heads_axis) + biases[3]
    grad_w_down = contract_tokens(cot_all, hidden_low)
    grad_up_bias = jnp.sum(grad_before.astype(jnp.float32), axis=0)
    grad_w_up = contract_tokens(source_two, grad_before)
    grad_out = cot.astype(jnp.float32)
    back_two, gain_two, shift_two = norm_backward(
        grad_normed_two, gains[1], normal_two, inverse_two
    )
    grad_middle = grad_out + back_two
    grad_middle_low = grad_middle.astype(jnp.bfloat16)
    grad_out_bias = jnp.sum(grad_middle_low.astype(jnp.float32), axis=0)
    grad_down_bias = jnp.sum(grad_out, axis=0)
    grad_middle_all = gather(grad_middle_low, heads_axis, 6)
    grad_att_low = multiply(grad_middle_all, out_t, False).astype(jnp.bfloat16).reshape(shape_four)
    grad_w_out_t = contract_tokens(grad_middle_all, attended_low)
    grad_q, grad_k, grad_v = attention_backward(
        queries, keys_all, values_all, grad_att_low, log_sums
    )
    grad_q = grad_q.reshape(rows_here, head_cols).astype(jnp.bfloat16)
    grad_k = grad_k.reshape(rows_here, head_cols).astype(jnp.bfloat16)
    grad_v = grad_v.reshape(rows_here, head_cols).astype(jnp.bfloat16)
    grad_qkv_low = jnp.concatenate([grad_q, grad_k, grad_v], axis=1)
    grad_qv = jnp.stack(
        [jnp.sum(grad_q.astype(jnp.float32), axis=0), jnp.sum(grad_v.astype(jnp.float32), axis=0)]
    )
    grad_normed_one = scatter_sum(multiply(grad_qkv_low, qkv_weight, True), heads_axis, 7)
    grad_w_qkv = contract_tokens(source_one, grad_qkv_low)
    back_one, gain_one, shift_one = norm_backward(
        grad_normed_one, gains[0], normal_one, inverse_one
    )
    grad_input = grad_middle + back_one

    mlp_sum = scatter_sum_async(jnp.concatenate([grad_w_up, grad_w_down], axis=1), split_axis)
    mlp_sum = flip(lax.psum(mlp_sum.astype(jnp.bfloat16), "dp")).astype(jnp.float32)
    att_sum = scatter_sum(jnp.concatenate([grad_w_qkv, grad_w_out_t], axis=1), split_axis, 8)
    att_sum = jnp.sum(
        swap(flip(att_sum.astype(jnp.bfloat16)), "dp", True, 9).astype(jnp.float32), axis=0
    )
    sum_up = mlp_sum[:, :width]
    sum_down = mlp_sum[:, width:]
    sum_qkv = att_sum[:, : 3 * head_cols].reshape(w_qkv.shape)
    sum_out = att_sum[:, 3 * head_cols :].T
    features = gains.shape[1]
    longest = max(features, width, 2 * head_cols)
    small = [gain_one, gain_two, shift_one, shift_two, grad_out_bias, grad_down_bias]
    small = small + [grad_up_bias, grad_qv.reshape(-1)]
    small = jnp.stack([jnp.pad(row, (0, longest - row.shape[0])) for row in small])
    small = jnp.sum(swap(small, "dp", True, 10), axis=0)
    small = jnp.sum(swap(small, split_axis, True, 11), axis=0)
    projected = flip(small[6:])
    sum_upb = projected[0, :width]
    sum_qv = projected[1, : 2 * head_cols].reshape(2, head_cols)
    share = norm_gains.shape[1]
    small = jnp.sum(swap(small[:6], heads_axis, True, 12), axis=0)
    small = lax.dynamic_slice_in_dim(small, lax.axis_index("row") * share, share, axis=1)
    output_t, grad_input_t = to_features(
        output.astype(jnp.bfloat16), grad_input.astype(jnp.bfloat16), 13
    )
    return (
        output_t,
        grad_input_t,
        small[:2],
        small[2:],
        sum_qkv,
        sum_qv,
        sum_out,
        sum_up,
        sum_upb,
        sum_down,
    )


MESH = pl.DeviceIdType.MESH
BIG = 63 * 1024 * 1024


def remote(target_id, source, target, send_sem, recv_sem):
    copy = pltpu.make_async_remote_copy(
        src_ref=source,
        dst_ref=target,
        send_sem=send_sem,
        recv_sem=recv_sem,
        device_id=target_id,
        device_id_type=MESH,
    )
    copy.start()
    return copy


def keep(source, target, sem):
    copy = pltpu.make_async_copy(source, target, sem)
    copy.start()
    return copy


def send(axis_name, peer, source, target, send_sem, recv_sem):
    return remote({axis_name: peer}, source, target, send_sem, recv_sem)


def place():
    core, row = lax.axis_index("dp"), lax.axis_index("row")
    home, level = lax.rem(row, 2), row // 2
    return core, 1 - core, home, level, 2 * core + home


def others(axis_name):
    count = lax.axis_size(axis_name)
    me = lax.axis_index(axis_name)
    return me, [lax.rem(me + step, count) for step in range(1, count)]


def meet(extra):
    barrier = pltpu.get_barrier_semaphore()
    pl.semaphore_signal(barrier, inc=1, device_id=extra, device_id_type=MESH)
    total = 1
    for name in ("row", "col", "dp"):
        _, peers = others(name)
        for peer in peers:
            pl.semaphore_signal(barrier, inc=1, device_id={name: peer}, device_id_type=MESH)
        total += len(peers)
    pl.semaphore_wait(barrier, total)


def rows_of(index, size):
    return pl.ds(pl.multiple_of(index * size, size), size)


def left_t(weight, acts):
    return lax.dot_general(weight, acts, (((0,), (0,)), ((), ())), preferred_element_type=jnp.float32)


def right_t(left, right):
    return lax.dot_general(left, right, (((1,), (1,)), ((), ())), preferred_element_type=jnp.float32)


def plain(left, right):
    return jnp.dot(left, right, preferred_element_type=jnp.float32)


def lane_sums(values):
    ones = jnp.ones((8, values.shape[1]), jnp.float32)
    return lax.dot_general(
        ones,
        values,
        (((1,), (1,)), ((), ())),
        precision=lax.Precision.HIGHEST,
        preferred_element_type=jnp.float32,
    )


def wait_recv_all(block, sems, count):
    for index in range(count):
        pltpu.make_async_copy(block, block, sems.at[index]).wait()


def crossings():
    core, twin, home, _, me = place()
    row = lax.axis_index("row")
    near = me + 1 - 2 * home
    side = 2 * twin + home
    return me, near, side, 3 - me, {"row": row + 1 - 2 * home}, {"dp": twin}


def gather_one(source, spot, send_sem, recv_sem):
    me, _, _, _, near_id, side_id = crossings()
    return [
        remote(near_id, source, spot(me), send_sem.at[0], recv_sem.at[0]),
        remote(side_id, source, spot(me), send_sem.at[1], recv_sem.at[1]),
    ]


def gather_two(copies, spot, send_sem, recv_sem):
    _, near, _, _, _, side_id = crossings()
    copies[0].wait_recv()
    copies.append(remote(side_id, spot(near), spot(near), send_sem.at[2], recv_sem.at[2]))


def gather_end(copies):
    copies[1].wait_recv()
    copies[2].wait_recv()


def reduce_one(part, got, send_sem, recv_sem):
    _, _, side, far, _, side_id = crossings()
    moves = ((1, far), (0, side))
    copies = [None, None]
    for slot, block in moves:
        copies[slot] = remote(side_id, part(block), got.at[slot], send_sem.at[slot], recv_sem.at[slot])
    return copies


def reduce_two(copies, part, got, middle, send_sem, recv_sem):
    _, near, _, _, near_id, _ = crossings()
    copies[1].wait_recv()
    middle[...] = (part(near)[...].astype(jnp.float32) + got[1].astype(jnp.float32)).astype(jnp.bfloat16)
    copies.append(remote(near_id, middle, got.at[2], send_sem.at[2], recv_sem.at[2]))


def reduce_end(copies, part, got):
    me = crossings()[0]
    copies[0].wait_recv()
    copies[2].wait_recv()
    total = part(me)[...].astype(jnp.float32) + got[0].astype(jnp.float32)
    return total + got[2].astype(jnp.float32)


def sent(*groups):
    for copies in groups:
        for copy in copies:
            copy.wait_send()


def block_kernel(names, seqs, *refs):
    count = len(refs) - 2 * len(names[1])
    arrays = dict(zip(names[0], refs[:count]))
    r = types.SimpleNamespace(**arrays)
    out_sems = types.SimpleNamespace(**dict(zip(names[1], refs[count::2])))
    in_sems = types.SimpleNamespace(**dict(zip(names[1], refs[count + 1 :: 2])))
    x_ref, c_ref = r.x, r.c
    x_all, c_all, ln_ref, qkv_ref, att_ref = r.x_all, r.c_all, r.ln, r.qkv, r.att
    wa_all, wu_all, wd_all = r.wa_all, r.wu_all, r.wd_all
    lse_ref, stat_ref, x1_ref, l2_ref, gx_ref = r.lse, r.stat, r.x1, r.l2, r.gx
    vcol_ref, tcol_ref = r.vcol, r.tcol
    hid, gra, y_ref, head_grad, mixed_grad, back = r.hid, r.gra, r.y, r.head_grad, r.mixed_grad, r.back
    low, full = jnp.bfloat16, jnp.float32
    share, tokens = x_ref.shape
    length = tokens // seqs
    width = x_all.shape[0]
    row, row_peers = others("row")
    col, col_peers = others("col")
    core, twin, home, level, me = place()
    near_row, over_row = row + 1 - 2 * home, lax.rem(row + 2, 4)
    swap_id = {"dp": twin, "row": over_row}
    stays = core == level
    rows, cols = len(row_peers) + 1, len(col_peers) + 1
    head_cols = r.wo.shape[0]
    heads = head_cols // HEAD
    hidden = wu_all.shape[1]
    mixed_cols = wa_all.shape[1]
    piece = length // rows
    chunk = length // 2
    half = share // 2
    slab = rows_of(me, share)
    spans = [pl.ds(seq * length, length) for seq in range(seqs)]
    owns = [pl.ds(pl.multiple_of(seq * length + me * piece, piece), piece) for seq in range(seqs)]
    owned = [slice(seq * piece, (seq + 1) * piece) for seq in range(seqs)]

    def slab_spot(ref, at):
        return lambda index: ref.at[rows_of(index, share), at]

    def half_rows(index, side):
        return pl.ds(pl.multiple_of(index * share + side * half, half), half)

    def token_spot(ref, seq):
        return lambda index: ref.at[:, pl.ds(pl.multiple_of(seq * length + index * piece, piece), piece)]

    def token_part(ref, seq):
        return lambda index: ref.at[seq * rows + index]

    class Gather:
        def __init__(self, sends, receives, seq, source, spot):
            self.sems = (sends.at[seq], receives.at[seq])
            self.spot = spot
            self.copies = gather_one(source, spot, *self.sems)

        def two(self):
            gather_two(self.copies, self.spot, *self.sems)

        def end(self):
            gather_end(self.copies)

    class Reduce:
        def __init__(self, sends, receives, got, middle, seq, part):
            self.sems = (sends.at[seq], receives.at[seq])
            self.got, self.middle = got.at[seq], middle.at[seq]
            self.part = part
            self.copies = reduce_one(part, self.got, *self.sems)

        def two(self):
            reduce_two(self.copies, self.part, self.got, self.middle, *self.sems)

        def end(self):
            return reduce_end(self.copies, self.part, self.got)

    def swap(source, target, send_sem, recv_sem):
        @pl.when(stays)
        def _():
            keep(source, target, recv_sem)

        @pl.when(jnp.logical_not(stays))
        def _():
            remote(swap_id, source, target, send_sem, recv_sem)

    def swap_sent(source, send_sem):
        @pl.when(jnp.logical_not(stays))
        def _():
            pltpu.make_async_copy(source, source, send_sem).wait()

    def landed(block, sem):
        pltpu.make_async_copy(block, block, sem).wait()

    wa_ref, vec_own, tip_own = r.wa_own, r.vec_own, r.tip_own
    wa_ref[:, :head_cols] = r.wo[...].T
    for index in range(3):
        for head in range(heads):
            first = head_cols + (3 * head + index) * HEAD
            wa_ref[:, first : first + HEAD] = r.wq[index, :, head * HEAD : (head + 1) * HEAD]
    vec_own[...] = jnp.zeros_like(vec_own)
    vec_own[0:2, :share] = r.gains[...]
    vec_own[2:6, :share] = r.biases[...]
    tip_own[...] = jnp.zeros_like(tip_own)
    tip_own[0:2, :head_cols] = r.qv_bias[...]
    lanes = tip_own.shape[1]
    for index in range(hidden // lanes):
        tip_own[2 + index : 3 + index, :] = r.up_bias[index * lanes : (index + 1) * lanes].reshape(1, lanes)
    weights = ((wa_ref, wa_all), (r.wu, wu_all), (r.wd, wd_all))
    zbuf, relay = r.zbuf, r.relay
    near_id, over_id, twin_id = {"row": near_row}, {"row": over_row}, {"dp": twin}
    weight_copies = []

    middle_lane = mixed_cols // 2
    early_strip, late_strip = slice(0, middle_lane), slice(middle_lane, mixed_cols)
    weight_parts = ((0, early_strip), (0, late_strip), (1, slice(0, hidden)), (2, slice(0, hidden)))

    def spread(part):
        index, strip = weight_parts[part]
        own, _ = weights[index]
        mine = own.at[pl.ds(pl.multiple_of(core * half, half), half), strip]
        keep(mine, zbuf.at[index, col, :, strip], in_sems.wz.at[part, col])
        for step, peer in enumerate(col_peers):
            weight_copies.append(
                send("col", peer, mine, zbuf.at[index, col, :, strip], out_sems.wz.at[part, step], in_sems.wz.at[part, col])
            )

    def weight_move(part, slot, target_id, source, target):
        weight_copies.append(
            remote(target_id, source, target, out_sems.wm.at[part, slot], in_sems.wm.at[part, slot])
        )

    def weight_one(part):
        index, strip = weight_parts[part]
        _, whole = weights[index]
        wait_recv_all(zbuf.at[0, 0, :, strip], in_sems.wz.at[part], cols)
        here = whole.at[half_rows(row, core), strip]
        away = 1 - home
        weight_move(part, 0, near_id, zbuf.at[index, away + 2 * core, :, strip], here)
        weight_move(part, 1, near_id, zbuf.at[index, away + 2 * twin, :, strip], relay.at[index, 0, :, strip])
        weight_move(part, 2, over_id, zbuf.at[index, home + 2 * core, :, strip], here)
        weight_move(part, 3, over_id, zbuf.at[index, home + 2 * twin, :, strip], relay.at[index, 1, :, strip])
        weight_move(part, 6, twin_id, zbuf.at[index, home + 2 * twin, :, strip], here)
        keep(zbuf.at[index, home + 2 * core, :, strip], here, in_sems.wl.at[part])

    def weight_two(part):
        index, strip = weight_parts[part]
        _, whole = weights[index]
        block = zbuf.at[0, 0, :, strip]
        there = whole.at[half_rows(near_row, core), strip]
        landed(block, in_sems.wm.at[part, 0])
        weight_move(part, 4, over_id, there, there)
        landed(block, in_sems.wm.at[part, 1])
        weight_move(part, 5, over_id, relay.at[index, 0, :, strip], relay.at[index, 2, :, strip])
        weight_move(part, 7, twin_id, relay.at[index, 0, :, strip], there)

    def weight_three(part):
        index, strip = weight_parts[part]
        _, whole = weights[index]
        block = zbuf.at[0, 0, :, strip]
        landed(block, in_sems.wm.at[part, 3])
        weight_move(part, 8, twin_id, relay.at[index, 1, :, strip], whole.at[half_rows(over_row, core), strip])
        landed(block, in_sems.wm.at[part, 5])
        weight_move(part, 9, twin_id, relay.at[index, 2, :, strip], whole.at[half_rows(3 - row, core), strip])

    def weight_end(part):
        index, strip = weight_parts[part]
        block = zbuf.at[0, 0, :, strip]
        landed(block, in_sems.wl.at[part])
        for slot in (2, 4, 6, 7, 8, 9):
            landed(block, in_sems.wm.at[part, slot])

    meet(swap_id)
    spread(0)
    x_own, c_own = r.x_own, r.c_own
    for seq, at in enumerate(spans):
        swap(x_ref.at[:, at], x_own.at[:, at], out_sems.xs.at[seq], in_sems.xs.at[seq])
    keep(vec_own, r.vec_all.at[row], in_sems.vec.at[row])
    keep(tip_own, r.tip_all.at[col], in_sems.tip.at[col])
    small_copies = [
        send("row", peer, vec_own, r.vec_all.at[row], out_sems.vec.at[step], in_sems.vec.at[row])
        for step, peer in enumerate(row_peers)
    ] + [
        send("col", peer, tip_own, r.tip_all.at[col], out_sems.tip.at[step], in_sems.tip.at[col])
        for step, peer in enumerate(col_peers)
    ]
    xs, cots = [], []
    for seq, at in enumerate(spans):
        landed(x_ref.at[:, at], in_sems.xs.at[seq])
        xs.append(Gather(out_sems.x, in_sems.x, seq, x_own.at[:, at], slab_spot(x_all, at)))
    swap(c_ref, c_own, out_sems.cs.at[0], in_sems.cs.at[0])
    x_all[slab, :] = x_own[...]
    wait_recv_all(vec_own, in_sems.vec, rows)
    for index in range(rows):
        flipped = r.vec_all[index].T
        vcol_ref[index * share : (index + 1) * share, :] = flipped[:share]
    wait_recv_all(tip_own, in_sems.tip, cols)
    tip = r.tip_all[me].T
    bias_q, bias_v = tip[:head_cols, 0:1], tip[:head_cols, 1:2]
    for index in range(hidden // lanes):
        tcol_ref[index * lanes : (index + 1) * lanes, :] = jnp.broadcast_to(
            tip[:, 2 + index : 3 + index], (lanes, 8)
        )
    weight_one(0)
    spread(1)
    for gather in xs:
        gather.two()

    def first_norm(step, carry):
        at = pl.ds(pl.multiple_of(step * chunk, chunk), chunk)
        values = x_all[:, at].astype(full)
        center = jnp.mean(values, axis=0, keepdims=True)
        offset = values - center
        inverse = lax.rsqrt(jnp.mean(offset * offset, axis=0, keepdims=True) + EPSILON)
        ln_ref[:, at] = (offset * inverse * vcol_ref[:, 0:1] + vcol_ref[:, 2:3]).astype(low)
        stat_ref[0:1, at] = center
        stat_ref[1:2, at] = inverse
        return carry

    def project(seq, low_head, high_head):
        def one(step, carry):
            at = pl.ds(pl.multiple_of(step * chunk, chunk), chunk)
            first = head_cols + 3 * HEAD * low_head
            mixed = left_t(wa_all[:, first : head_cols + 3 * HEAD * high_head], ln_ref[:, at])
            for head in range(low_head, high_head):
                here, there = 3 * HEAD * (head - low_head), 3 * HEAD * head
                of_head = slice(head * HEAD, (head + 1) * HEAD)
                queries = (mixed[here : here + HEAD] + bias_q[of_head]) * HEAD**-0.5
                values = mixed[here + 2 * HEAD : here + 3 * HEAD] + bias_v[of_head]
                qkv_ref[there : there + HEAD, at] = queries.astype(low)
                qkv_ref[there + HEAD : there + 2 * HEAD, at] = mixed[here + HEAD : here + 2 * HEAD].astype(low)
                qkv_ref[there + 2 * HEAD : there + 3 * HEAD, at] = values.astype(low)
            return carry

        lax.fori_loop(2 * seq, 2 * seq + 2, one, 0)

    def causal(part_q):
        keys = (part_q + 1) * chunk
        key_at = lax.broadcasted_iota(jnp.int32, (keys, chunk), 0)
        return key_at <= lax.broadcasted_iota(jnp.int32, (keys, chunk), 1) + part_q * chunk

    def attend(seq, head):
        top = 3 * HEAD * head
        for part_q in range(2):
            here = pl.ds(seq * length + part_q * chunk, chunk)
            span = pl.ds(seq * length, (part_q + 1) * chunk)
            scores = left_t(qkv_ref[top + HEAD : top + 2 * HEAD, span], qkv_ref[top : top + HEAD, here])
            scores = jnp.where(causal(part_q), scores, -1e30)
            summit = jnp.max(scores, axis=0, keepdims=True)
            expos = jnp.exp(scores - summit)
            total = jnp.sum(expos, axis=0, keepdims=True)
            mixed = plain(qkv_ref[top + 2 * HEAD : top + 3 * HEAD, span], expos.astype(low))
            att_ref[head * HEAD : (head + 1) * HEAD, here] = (mixed / total).astype(low)
            lse_ref[seq * heads + head, :, pl.ds(part_q * chunk, chunk)] = jnp.broadcast_to(
                summit + jnp.log(total), (8, chunk)
            )

    xs[0].end()
    lax.fori_loop(0, 2, first_norm, 0)
    weight_two(0)
    xs[1].end()
    lax.fori_loop(2, 4, first_norm, 0)
    weight_one(1)
    spread(2)
    weight_three(0)
    landed(c_ref, in_sems.cs.at[0])
    for seq, at in enumerate(spans):
        cots.append(Gather(out_sems.c, in_sems.c, seq, c_own.at[:, at], slab_spot(c_all, at)))
    c_all[slab, :] = c_own[...]
    weight_end(0)
    early = (mixed_cols // 2 - head_cols) // (3 * HEAD)
    outs = []

    def out_side(seq):
        mixed = plain(wa_all[:, :head_cols], att_ref[:, seq * length : (seq + 1) * length])
        for index in range(rows):
            r.o_part[seq * rows + index] = mixed[:, index * piece : (index + 1) * piece].astype(low)
        outs.append(Reduce(out_sems.o, in_sems.o, r.o_got, r.o_middle, seq, token_part(r.o_part, seq)))

    project(0, 0, early)
    weight_two(1)
    for head in range(early):
        attend(0, head)
    project(1, 0, early)
    for head in range(early):
        attend(1, head)
    weight_three(1)
    weight_end(1)
    project(0, early, heads)
    attend(0, early)
    weight_one(2)
    spread(3)
    for head in range(early + 1, heads):
        attend(0, head)
    out_side(0)
    for gather in cots:
        gather.two()
    project(1, early, heads)
    outs[0].two()
    attend(1, early)
    weight_two(2)
    for head in range(early + 1, heads):
        attend(1, head)
    out_side(1)
    l2s = []

    def second_norm(seq):
        middle = x_all[:, owns[seq]].astype(full) + outs[seq].end() + vcol_ref[:, 4:5]
        x1_ref[:, owned[seq]] = middle
        center = jnp.mean(middle, axis=0, keepdims=True)
        offset = middle - center
        inverse = lax.rsqrt(jnp.mean(offset * offset, axis=0, keepdims=True) + EPSILON)
        l2_ref[:, owns[seq]] = (offset * inverse * vcol_ref[:, 1:2] + vcol_ref[:, 3:4]).astype(low)
        spot = token_spot(l2_ref, seq)
        l2s.append(Gather(out_sems.l, in_sems.l, seq, spot(me), spot))

    second_norm(0)
    outs[1].two()
    weight_one(3)
    weight_three(2)
    weight_end(2)
    wu_t, wd_t, g_part = r.wu_t, r.wd_t, r.g_part
    wu_t[...] = wu_all[...].T
    l2s[0].two()
    weight_two(3)
    second_norm(1)

    pieces = chunk // piece

    def forward(step, carry):
        at = pl.ds(pl.multiple_of(step * chunk, chunk), chunk)
        before = plain(wu_t[...], l2_ref[:, at]) + tcol_ref[:, 0:1]
        square = before * before
        tanh = jnp.tanh(GELU_COEF * (before + 0.044715 * before * square))
        hid[:, at] = (0.5 * before * (1.0 + tanh)).astype(low)
        r.slope[:, at] = 0.5 * (1.0 + tanh) + 0.5 * before * (1.0 - tanh * tanh) * (
            GELU_COEF * (1.0 + 3.0 * 0.044715 * square)
        )
        return carry

    def returning(step, carry):
        at = pl.ds(pl.multiple_of(step * chunk, chunk), chunk)
        grad = (plain(wd_t[...], c_all[:, at]) * r.slope[:, at]).astype(low)
        gra[:, at] = grad
        backs = plain(wu_all[...], grad)
        for index in range(pieces):
            g_part[step * pieces + index] = backs[:, index * piece : (index + 1) * piece].astype(low)
        return carry

    def finish(step, carry):
        at = pl.ds(pl.multiple_of(step * chunk, chunk), chunk)
        y_ref[:, at] = plain(wd_all[...], hid[:, at]).astype(low)
        return carry

    block = width // 4

    def up_weight(step, carry):
        place = pl.ds(pl.multiple_of(step * block, block), block)
        r.du[place, :] = right_t(l2_ref[place, :], gra[...]).astype(low)
        return carry

    def down_weight(step, carry):
        place = pl.ds(pl.multiple_of(step * block, block), block)
        r.dd[place, :] = right_t(c_all[place, :], hid[...]).astype(low)
        return carry

    grads = (r.du, r.dd, r.da)
    finals = (r.gu, r.gd, r.ga)
    pair, over, aside, plane, line = r.pair, r.over, r.aside, r.plane, r.line
    grad_copies = []
    parts = ((0, slice(0, hidden)), (1, slice(0, hidden)), (2, early_strip), (2, late_strip))
    grad_blocks = [pair.at[0, 0, :, strip] for _, strip in parts]

    def cutter(part):
        index, strip = parts[part]
        return lambda ref, slot: ref.at[index, slot, :, strip]

    def pair_start(part):
        index, strip = parts[part]
        cut = cutter(part)
        for block_row in range(rows):
            grad_copies.append(
                remote(
                    twin_id,
                    grads[index].at[half_rows(block_row, twin), strip],
                    cut(pair, block_row),
                    out_sems.pair.at[part, block_row],
                    in_sems.pair.at[part, block_row],
                )
            )

    def pair_finish(part):
        index, strip = parts[part]
        cut = cutter(part)
        wait_recv_all(grad_blocks[part], in_sems.pair.at[part], rows)
        for slot, block_row in enumerate((over_row, 3 - row)):
            moves = ((0, grads[index].at[half_rows(block_row, core), strip]), (1, cut(pair, block_row)))
            for which, source in moves:
                place_at = 2 * slot + which
                grad_copies.append(
                    remote(
                        over_id,
                        source,
                        cut(over, place_at),
                        out_sems.over.at[part, place_at],
                        in_sems.over.at[part, place_at],
                    )
                )

    def over_finish(part):
        index, strip = parts[part]
        cut = cutter(part)
        for slot, block_row in ((1, near_row), (0, row)):
            for which, owner in ((0, core), (1, twin)):
                landed(grad_blocks[part], in_sems.over.at[part, 2 * slot + which])
                if which == 0:
                    mine = grads[index][half_rows(block_row, core), strip].astype(full)
                else:
                    mine = cut(pair, block_row)[...].astype(full)
                total = (mine + cut(over, 2 * slot + which)[...].astype(full)).astype(low)
                if slot == 0:
                    cut(plane, home + 2 * owner)[...] = total
                else:
                    cut(aside, which)[...] = total
                    grad_copies.append(
                        remote(
                            near_id,
                            cut(aside, which),
                            cut(plane, home + 2 * owner),
                            out_sems.aside.at[part, which],
                            in_sems.aside.at[part, which],
                        )
                    )

    def line_start(part):
        index, strip = parts[part]
        cut = cutter(part)
        wait_recv_all(grad_blocks[part], in_sems.aside.at[part], 2)
        keep(cut(plane, col), cut(line, col), in_sems.line.at[part, col])
        for step, peer in enumerate(col_peers):
            grad_copies.append(
                send(
                    "col",
                    peer,
                    cut(plane, peer),
                    cut(line, col),
                    out_sems.line.at[part, step],
                    in_sems.line.at[part, col],
                )
            )

    def line_finish(part):
        index, strip = parts[part]
        cut = cutter(part)
        wait_recv_all(grad_blocks[part], in_sems.line.at[part], cols)
        total = cut(line, 0)[...].astype(full)
        for other in range(1, cols):
            total = total + cut(line, other)[...].astype(full)
        at = pl.ds(pl.multiple_of(core * half, half), half)
        finals[index][at, strip] = total
        grad_copies.append(
            remote(
                twin_id,
                finals[index].at[at, strip],
                finals[index].at[at, strip],
                out_sems.final.at[part],
                in_sems.final.at[part],
            )
        )

    gls = []
    l2s[0].end()
    lax.fori_loop(0, 2, forward, 0)
    l2s[1].two()
    weight_three(3)
    l2s[1].end()
    lax.fori_loop(2, 4, forward, 0)
    weight_end(3)
    wd_t[...] = wd_all[...].T
    for seq in range(seqs):
        cots[seq].end()
        lax.fori_loop(2 * seq, 2 * seq + 1, returning, 0)
        if seq == 1:
            gls[0].two()
        lax.fori_loop(2 * seq + 1, 2 * seq + 2, returning, 0)
        gls.append(Reduce(out_sems.g, in_sems.g, r.g_got, r.g_middle, seq, token_part(g_part, seq)))
    lax.fori_loop(0, 4, up_weight, 0)
    pair_start(0)
    gls[1].two()
    lax.fori_loop(0, 4, down_weight, 0)
    pair_start(1)
    pair_finish(0)
    gxs = []
    sums = [0.0] * 4
    for seq in range(seqs):
        grad = gls[seq].end()
        middle = x1_ref[:, owned[seq]]
        center = jnp.mean(middle, axis=0, keepdims=True)
        offset = middle - center
        inverse = lax.rsqrt(jnp.mean(offset * offset, axis=0, keepdims=True) + EPSILON)
        normal = offset * inverse
        scaled = grad * vcol_ref[:, 1:2]
        first = jnp.mean(scaled, axis=0, keepdims=True)
        second = jnp.mean(scaled * normal, axis=0, keepdims=True)
        outer = c_all[:, owns[seq]].astype(full)
        result = (outer + inverse * (scaled - first - normal * second)).astype(low)
        gx_ref[:, owns[seq]] = result
        spot = token_spot(gx_ref, seq)
        gxs.append(Gather(out_sems.gx, in_sems.gx, seq, spot(me), spot))
        terms = (grad * normal, grad, result.astype(full), outer)
        sums = [old + new for old, new in zip(sums, terms)]
    pack_own = r.pack_own
    pack_own[...] = jnp.zeros_like(pack_own)
    for index in range(4):
        pack_own[index : index + 1, :] = lane_sums(sums[index])[0:1]
    pair_finish(1)
    gxs[0].two()
    gxs[1].two()
    lax.fori_loop(0, 2 * seqs, finish, 0)
    for seq in range(seqs):
        y_own = plain(wd_all[...], hid[:, owns[seq]]) + x1_ref[:, owned[seq]] + vcol_ref[:, 5:6]
        y_ref[:, owns[seq]] = y_own.astype(low)

    def head_side(step, carry):
        at = pl.ds(pl.multiple_of(step * chunk, chunk), chunk)
        mixed_grad[:, at] = left_t(wa_all[:, :head_cols], gx_ref[:, at]).astype(low)
        return carry

    def attend_back(seq, head):
        top = 3 * HEAD * head
        key_rows, value_rows = slice(top + HEAD, top + 2 * HEAD), slice(top + 2 * HEAD, top + 3 * HEAD)
        of_head = slice(head * HEAD, (head + 1) * HEAD)
        kept = []
        for part_q in range(2):
            here = pl.ds(seq * length + part_q * chunk, chunk)
            span = pl.ds(seq * length, (part_q + 1) * chunk)
            queries = qkv_ref[top : top + HEAD, here]
            key = qkv_ref[key_rows, span]
            outer = mixed_grad[of_head, here]
            shift = lse_ref[seq * heads + head, 0:1, pl.ds(part_q * chunk, chunk)]
            probs = jnp.exp(jnp.where(causal(part_q), left_t(key, queries) - shift, -1e30))
            delta = jnp.sum(outer.astype(full) * att_ref[of_head, here].astype(full), axis=0, keepdims=True)
            slope = (probs * (left_t(qkv_ref[value_rows, span], outer) - delta)).astype(low)
            head_grad[top : top + HEAD, here] = (plain(key, slope) * HEAD**-0.5).astype(low)
            kept.append((right_t(queries, slope), right_t(outer, probs.astype(low))))
        first_half, second_half = pl.ds(seq * length, chunk), pl.ds(seq * length + chunk, chunk)
        for rows_at, index in ((key_rows, 0), (value_rows, 1)):
            second = kept[1][index]
            head_grad[rows_at, first_half] = (second[:, :chunk] + kept[0][index]).astype(low)
            head_grad[rows_at, second_half] = second[:, chunk:].astype(low)

    def backward(step, carry):
        at = pl.ds(pl.multiple_of(step * chunk, chunk), chunk)
        back[:, at] = plain(wa_all[:, head_cols:], head_grad[:, at]).astype(low)
        return carry

    early_rows = 3 * HEAD * early

    def mixed_early(step, carry):
        at = pl.ds(pl.multiple_of(step * block, block), block)
        r.da[at, :head_cols] = right_t(gx_ref[at, :], att_ref[...]).astype(low)
        r.da[at, head_cols : head_cols + early_rows] = right_t(ln_ref[at, :], head_grad[:early_rows]).astype(low)
        return carry

    def mixed_late(step, carry):
        at = pl.ds(pl.multiple_of(step * block, block), block)
        r.da[at, head_cols + early_rows :] = right_t(ln_ref[at, :], head_grad[early_rows:]).astype(low)
        return carry

    ones = []

    def norm_side(seq):
        lax.fori_loop(2 * seq, 2 * seq + 2, backward, 0)
        ones.append(Reduce(out_sems.n, in_sems.n, r.n_got, r.n_middle, seq, slab_spot(back, spans[seq])))

    gxs[0].end()
    lax.fori_loop(0, 2, head_side, 0)
    for head in range(early):
        attend_back(0, head)
    over_finish(0)
    attend_back(0, early)
    gxs[1].end()
    lax.fori_loop(2, 4, head_side, 0)
    for head in range(early):
        attend_back(1, head)
    lax.fori_loop(0, 4, mixed_early, 0)
    pair_start(2)
    for head in range(early + 1, heads):
        attend_back(0, head)
    norm_side(0)
    pair_finish(2)
    line_start(0)
    attend_back(1, early)
    ones[0].two()
    over_finish(1)
    for head in range(early + 1, heads):
        attend_back(1, head)
    norm_side(1)
    lax.fori_loop(0, 4, mixed_late, 0)
    pair_start(3)
    ones[1].two()
    over_finish(2)
    pair_finish(3)
    line_start(1)

    count = jnp.ones((8, tokens), low)
    pack_own[6:7, :hidden] = right_t(count, gra[...])[0:1]
    pack_own[7:8, : 3 * head_cols] = right_t(count, head_grad[...])[0:1]
    stat_own, stat_side, stat_near, stat_sum = r.stat_own, r.stat_side, r.stat_near, r.stat_sum
    gain = vcol_ref[slab, 0:1]
    stat_own[...] = jnp.zeros_like(stat_own)
    scale_sum, shift_sum = 0.0, 0.0
    saved = []
    for seq, at in enumerate(spans):
        grad = ones[seq].end()
        normal = (x_own[:, at].astype(full) - stat_ref[0:1, at]) * stat_ref[1:2, at]
        scaled = grad * gain
        stat_own[0:1, at] = jnp.sum(scaled, axis=0, keepdims=True)
        stat_own[1:2, at] = jnp.sum(scaled * normal, axis=0, keepdims=True)
        saved.append((scaled, normal))
        scale_sum = scale_sum + grad * normal
        shift_sum = shift_sum + grad
    stat_copies = [remote(twin_id, stat_own, stat_side, out_sems.stat.at[0], in_sems.stat.at[0])]
    pack_own[4:5, :share] = lane_sums(scale_sum)[0:1]
    pack_own[5:6, :share] = lane_sums(shift_sum)[0:1]
    stat_copies[0].wait_recv()
    stat_sum[...] = stat_own[...] + stat_side[...]
    stat_copies.append(remote(near_id, stat_sum, stat_near, out_sems.stat.at[1], in_sems.stat.at[1]))
    pack_all, mid_own, mid_pair, blocks = r.pack_all, r.mid_own, r.mid_pair, r.blocks
    keep(pack_own, pack_all.at[row], in_sems.pack.at[row])
    small_copies += [
        send("row", peer, pack_own, pack_all.at[row], out_sems.pack.at[step], in_sems.pack.at[row])
        for step, peer in enumerate(row_peers)
    ]
    line_start(2)
    ys = Reduce(out_sems.y, in_sems.y, r.y_got, r.y_middle, 0, slab_spot(y_ref, pl.ds(0, tokens)))
    stat_copies[1].wait_recv()
    total = (stat_sum[...] + stat_near[...]) * (1.0 / width)
    for seq, at in enumerate(spans):
        scaled, normal = saved[seq]
        here = slice(seq * length, (seq + 1) * length)
        result = stat_ref[1:2, at] * (scaled - total[0:1, here] - normal * total[1:2, here])
        r.gin_own[:, at] = (gx_ref[slab, at].astype(full) + result).astype(low)
    for seq, at in enumerate(spans):
        swap_sent(x_ref.at[:, at], out_sems.xs.at[seq])
    swap(r.gin_own, r.gin, out_sems.gs.at[0], in_sems.gs.at[0])
    wait_recv_all(pack_own, in_sems.pack, rows)
    total = pack_all[0, 0:4]
    for index in range(1, rows):
        total = total + pack_all[index, 0:4]
    mid_own[0, 4:8] = total
    for index in range(2):
        mid_own[index, 0:4] = pack_all[index, 4:8] + pack_all[2 + index, 4:8]
    mid_own[1, 4:8] = total
    small_copies.append(remote(twin_id, mid_own, mid_pair, out_sems.mid.at[0], in_sems.mid.at[0]))
    ys.two()
    landed(mid_own, in_sems.mid.at[0])
    total = mid_own[0, 4:8] + mid_pair[0, 4:8]
    for index in range(2):
        blocks[2 * core + index, 0:4] = mid_own[index, 0:4]
        blocks[2 * twin + index, 0:4] = mid_pair[index, 0:4]
    for index in range(rows):
        blocks[index, 4:8] = total
    a_all, b_all = r.a_all, r.b_all
    keep(blocks.at[row], a_all.at[col], in_sems.t.at[0, col])
    keep(blocks.at[col], b_all.at[col], in_sems.t.at[1, col])
    for step, peer in enumerate(col_peers):
        small_copies += [
            send("col", peer, blocks.at[row], a_all.at[col], out_sems.t.at[0, step], in_sems.t.at[0, col]),
            send("col", peer, blocks.at[peer], b_all.at[col], out_sems.t.at[1, step], in_sems.t.at[1, col]),
        ]
    over_finish(3)
    line_finish(0)
    line_finish(1)
    line_start(3)
    wait_recv_all(pack_own, in_sems.t.at[0], cols)
    wait_recv_all(pack_own, in_sems.t.at[1], cols)
    a_total, b_total = a_all[0], b_all[0]
    for index in range(1, cols):
        a_total, b_total = a_total + a_all[index], b_total + b_all[index]
    wide = jnp.zeros((4, share), full)
    for index in range(rows):
        wide = wide + jnp.where(row == index, a_total[4:8, index * share : (index + 1) * share], 0.0)
    r.g_gains[0:1, :] = a_total[0:1, :share]
    r.g_gains[1:2, :] = wide[0:1]
    r.g_biases[0:1, :] = a_total[1:2, :share]
    r.g_biases[1:4, :] = wide[1:4]
    r.g_up_bias[...] = b_total[2, :hidden]
    for head in range(heads):
        top, of_head = 3 * HEAD * head, slice(head * HEAD, (head + 1) * HEAD)
        r.g_qv[0:1, of_head] = b_total[3:4, top : top + HEAD]
        r.g_qv[1:2, of_head] = b_total[3:4, top + 2 * HEAD : top + 3 * HEAD]
    r.out_own[...] = ys.end().astype(low)
    swap_sent(c_ref, out_sems.cs.at[0])
    swap(r.out_own, r.out, out_sems.gs.at[1], in_sems.gs.at[1])
    line_finish(2)
    line_finish(3)
    for part, (index, strip) in enumerate(parts):
        landed(finals[index].at[pl.ds(0, half), strip], in_sems.final.at[part])
    for index in range(3):
        for head in range(heads):
            first = head_cols + (3 * head + index) * HEAD
            r.g_wq[index, :, head * HEAD : (head + 1) * HEAD] = r.ga[:, first : first + HEAD]
    r.g_wo[...] = r.ga[:, :head_cols].T
    landed(r.gin, in_sems.gs.at[0])
    landed(r.out, in_sems.gs.at[1])
    swap_sent(r.gin, out_sems.gs.at[0])
    swap_sent(r.out, out_sems.gs.at[1])
    sent(small_copies, stat_copies, weight_copies, grad_copies)
    sent(*[move.copies for move in xs + cots + outs + l2s + gls + gxs + ones + [ys]])


def settle_kernel(count, *refs):
    for index in range(count):
        refs[count + index][...] = refs[index][...]


def settle(arrays):
    count = len(arrays)
    return pl.pallas_call(
        functools.partial(settle_kernel, count),
        out_shape=[jax.ShapeDtypeStruct(array.shape, array.dtype) for array in arrays],
        in_specs=[pl.BlockSpec(memory_space=pltpu.VMEM)] * count,
        out_specs=[pl.BlockSpec(memory_space=pltpu.VMEM)] * count,
    )(*arrays)


def square_body(
    block_input, norm_gains, row_biases, w_qkv, qv_bias, w_out, w_up, up_bias, w_down, cotangent
):
    low, full = jnp.bfloat16, jnp.float32
    share, tokens = block_input.shape
    rows, cols = lax.axis_size("row"), lax.axis_size("col")
    width = share * rows
    head_cols = w_out.shape[0]
    mixed = 3 * head_cols + share
    hidden = w_up.shape[1]
    seqs = tokens // LENGTH
    heads = head_cols // HEAD
    piece = LENGTH // rows
    half = share // 2
    lanes = -(-share // 128) * 128
    tips = -(-(2 + hidden // lanes) // 8) * 8
    inputs = dict(
        x=block_input,
        c=cotangent,
        gains=norm_gains,
        biases=row_biases,
        qv_bias=qv_bias,
        up_bias=up_bias,
        wq=w_qkv.transpose(1, 0, 2),
        wo=w_out,
        wu=w_up,
        wd=w_down,
    )
    outputs = dict(
        out=((share, tokens), low),
        gin=((share, tokens), low),
        g_gains=((2, share), full),
        g_biases=((4, share), full),
        g_wq=((3, share, head_cols), full),
        g_qv=((2, head_cols), full),
        g_wo=((head_cols, share), full),
        gu=((share, hidden), full),
        g_up_bias=((hidden,), full),
        gd=((share, hidden), full),
    )
    token_got, token_middle = (seqs, 3, width, piece), (seqs, width, piece)
    buffers = dict(
        x_all=((width, tokens), low),
        c_all=((width, tokens), low),
        wa_all=((width, mixed), low),
        wu_all=((width, hidden), low),
        wd_all=((width, hidden), low),
        ln=((width, tokens), low),
        qkv=((3 * head_cols, tokens), low),
        att=((head_cols, tokens), low),
        lse=((seqs * heads, 8, LENGTH), full),
        stat=((8, tokens), full),
        x1=((width, seqs * piece), full),
        l2=((width, tokens), low),
        gx=((width, tokens), low),
        vcol=((width, 8), full),
        tcol=((hidden, 8), full),
        wa_own=((share, mixed), low),
        vec_own=((8, lanes), full),
        tip_own=((tips, lanes), full),
        vec_all=((rows, 8, lanes), full),
        tip_all=((cols, tips, lanes), full),
        zbuf=((3, cols, half, mixed), low),
        relay=((3, 3, half, mixed), low),
        x_own=((share, tokens), low),
        c_own=((share, tokens), low),
        gin_own=((share, tokens), low),
        out_own=((share, tokens), low),
        o_part=((seqs * rows, width, piece), low),
        o_got=(token_got, low),
        o_middle=(token_middle, low),
        wu_t=((hidden, width), low),
        wd_t=((hidden, width), low),
        hid=((hidden, tokens), low),
        gra=((hidden, tokens), low),
        slope=((hidden, tokens), full),
        g_part=((seqs * rows, width, piece), low),
        g_got=(token_got, low),
        g_middle=(token_middle, low),
        y=((width, tokens), low),
        y_got=((1, 3, share, tokens), low),
        y_middle=((1, share, tokens), low),
        du=((width, hidden), low),
        dd=((width, hidden), low),
        da=((width, mixed), low),
        pack_own=((8, width), full),
        mixed_grad=((head_cols, tokens), low),
        head_grad=((3 * head_cols, tokens), low),
        back=((width, tokens), low),
        n_got=((seqs, 3, share, LENGTH), low),
        n_middle=((seqs, share, LENGTH), low),
        ga=((share, mixed), full),
        stat_own=((8, tokens), full),
        stat_side=((8, tokens), full),
        stat_near=((8, tokens), full),
        stat_sum=((8, tokens), full),
        pair=((3, rows, half, mixed), low),
        over=((3, 4, half, mixed), low),
        aside=((3, 2, half, mixed), low),
        plane=((3, cols, half, mixed), low),
        line=((3, cols, half, mixed), low),
        pack_all=((rows, 8, width), full),
        mid_own=((2, 8, width), full),
        mid_pair=((2, 8, width), full),
        blocks=((rows, 8, width), full),
        a_all=((cols, 8, width), full),
        b_all=((cols, 8, width), full),
    )
    arrivals = dict(
        x=((seqs, 3), (seqs, 3)),
        c=((seqs, 3), (seqs, 3)),
        l=((seqs, 3), (seqs, 3)),
        gx=((seqs, 3), (seqs, 3)),
        o=((seqs, 3), (seqs, 3)),
        g=((seqs, 3), (seqs, 3)),
        n=((seqs, 3), (seqs, 3)),
        y=((1, 3), (1, 3)),
        xs=((seqs,), (seqs,)),
        cs=((1,), (1,)),
        gs=((2,), (2,)),
        vec=((rows - 1,), (rows,)),
        tip=((cols - 1,), (cols,)),
        wz=((4, cols - 1), (4, cols)),
        wm=((4, 10), (4, 10)),
        wl=((4,), (4,)),
        pair=((4, rows), (4, rows)),
        over=((4, 4), (4, 4)),
        aside=((4, 2), (4, 2)),
        line=((4, cols - 1), (4, cols)),
        final=((4,), (4,)),
        stat=((2,), (2,)),
        pack=((rows - 1,), (rows,)),
        mid=((1,), (1,)),
        t=((2, cols - 1), (2, cols)),
    )
    names = (list(inputs) + list(outputs) + list(buffers), list(arrivals))
    scratch = [pltpu.VMEM(*shape) for shape in buffers.values()]
    for sends, receives in arrivals.values():
        scratch += [pltpu.SemaphoreType.DMA(sends), pltpu.SemaphoreType.DMA(receives)]
    results = pl.pallas_call(
        functools.partial(block_kernel, names, seqs),
        out_shape=[jax.ShapeDtypeStruct(*shape) for shape in outputs.values()],
        in_specs=[pl.BlockSpec(memory_space=pltpu.VMEM)] * len(inputs),
        out_specs=[pl.BlockSpec(memory_space=pltpu.VMEM)] * len(outputs),
        scratch_shapes=scratch,
        compiler_params=pltpu.CompilerParams(
            collective_id=0, has_side_effects=True, vmem_limit_bytes=BIG
        ),
    )(*inputs.values())
    out, gin, gains, biases, g_wq, g_qv, g_wo, gu, g_up_bias, gd = settle(results)
    return (out, gin, gains, biases, g_wq.transpose(1, 0, 2), g_qv, g_wo, gu, g_up_bias, gd)


def fits(mesh):
    sizes = mesh.shape
    return sizes["row"] == 4 and sizes["col"] == 4 and sizes["dp"] == 2


def solution(mesh):
    in_specs = (
        P("row", ("dp", "col")),
        P(None, "row"),
        P(None, "row"),
        P("row", None, "col"),
        P(None, "col"),
        P("col", "row"),
        P("row", "col"),
        P("col"),
        P("row", "col"),
        P("row", ("dp", "col")),
    )
    out_specs = (
        P("row", ("dp", "col")),
        P("row", ("dp", "col")),
        P(None, "row"),
        P(None, "row"),
        P("row", None, "col"),
        P(None, "col"),
        P("col", "row"),
        P("row", "col"),
        P("col"),
        P("row", "col"),
    )
    chosen = square_body if fits(mesh) else body
    return jax.shard_map(chosen, mesh=mesh, in_specs=in_specs, out_specs=out_specs, check_vma=False)
```

```python
import functools
import types

import jax
import jax.numpy as jnp
from jax import lax
from jax.experimental import pallas as pl
from jax.experimental.pallas import tpu as pltpu
from jax.sharding import PartitionSpec as P

D = 768
HEAD = 64
LENGTH = 512


EPSILON = 1e-05
GELU_COEF = 0.7978845608028654


def gelu_tanh(values):
    return (
        0.5 * values * (1.0 + jnp.tanh(GELU_COEF * (values + 0.044715 * values * values * values)))
    )


def multiply(rows, weight, flipped):
    if flipped:
        return lax.dot_general(
            rows, weight, (((1,), (1,)), ((), ())), preferred_element_type=jnp.float32
        )
    return jnp.dot(rows, weight, preferred_element_type=jnp.float32)


def contract_tokens(left, right):
    return lax.dot_general(
        left, right, (((0,), (0,)), ((), ())), preferred_element_type=jnp.float32
    )


def swap_kernel(axis_name, count, shared, x_ref, o_ref, send_sem, recv_sem, own_sem):
    me = lax.axis_index(axis_name)
    barrier = pltpu.get_barrier_semaphore()
    peers = [lax.rem(me + step, count) for step in range(1, count)]
    for peer in peers:
        pl.semaphore_signal(
            barrier, inc=1, device_id={axis_name: peer}, device_id_type=pl.DeviceIdType.MESH
        )
    own = pltpu.make_async_copy(x_ref if shared else x_ref.at[me], o_ref.at[me], own_sem)
    own.start()
    pl.semaphore_wait(barrier, count - 1)
    copies = []
    for slot, peer in enumerate(peers):
        copy = pltpu.make_async_remote_copy(
            src_ref=x_ref if shared else x_ref.at[peer],
            dst_ref=o_ref.at[me],
            send_sem=send_sem.at[slot],
            recv_sem=recv_sem.at[slot],
            device_id={axis_name: peer},
            device_id_type=pl.DeviceIdType.MESH,
        )
        copy.start()
        copies.append(copy)
    own.wait()
    for copy in copies:
        copy.wait()


def swap(values, axis_name, shared, ident):
    count = lax.axis_size(axis_name)
    block = values.shape if shared else values.shape[1:]
    moved = values.size * values.dtype.itemsize
    return pl.pallas_call(
        functools.partial(swap_kernel, axis_name, count, shared),
        out_shape=jax.ShapeDtypeStruct((count, *block), values.dtype),
        in_specs=[pl.BlockSpec(memory_space=pltpu.VMEM)],
        out_specs=pl.BlockSpec(memory_space=pltpu.VMEM),
        scratch_shapes=[
            pltpu.SemaphoreType.DMA((count - 1,)),
            pltpu.SemaphoreType.DMA((count - 1,)),
            pltpu.SemaphoreType.DMA,
        ],
        compiler_params=pltpu.CompilerParams(collective_id=ident, has_side_effects=True),
        cost_estimate=pl.CostEstimate(
            flops=0, bytes_accessed=(20 if not shared else 60) * moved, transcendentals=0
        ),
    )(values)


def gather_async(local, axis_name):
    return lax.all_gather(local, axis_name, axis=0, tiled=True)


def scatter_sum_async(partial, axis_name):
    return lax.psum_scatter(
        partial.astype(jnp.bfloat16), axis_name, scatter_dimension=0, tiled=True
    ).astype(jnp.float32)


def gather(local, axis_name, ident):
    return swap(local, axis_name, True, ident).reshape(-1, *local.shape[1:])


def scatter_sum(partial, axis_name, ident):
    count = lax.axis_size(axis_name)
    pieces = partial.astype(jnp.bfloat16).reshape(count, -1, *partial.shape[1:])
    return jnp.sum(swap(pieces, axis_name, False, ident).astype(jnp.float32), axis=0)


def to_tokens(first, second, ident):
    rows, cols = lax.axis_size("row"), lax.axis_size("col")
    share = first.shape[0]
    block = jnp.concatenate([first.T, second.T], axis=1).reshape(rows, -1, 2 * share)
    block = swap(block, "row", False, ident)
    if rows != cols:
        moves = [(r * cols + c, c * rows + r) for r in range(rows) for c in range(cols)]
        block = lax.ppermute(block, ("row", "col"), moves)
    first = jnp.concatenate([block[r, :, :share] for r in range(rows)], axis=1)
    second = jnp.concatenate([block[r, :, share:] for r in range(rows)], axis=1)
    return first, second


def to_features(first, second, ident):
    rows, cols = lax.axis_size("row"), lax.axis_size("col")
    share = first.shape[1] // rows
    block = jnp.stack(
        [
            jnp.concatenate(
                [first[:, r * share : (r + 1) * share], second[:, r * share : (r + 1) * share]], axis=1
            )
            for r in range(rows)
        ]
    )
    if rows != cols:
        moves = [(c * rows + r, r * cols + c) for r in range(rows) for c in range(cols)]
        block = lax.ppermute(block, ("row", "col"), moves)
    block = swap(block, "row", False, ident).reshape(-1, 2 * share)
    return block[:, :share].T, block[:, share:].T


def flip(block):
    rows, cols = lax.axis_size("row"), lax.axis_size("col")
    if rows != cols:
        return block
    moves = [(r * cols + c, c * rows + r) for r in range(rows) for c in range(cols)]
    return lax.ppermute(block, ("row", "col"), moves)


def norm_forward(values, gain, bias):
    center = jnp.mean(values, axis=1, keepdims=True)
    offset = values - center
    inverse = lax.rsqrt(jnp.mean(offset * offset, axis=1, keepdims=True) + EPSILON)
    normal = offset * inverse
    return (normal * gain + bias, normal, inverse)


def norm_backward(grad, gain, normal, inverse):
    scaled = grad * gain
    first = jnp.mean(scaled, axis=1, keepdims=True)
    second = jnp.mean(scaled * normal, axis=1, keepdims=True)
    result = inverse * (scaled - first - normal * second)
    return (result, jnp.sum(grad * normal, axis=0), jnp.sum(grad, axis=0))


def causal_mask(length):
    positions = jnp.arange(length)
    return positions[None, :] <= positions[:, None]


def attention_forward(queries, keys, values):
    factor = HEAD ** (-0.5)

    def one_sequence(pieces):
        seq_q, seq_k, seq_v = pieces
        scores = (
            jnp.einsum("qhd,khd->hqk", seq_q, seq_k, preferred_element_type=jnp.float32) * factor
        )
        scores = jnp.where(causal_mask(seq_q.shape[0])[None], scores, -1e30)
        summit = jnp.max(scores, axis=-1, keepdims=True)
        expos = jnp.exp(scores - summit)
        total = jnp.sum(expos, axis=-1, keepdims=True)
        probs = (expos / total).astype(jnp.bfloat16)
        output = jnp.einsum("hqk,khd->qhd", probs, seq_v, preferred_element_type=jnp.float32)
        return (output, summit[..., 0] + jnp.log(total[..., 0]))

    return lax.map(one_sequence, (queries, keys, values))


def attention_backward(queries, keys, values, grad_out, log_sums):
    factor = HEAD ** (-0.5)

    def one_sequence(pieces):
        seq_q, seq_k, seq_v, seq_g, seq_l = pieces
        scores = (
            jnp.einsum("qhd,khd->hqk", seq_q, seq_k, preferred_element_type=jnp.float32) * factor
        )
        scores = jnp.where(causal_mask(seq_q.shape[0])[None], scores, -1e30)
        probs = jnp.exp(scores - seq_l[..., None])
        grad_v = jnp.einsum(
            "hqk,qhd->khd", probs.astype(jnp.bfloat16), seq_g, preferred_element_type=jnp.float32
        )
        grad_p = jnp.einsum("qhd,khd->hqk", seq_g, seq_v, preferred_element_type=jnp.float32)
        inner = jnp.sum(grad_p * probs, axis=-1, keepdims=True)
        grad_s = (probs * (grad_p - inner)).astype(jnp.bfloat16)
        grad_q = (
            jnp.einsum("hqk,khd->qhd", grad_s, seq_k, preferred_element_type=jnp.float32) * factor
        )
        grad_k = (
            jnp.einsum("hqk,qhd->khd", grad_s, seq_q, preferred_element_type=jnp.float32) * factor
        )
        return (grad_q, grad_k, grad_v)

    return lax.map(one_sequence, (queries, keys, values, grad_out, log_sums))


def body(
    block_input, norm_gains, row_biases, w_qkv, qv_bias, w_out, w_up, up_bias, w_down, cotangent
):
    head_cols = w_qkv.shape[2]
    square = lax.axis_size("row") == lax.axis_size("col")
    heads_axis, split_axis = ("row", "col") if square else ("col", "row")
    qv_bias, up_bias = flip(qv_bias), flip(up_bias)
    inputs, cot = to_tokens(block_input, cotangent, 0)
    inputs = inputs.astype(jnp.float32)
    vectors = swap(jnp.concatenate([norm_gains, row_biases], axis=0), "row", True, 1)
    vectors = jnp.concatenate([vectors[r] for r in range(vectors.shape[0])], axis=1)
    gains, biases = vectors[:2], vectors[2:]
    qkv_weight = gather_async(flip(w_qkv.reshape(w_qkv.shape[0], -1)), split_axis)
    rest = gather_async(flip(jnp.concatenate([w_out.T, w_up, w_down], axis=1)), split_axis)
    width = w_up.shape[1]
    out_t = rest[:, :head_cols]
    up = rest[:, head_cols : head_cols + width]
    down = rest[:, head_cols + width :]

    normed_one, normal_one, inverse_one = norm_forward(inputs, gains[0], biases[0])
    source_one = gather(normed_one.astype(jnp.bfloat16), heads_axis, 2)
    qkv_sum = multiply(source_one, qkv_weight, False)
    rows_here = qkv_sum.shape[0]
    qkv_sum = qkv_sum.reshape(rows_here, 3, head_cols)
    shape_four = (rows_here // LENGTH, LENGTH, head_cols // HEAD, HEAD)
    queries = (qkv_sum[:, 0] + qv_bias[0]).astype(jnp.bfloat16).reshape(shape_four)
    keys_all = qkv_sum[:, 1].astype(jnp.bfloat16).reshape(shape_four)
    values_all = (qkv_sum[:, 2] + qv_bias[1]).astype(jnp.bfloat16).reshape(shape_four)
    attended, log_sums = attention_forward(queries, keys_all, values_all)
    attended_low = attended.reshape(rows_here, head_cols).astype(jnp.bfloat16)
    middle = inputs + scatter_sum(multiply(attended_low, out_t, True), heads_axis, 3) + biases[2]
    normed_two, normal_two, inverse_two = norm_forward(middle, gains[1], biases[1])
    source_two = gather(normed_two.astype(jnp.bfloat16), heads_axis, 4)
    cot_all = gather_async(cot, heads_axis)
    before = multiply(source_two, up, False) + up_bias
    hidden_low = gelu_tanh(before).astype(jnp.bfloat16)
    grad_hidden = multiply(cot_all, down, False)
    grad_before = jax.vjp(gelu_tanh, before)[1](grad_hidden)[0].astype(jnp.bfloat16)
    grad_normed_two = scatter_sum(multiply(grad_before, up, True), heads_axis, 5)
    output = middle + scatter_sum_async(multiply(hidden_low, down, True), heads_axis) + biases[3]
    grad_w_down = contract_tokens(cot_all, hidden_low)
    grad_up_bias = jnp.sum(grad_before.astype(jnp.float32), axis=0)
    grad_w_up = contract_tokens(source_two, grad_before)
    grad_out = cot.astype(jnp.float32)
    back_two, gain_two, shift_two = norm_backward(
        grad_normed_two, gains[1], normal_two, inverse_two
    )
    grad_middle = grad_out + back_two
    grad_middle_low = grad_middle.astype(jnp.bfloat16)
    grad_out_bias = jnp.sum(grad_middle_low.astype(jnp.float32), axis=0)
    grad_down_bias = jnp.sum(grad_out, axis=0)
    grad_middle_all = gather(grad_middle_low, heads_axis, 6)
    grad_att_low = multiply(grad_middle_all, out_t, False).astype(jnp.bfloat16).reshape(shape_four)
    grad_w_out_t = contract_tokens(grad_middle_all, attended_low)
    grad_q, grad_k, grad_v = attention_backward(
        queries, keys_all, values_all, grad_att_low, log_sums
    )
    grad_q = grad_q.reshape(rows_here, head_cols).astype(jnp.bfloat16)
    grad_k = grad_k.reshape(rows_here, head_cols).astype(jnp.bfloat16)
    grad_v = grad_v.reshape(rows_here, head_cols).astype(jnp.bfloat16)
    grad_qkv_low = jnp.concatenate([grad_q, grad_k, grad_v], axis=1)
    grad_qv = jnp.stack(
        [jnp.sum(grad_q.astype(jnp.float32), axis=0), jnp.sum(grad_v.astype(jnp.float32), axis=0)]
    )
    grad_normed_one = scatter_sum(multiply(grad_qkv_low, qkv_weight, True), heads_axis, 7)
    grad_w_qkv = contract_tokens(source_one, grad_qkv_low)
    back_one, gain_one, shift_one = norm_backward(
        grad_normed_one, gains[0], normal_one, inverse_one
    )
    grad_input = grad_middle + back_one

    mlp_sum = scatter_sum_async(jnp.concatenate([grad_w_up, grad_w_down], axis=1), split_axis)
    mlp_sum = flip(lax.psum(mlp_sum.astype(jnp.bfloat16), "dp")).astype(jnp.float32)
    att_sum = scatter_sum(jnp.concatenate([grad_w_qkv, grad_w_out_t], axis=1), split_axis, 8)
    att_sum = jnp.sum(
        swap(flip(att_sum.astype(jnp.bfloat16)), "dp", True, 9).astype(jnp.float32), axis=0
    )
    sum_up = mlp_sum[:, :width]
    sum_down = mlp_sum[:, width:]
    sum_qkv = att_sum[:, : 3 * head_cols].reshape(w_qkv.shape)
    sum_out = att_sum[:, 3 * head_cols :].T
    features = gains.shape[1]
    longest = max(features, width, 2 * head_cols)
    small = [gain_one, gain_two, shift_one, shift_two, grad_out_bias, grad_down_bias]
    small = small + [grad_up_bias, grad_qv.reshape(-1)]
    small = jnp.stack([jnp.pad(row, (0, longest - row.shape[0])) for row in small])
    small = jnp.sum(swap(small, "dp", True, 10), axis=0)
    small = jnp.sum(swap(small, split_axis, True, 11), axis=0)
    projected = flip(small[6:])
    sum_upb = projected[0, :width]
    sum_qv = projected[1, : 2 * head_cols].reshape(2, head_cols)
    share = norm_gains.shape[1]
    small = jnp.sum(swap(small[:6], heads_axis, True, 12), axis=0)
    small = lax.dynamic_slice_in_dim(small, lax.axis_index("row") * share, share, axis=1)
    output_t, grad_input_t = to_features(
        output.astype(jnp.bfloat16), grad_input.astype(jnp.bfloat16), 13
    )
    return (
        output_t,
        grad_input_t,
        small[:2],
        small[2:],
        sum_qkv,
        sum_qv,
        sum_out,
        sum_up,
        sum_upb,
        sum_down,
    )


MESH = pl.DeviceIdType.MESH
BIG = 63 * 1024 * 1024


def remote(target_id, source, target, send_sem, recv_sem):
    copy = pltpu.make_async_remote_copy(
        src_ref=source,
        dst_ref=target,
        send_sem=send_sem,
        recv_sem=recv_sem,
        device_id=target_id,
        device_id_type=MESH,
    )
    copy.start()
    return copy


def keep(source, target, sem):
    copy = pltpu.make_async_copy(source, target, sem)
    copy.start()
    return copy


def send(axis_name, peer, source, target, send_sem, recv_sem):
    return remote({axis_name: peer}, source, target, send_sem, recv_sem)


def place():
    core, row = lax.axis_index("dp"), lax.axis_index("row")
    home, level = lax.rem(row, 2), row // 2
    return core, 1 - core, home, level, 2 * core + home


def others(axis_name):
    count = lax.axis_size(axis_name)
    me = lax.axis_index(axis_name)
    return me, [lax.rem(me + step, count) for step in range(1, count)]


def meet(extra):
    barrier = pltpu.get_barrier_semaphore()
    pl.semaphore_signal(barrier, inc=1, device_id=extra, device_id_type=MESH)
    total = 1
    for name in ("row", "col", "dp"):
        _, peers = others(name)
        for peer in peers:
            pl.semaphore_signal(barrier, inc=1, device_id={name: peer}, device_id_type=MESH)
        total += len(peers)
    pl.semaphore_wait(barrier, total)


def rows_of(index, size):
    return pl.ds(pl.multiple_of(index * size, size), size)


def left_t(weight, acts):
    return lax.dot_general(weight, acts, (((0,), (0,)), ((), ())), preferred_element_type=jnp.float32)


def right_t(left, right):
    return lax.dot_general(left, right, (((1,), (1,)), ((), ())), preferred_element_type=jnp.float32)


def plain(left, right):
    return jnp.dot(left, right, preferred_element_type=jnp.float32)


def lane_sums(values):
    ones = jnp.ones((8, values.shape[1]), jnp.float32)
    return lax.dot_general(
        ones,
        values,
        (((1,), (1,)), ((), ())),
        precision=lax.Precision.HIGHEST,
        preferred_element_type=jnp.float32,
    )


def wait_recv_all(block, sems, count):
    for index in range(count):
        pltpu.make_async_copy(block, block, sems.at[index]).wait()


def crossings():
    core, twin, home, _, me = place()
    row = lax.axis_index("row")
    near = me + 1 - 2 * home
    side = 2 * twin + home
    return me, near, side, 3 - me, {"row": row + 1 - 2 * home}, {"dp": twin}


def gather_one(source, spot, send_sem, recv_sem):
    me, _, _, _, near_id, side_id = crossings()
    return [
        remote(near_id, source, spot(me), send_sem.at[0], recv_sem.at[0]),
        remote(side_id, source, spot(me), send_sem.at[1], recv_sem.at[1]),
    ]


def gather_two(copies, spot, send_sem, recv_sem):
    _, near, _, _, _, side_id = crossings()
    copies[0].wait_recv()
    copies.append(remote(side_id, spot(near), spot(near), send_sem.at[2], recv_sem.at[2]))


def gather_end(copies):
    copies[1].wait_recv()
    copies[2].wait_recv()


def reduce_one(part, got, send_sem, recv_sem):
    _, _, side, far, _, side_id = crossings()
    moves = ((1, far), (0, side))
    copies = [None, None]
    for slot, block in moves:
        copies[slot] = remote(side_id, part(block), got.at[slot], send_sem.at[slot], recv_sem.at[slot])
    return copies


def reduce_two(copies, part, got, middle, send_sem, recv_sem):
    _, near, _, _, near_id, _ = crossings()
    copies[1].wait_recv()
    middle[...] = (part(near)[...].astype(jnp.float32) + got[1].astype(jnp.float32)).astype(jnp.bfloat16)
    copies.append(remote(near_id, middle, got.at[2], send_sem.at[2], recv_sem.at[2]))


def reduce_end(copies, part, got):
    me = crossings()[0]
    copies[0].wait_recv()
    copies[2].wait_recv()
    total = part(me)[...].astype(jnp.float32) + got[0].astype(jnp.float32)
    return total + got[2].astype(jnp.float32)


def sent(*groups):
    for copies in groups:
        for copy in copies:
            copy.wait_send()


def block_kernel(names, seqs, *refs):
    count = len(refs) - 2 * len(names[1])
    arrays = dict(zip(names[0], refs[:count]))
    r = types.SimpleNamespace(**arrays)
    out_sems = types.SimpleNamespace(**dict(zip(names[1], refs[count::2])))
    in_sems = types.SimpleNamespace(**dict(zip(names[1], refs[count + 1 :: 2])))
    x_ref, c_ref = r.x, r.c
    x_all, c_all, ln_ref, qkv_ref, att_ref = r.x_all, r.c_all, r.ln, r.qkv, r.att
    wa_all, wu_all, wd_all = r.wa_all, r.wu_all, r.wd_all
    lse_ref, stat_ref, x1_ref, l2_ref, gx_ref = r.lse, r.stat, r.x1, r.l2, r.gx
    vcol_ref, tcol_ref = r.vcol, r.tcol
    hid, gra, y_ref, head_grad, mixed_grad, back = r.hid, r.gra, r.y, r.head_grad, r.mixed_grad, r.back
    low, full = jnp.bfloat16, jnp.float32
    share, tokens = x_ref.shape
    length = tokens // seqs
    width = x_all.shape[0]
    row, row_peers = others("row")
    col, col_peers = others("col")
    core, twin, home, level, me = place()
    near_row, over_row = row + 1 - 2 * home, lax.rem(row + 2, 4)
    swap_id = {"dp": twin, "row": over_row}
    stays = core == level
    rows, cols = len(row_peers) + 1, len(col_peers) + 1
    head_cols = r.wo.shape[0]
    heads = head_cols // HEAD
    hidden = wu_all.shape[1]
    mixed_cols = wa_all.shape[1]
    piece = length // rows
    chunk = length // 2
    half = share // 2
    slab = rows_of(me, share)
    spans = [pl.ds(seq * length, length) for seq in range(seqs)]
    owns = [pl.ds(pl.multiple_of(seq * length + me * piece, piece), piece) for seq in range(seqs)]
    owned = [slice(seq * piece, (seq + 1) * piece) for seq in range(seqs)]

    def slab_spot(ref, at):
        return lambda index: ref.at[rows_of(index, share), at]

    def half_rows(index, side):
        return pl.ds(pl.multiple_of(index * share + side * half, half), half)

    def token_spot(ref, seq):
        return lambda index: ref.at[:, pl.ds(pl.multiple_of(seq * length + index * piece, piece), piece)]

    def token_part(ref, seq):
        return lambda index: ref.at[seq * rows + index]

    class Gather:
        def __init__(self, sends, receives, seq, source, spot):
            self.sems = (sends.at[seq], receives.at[seq])
            self.spot = spot
            self.copies = gather_one(source, spot, *self.sems)

        def two(self):
            gather_two(self.copies, self.spot, *self.sems)

        def end(self):
            gather_end(self.copies)

    class Reduce:
        def __init__(self, sends, receives, got, middle, seq, part):
            self.sems = (sends.at[seq], receives.at[seq])
            self.got, self.middle = got.at[seq], middle.at[seq]
            self.part = part
            self.copies = reduce_one(part, self.got, *self.sems)

        def two(self):
            reduce_two(self.copies, self.part, self.got, self.middle, *self.sems)

        def end(self):
            return reduce_end(self.copies, self.part, self.got)

    def swap(source, target, send_sem, recv_sem):
        @pl.when(stays)
        def _():
            keep(source, target, recv_sem)

        @pl.when(jnp.logical_not(stays))
        def _():
            remote(swap_id, source, target, send_sem, recv_sem)

    def swap_sent(source, send_sem):
        @pl.when(jnp.logical_not(stays))
        def _():
            pltpu.make_async_copy(source, source, send_sem).wait()

    def landed(block, sem):
        pltpu.make_async_copy(block, block, sem).wait()

    wa_ref, vec_own, tip_own = r.wa_own, r.vec_own, r.tip_own
    wa_ref[:, :head_cols] = r.wo[...].T
    for index in range(3):
        for head in range(heads):
            first = head_cols + (3 * head + index) * HEAD
            wa_ref[:, first : first + HEAD] = r.wq[index, :, head * HEAD : (head + 1) * HEAD]
    vec_own[...] = jnp.zeros_like(vec_own)
    vec_own[0:2, :share] = r.gains[...]
    vec_own[2:6, :share] = r.biases[...]
    tip_own[...] = jnp.zeros_like(tip_own)
    tip_own[0:2, :head_cols] = r.qv_bias[...]
    lanes = tip_own.shape[1]
    for index in range(hidden // lanes):
        tip_own[2 + index : 3 + index, :] = r.up_bias[index * lanes : (index + 1) * lanes].reshape(1, lanes)
    weights = ((wa_ref, wa_all), (r.wu, wu_all), (r.wd, wd_all))
    zbuf, relay = r.zbuf, r.relay
    near_id, over_id, twin_id = {"row": near_row}, {"row": over_row}, {"dp": twin}
    weight_copies = []

    middle_lane = mixed_cols // 2
    early_strip, late_strip = slice(0, middle_lane), slice(middle_lane, mixed_cols)
    weight_parts = ((0, early_strip), (0, late_strip), (1, slice(0, hidden)), (2, slice(0, hidden)))

    def spread(part):
        index, strip = weight_parts[part]
        own, _ = weights[index]
        mine = own.at[pl.ds(pl.multiple_of(core * half, half), half), strip]
        keep(mine, zbuf.at[index, col, :, strip], in_sems.wz.at[part, col])
        for step, peer in enumerate(col_peers):
            weight_copies.append(
                send("col", peer, mine, zbuf.at[index, col, :, strip], out_sems.wz.at[part, step], in_sems.wz.at[part, col])
            )

    def weight_move(part, slot, target_id, source, target):
        weight_copies.append(
            remote(target_id, source, target, out_sems.wm.at[part, slot], in_sems.wm.at[part, slot])
        )

    def weight_one(part):
        index, strip = weight_parts[part]
        _, whole = weights[index]
        wait_recv_all(zbuf.at[0, 0, :, strip], in_sems.wz.at[part], cols)
        here = whole.at[half_rows(row, core), strip]
        away = 1 - home
        weight_move(part, 0, near_id, zbuf.at[index, away + 2 * core, :, strip], here)
        weight_move(part, 1, near_id, zbuf.at[index, away + 2 * twin, :, strip], relay.at[index, 0, :, strip])
        weight_move(part, 2, over_id, zbuf.at[index, home + 2 * core, :, strip], here)
        weight_move(part, 3, over_id, zbuf.at[index, home + 2 * twin, :, strip], relay.at[index, 1, :, strip])
        weight_move(part, 6, twin_id, zbuf.at[index, home + 2 * twin, :, strip], here)
        keep(zbuf.at[index, home + 2 * core, :, strip], here, in_sems.wl.at[part])

    def weight_two(part):
        index, strip = weight_parts[part]
        _, whole = weights[index]
        block = zbuf.at[0, 0, :, strip]
        there = whole.at[half_rows(near_row, core), strip]
        landed(block, in_sems.wm.at[part, 0])
        weight_move(part, 4, over_id, there, there)
        landed(block, in_sems.wm.at[part, 1])
        weight_move(part, 5, over_id, relay.at[index, 0, :, strip], relay.at[index, 2, :, strip])
        weight_move(part, 7, twin_id, relay.at[index, 0, :, strip], there)

    def weight_three(part):
        index, strip = weight_parts[part]
        _, whole = weights[index]
        block = zbuf.at[0, 0, :, strip]
        landed(block, in_sems.wm.at[part, 3])
        weight_move(part, 8, twin_id, relay.at[index, 1, :, strip], whole.at[half_rows(over_row, core), strip])
        landed(block, in_sems.wm.at[part, 5])
        weight_move(part, 9, twin_id, relay.at[index, 2, :, strip], whole.at[half_rows(3 - row, core), strip])

    def weight_end(part):
        index, strip = weight_parts[part]
        block = zbuf.at[0, 0, :, strip]
        landed(block, in_sems.wl.at[part])
        for slot in (2, 4, 6, 7, 8, 9):
            landed(block, in_sems.wm.at[part, slot])

    meet(swap_id)
    spread(0)
    x_own, c_own = r.x_own, r.c_own
    for seq, at in enumerate(spans):
        swap(x_ref.at[:, at], x_own.at[:, at], out_sems.xs.at[seq], in_sems.xs.at[seq])
    keep(vec_own, r.vec_all.at[row], in_sems.vec.at[row])
    keep(tip_own, r.tip_all.at[col], in_sems.tip.at[col])
    small_copies = [
        send("row", peer, vec_own, r.vec_all.at[row], out_sems.vec.at[step], in_sems.vec.at[row])
        for step, peer in enumerate(row_peers)
    ] + [
        send("col", peer, tip_own, r.tip_all.at[col], out_sems.tip.at[step], in_sems.tip.at[col])
        for step, peer in enumerate(col_peers)
    ]
    xs, cots = [], []
    for seq, at in enumerate(spans):
        landed(x_ref.at[:, at], in_sems.xs.at[seq])
        xs.append(Gather(out_sems.x, in_sems.x, seq, x_own.at[:, at], slab_spot(x_all, at)))
    swap(c_ref, c_own, out_sems.cs.at[0], in_sems.cs.at[0])
    x_all[slab, :] = x_own[...]
    wait_recv_all(vec_own, in_sems.vec, rows)
    for index in range(rows):
        flipped = r.vec_all[index].T
        vcol_ref[index * share : (index + 1) * share, :] = flipped[:share]
    wait_recv_all(tip_own, in_sems.tip, cols)
    tip = r.tip_all[me].T
    bias_q, bias_v = tip[:head_cols, 0:1], tip[:head_cols, 1:2]
    for index in range(hidden // lanes):
        tcol_ref[index * lanes : (index + 1) * lanes, :] = jnp.broadcast_to(
            tip[:, 2 + index : 3 + index], (lanes, 8)
        )
    weight_one(0)
    spread(1)
    for gather in xs:
        gather.two()

    def first_norm(step, carry):
        at = pl.ds(pl.multiple_of(step * chunk, chunk), chunk)
        values = x_all[:, at].astype(full)
        center = jnp.mean(values, axis=0, keepdims=True)
        offset = values - center
        inverse = lax.rsqrt(jnp.mean(offset * offset, axis=0, keepdims=True) + EPSILON)
        ln_ref[:, at] = (offset * inverse * vcol_ref[:, 0:1] + vcol_ref[:, 2:3]).astype(low)
        stat_ref[0:1, at] = center
        stat_ref[1:2, at] = inverse
        return carry

    def project(seq, low_head, high_head):
        def one(step, carry):
            at = pl.ds(pl.multiple_of(step * chunk, chunk), chunk)
            first = head_cols + 3 * HEAD * low_head
            mixed = left_t(wa_all[:, first : head_cols + 3 * HEAD * high_head], ln_ref[:, at])
            for head in range(low_head, high_head):
                here, there = 3 * HEAD * (head - low_head), 3 * HEAD * head
                of_head = slice(head * HEAD, (head + 1) * HEAD)
                queries = (mixed[here : here + HEAD] + bias_q[of_head]) * HEAD**-0.5
                values = mixed[here + 2 * HEAD : here + 3 * HEAD] + bias_v[of_head]
                qkv_ref[there : there + HEAD, at] = queries.astype(low)
                qkv_ref[there + HEAD : there + 2 * HEAD, at] = mixed[here + HEAD : here + 2 * HEAD].astype(low)
                qkv_ref[there + 2 * HEAD : there + 3 * HEAD, at] = values.astype(low)
            return carry

        lax.fori_loop(2 * seq, 2 * seq + 2, one, 0)

    def causal(part_q):
        keys = (part_q + 1) * chunk
        key_at = lax.broadcasted_iota(jnp.int32, (keys, chunk), 0)
        return key_at <= lax.broadcasted_iota(jnp.int32, (keys, chunk), 1) + part_q * chunk

    def attend(seq, head):
        top = 3 * HEAD * head
        for part_q in range(2):
            here = pl.ds(seq * length + part_q * chunk, chunk)
            span = pl.ds(seq * length, (part_q + 1) * chunk)
            scores = left_t(qkv_ref[top + HEAD : top + 2 * HEAD, span], qkv_ref[top : top + HEAD, here])
            scores = jnp.where(causal(part_q), scores, -1e30)
            summit = jnp.max(scores, axis=0, keepdims=True)
            expos = jnp.exp(scores - summit)
            total = jnp.sum(expos, axis=0, keepdims=True)
            mixed = plain(qkv_ref[top + 2 * HEAD : top + 3 * HEAD, span], expos.astype(low))
            att_ref[head * HEAD : (head + 1) * HEAD, here] = (mixed / total).astype(low)
            lse_ref[seq * heads + head, :, pl.ds(part_q * chunk, chunk)] = jnp.broadcast_to(
                summit + jnp.log(total), (8, chunk)
            )

    xs[0].end()
    lax.fori_loop(0, 2, first_norm, 0)
    weight_two(0)
    xs[1].end()
    lax.fori_loop(2, 4, first_norm, 0)
    weight_one(1)
    spread(2)
    weight_three(0)
    landed(c_ref, in_sems.cs.at[0])
    for seq, at in enumerate(spans):
        cots.append(Gather(out_sems.c, in_sems.c, seq, c_own.at[:, at], slab_spot(c_all, at)))
    c_all[slab, :] = c_own[...]
    weight_end(0)
    early = (mixed_cols // 2 - head_cols) // (3 * HEAD)
    outs = []

    def out_side(seq):
        mixed = plain(wa_all[:, :head_cols], att_ref[:, seq * length : (seq + 1) * length])
        for index in range(rows):
            r.o_part[seq * rows + index] = mixed[:, index * piece : (index + 1) * piece].astype(low)
        outs.append(Reduce(out_sems.o, in_sems.o, r.o_got, r.o_middle, seq, token_part(r.o_part, seq)))

    project(0, 0, early)
    weight_two(1)
    for head in range(early):
        attend(0, head)
    project(1, 0, early)
    for head in range(early):
        attend(1, head)
    weight_three(1)
    weight_end(1)
    project(0, early, heads)
    attend(0, early)
    weight_one(2)
    spread(3)
    for head in range(early + 1, heads):
        attend(0, head)
    out_side(0)
    for gather in cots:
        gather.two()
    project(1, early, heads)
    outs[0].two()
    attend(1, early)
    weight_two(2)
    for head in range(early + 1, heads):
        attend(1, head)
    out_side(1)
    l2s = []

    def second_norm(seq):
        middle = x_all[:, owns[seq]].astype(full) + outs[seq].end() + vcol_ref[:, 4:5]
        x1_ref[:, owned[seq]] = middle
        center = jnp.mean(middle, axis=0, keepdims=True)
        offset = middle - center
        inverse = lax.rsqrt(jnp.mean(offset * offset, axis=0, keepdims=True) + EPSILON)
        l2_ref[:, owns[seq]] = (offset * inverse * vcol_ref[:, 1:2] + vcol_ref[:, 3:4]).astype(low)
        spot = token_spot(l2_ref, seq)
        l2s.append(Gather(out_sems.l, in_sems.l, seq, spot(me), spot))

    second_norm(0)
    outs[1].two()
    weight_one(3)
    weight_three(2)
    weight_end(2)
    wu_t, wd_t, g_part = r.wu_t, r.wd_t, r.g_part
    wu_t[...] = wu_all[...].T
    l2s[0].two()
    weight_two(3)
    second_norm(1)

    pieces = chunk // piece

    def forward(step, carry):
        at = pl.ds(pl.multiple_of(step * chunk, chunk), chunk)
        before = plain(wu_t[...], l2_ref[:, at]) + tcol_ref[:, 0:1]
        square = before * before
        tanh = jnp.tanh(GELU_COEF * (before + 0.044715 * before * square))
        hid[:, at] = (0.5 * before * (1.0 + tanh)).astype(low)
        r.slope[:, at] = 0.5 * (1.0 + tanh) + 0.5 * before * (1.0 - tanh * tanh) * (
            GELU_COEF * (1.0 + 3.0 * 0.044715 * square)
        )
        return carry

    def returning(step, carry):
        at = pl.ds(pl.multiple_of(step * chunk, chunk), chunk)
        grad = (plain(wd_t[...], c_all[:, at]) * r.slope[:, at]).astype(low)
        gra[:, at] = grad
        backs = plain(wu_all[...], grad)
        for index in range(pieces):
            g_part[step * pieces + index] = backs[:, index * piece : (index + 1) * piece].astype(low)
        return carry

    def finish(step, carry):
        at = pl.ds(pl.multiple_of(step * chunk, chunk), chunk)
        y_ref[:, at] = plain(wd_all[...], hid[:, at]).astype(low)
        return carry

    block = width // 4

    def up_weight(step, carry):
        place = pl.ds(pl.multiple_of(step * block, block), block)
        r.du[place, :] = right_t(l2_ref[place, :], gra[...]).astype(low)
        return carry

    def down_weight(step, carry):
        place = pl.ds(pl.multiple_of(step * block, block), block)
        r.dd[place, :] = right_t(c_all[place, :], hid[...]).astype(low)
        return carry

    grads = (r.du, r.dd, r.da)
    finals = (r.gu, r.gd, r.ga)
    pair, over, aside, plane, line = r.pair, r.over, r.aside, r.plane, r.line
    grad_copies = []
    parts = ((0, slice(0, hidden)), (1, slice(0, hidden)), (2, early_strip), (2, late_strip))
    grad_blocks = [pair.at[0, 0, :, strip] for _, strip in parts]

    def cutter(part):
        index, strip = parts[part]
        return lambda ref, slot: ref.at[index, slot, :, strip]

    def pair_start(part):
        index, strip = parts[part]
        cut = cutter(part)
        for block_row in range(rows):
            grad_copies.append(
                remote(
                    twin_id,
                    grads[index].at[half_rows(block_row, twin), strip],
                    cut(pair, block_row),
                    out_sems.pair.at[part, block_row],
                    in_sems.pair.at[part, block_row],
                )
            )

    def pair_finish(part):
        index, strip = parts[part]
        cut = cutter(part)
        wait_recv_all(grad_blocks[part], in_sems.pair.at[part], rows)
        for slot, block_row in enumerate((over_row, 3 - row)):
            moves = ((0, grads[index].at[half_rows(block_row, core), strip]), (1, cut(pair, block_row)))
            for which, source in moves:
                place_at = 2 * slot + which
                grad_copies.append(
                    remote(
                        over_id,
                        source,
                        cut(over, place_at),
                        out_sems.over.at[part, place_at],
                        in_sems.over.at[part, place_at],
                    )
                )

    def over_finish(part):
        index, strip = parts[part]
        cut = cutter(part)
        for slot, block_row in ((1, near_row), (0, row)):
            for which, owner in ((0, core), (1, twin)):
                landed(grad_blocks[part], in_sems.over.at[part, 2 * slot + which])
                if which == 0:
                    mine = grads[index][half_rows(block_row, core), strip].astype(full)
                else:
                    mine = cut(pair, block_row)[...].astype(full)
                total = (mine + cut(over, 2 * slot + which)[...].astype(full)).astype(low)
                if slot == 0:
                    cut(plane, home + 2 * owner)[...] = total
                else:
                    cut(aside, which)[...] = total
                    grad_copies.append(
                        remote(
                            near_id,
                            cut(aside, which),
                            cut(plane, home + 2 * owner),
                            out_sems.aside.at[part, which],
                            in_sems.aside.at[part, which],
                        )
                    )

    def line_start(part):
        index, strip = parts[part]
        cut = cutter(part)
        wait_recv_all(grad_blocks[part], in_sems.aside.at[part], 2)
        keep(cut(plane, col), cut(line, col), in_sems.line.at[part, col])
        for step, peer in enumerate(col_peers):
            grad_copies.append(
                send(
                    "col",
                    peer,
                    cut(plane, peer),
                    cut(line, col),
                    out_sems.line.at[part, step],
                    in_sems.line.at[part, col],
                )
            )

    def line_finish(part):
        index, strip = parts[part]
        cut = cutter(part)
        wait_recv_all(grad_blocks[part], in_sems.line.at[part], cols)
        total = cut(line, 0)[...].astype(full)
        for other in range(1, cols):
            total = total + cut(line, other)[...].astype(full)
        at = pl.ds(pl.multiple_of(core * half, half), half)
        finals[index][at, strip] = total
        grad_copies.append(
            remote(
                twin_id,
                finals[index].at[at, strip],
                finals[index].at[at, strip],
                out_sems.final.at[part],
                in_sems.final.at[part],
            )
        )

    gls = []
    l2s[0].end()
    lax.fori_loop(0, 2, forward, 0)
    l2s[1].two()
    weight_three(3)
    l2s[1].end()
    lax.fori_loop(2, 4, forward, 0)
    weight_end(3)
    wd_t[...] = wd_all[...].T
    for seq in range(seqs):
        cots[seq].end()
        lax.fori_loop(2 * seq, 2 * seq + 1, returning, 0)
        if seq == 1:
            gls[0].two()
        lax.fori_loop(2 * seq + 1, 2 * seq + 2, returning, 0)
        gls.append(Reduce(out_sems.g, in_sems.g, r.g_got, r.g_middle, seq, token_part(g_part, seq)))
    lax.fori_loop(0, 4, up_weight, 0)
    pair_start(0)
    gls[1].two()
    lax.fori_loop(0, 4, down_weight, 0)
    pair_start(1)
    pair_finish(0)
    gxs = []
    sums = [0.0] * 4
    for seq in range(seqs):
        grad = gls[seq].end()
        middle = x1_ref[:, owned[seq]]
        center = jnp.mean(middle, axis=0, keepdims=True)
        offset = middle - center
        inverse = lax.rsqrt(jnp.mean(offset * offset, axis=0, keepdims=True) + EPSILON)
        normal = offset * inverse
        scaled = grad * vcol_ref[:, 1:2]
        first = jnp.mean(scaled, axis=0, keepdims=True)
        second = jnp.mean(scaled * normal, axis=0, keepdims=True)
        outer = c_all[:, owns[seq]].astype(full)
        result = (outer + inverse * (scaled - first - normal * second)).astype(low)
        gx_ref[:, owns[seq]] = result
        spot = token_spot(gx_ref, seq)
        gxs.append(Gather(out_sems.gx, in_sems.gx, seq, spot(me), spot))
        terms = (grad * normal, grad, result.astype(full), outer)
        sums = [old + new for old, new in zip(sums, terms)]
    pack_own = r.pack_own
    pack_own[...] = jnp.zeros_like(pack_own)
    for index in range(4):
        pack_own[index : index + 1, :] = lane_sums(sums[index])[0:1]
    pair_finish(1)
    gxs[0].two()
    gxs[1].two()
    lax.fori_loop(0, 2 * seqs, finish, 0)
    for seq in range(seqs):
        y_own = plain(wd_all[...], hid[:, owns[seq]]) + x1_ref[:, owned[seq]] + vcol_ref[:, 5:6]
        y_ref[:, owns[seq]] = y_own.astype(low)

    def head_side(step, carry):
        at = pl.ds(pl.multiple_of(step * chunk, chunk), chunk)
        mixed_grad[:, at] = left_t(wa_all[:, :head_cols], gx_ref[:, at]).astype(low)
        return carry

    def attend_back(seq, head):
        top = 3 * HEAD * head
        key_rows, value_rows = slice(top + HEAD, top + 2 * HEAD), slice(top + 2 * HEAD, top + 3 * HEAD)
        of_head = slice(head * HEAD, (head + 1) * HEAD)
        kept = []
        for part_q in range(2):
            here = pl.ds(seq * length + part_q * chunk, chunk)
            span = pl.ds(seq * length, (part_q + 1) * chunk)
            queries = qkv_ref[top : top + HEAD, here]
            key = qkv_ref[key_rows, span]
            outer = mixed_grad[of_head, here]
            shift = lse_ref[seq * heads + head, 0:1, pl.ds(part_q * chunk, chunk)]
            probs = jnp.exp(jnp.where(causal(part_q), left_t(key, queries) - shift, -1e30))
            delta = jnp.sum(outer.astype(full) * att_ref[of_head, here].astype(full), axis=0, keepdims=True)
            slope = (probs * (left_t(qkv_ref[value_rows, span], outer) - delta)).astype(low)
            head_grad[top : top + HEAD, here] = (plain(key, slope) * HEAD**-0.5).astype(low)
            kept.append((right_t(queries, slope), right_t(outer, probs.astype(low))))
        first_half, second_half = pl.ds(seq * length, chunk), pl.ds(seq * length + chunk, chunk)
        for rows_at, index in ((key_rows, 0), (value_rows, 1)):
            second = kept[1][index]
            head_grad[rows_at, first_half] = (second[:, :chunk] + kept[0][index]).astype(low)
            head_grad[rows_at, second_half] = second[:, chunk:].astype(low)

    def backward(step, carry):
        at = pl.ds(pl.multiple_of(step * chunk, chunk), chunk)
        back[:, at] = plain(wa_all[:, head_cols:], head_grad[:, at]).astype(low)
        return carry

    early_rows = 3 * HEAD * early

    def mixed_early(step, carry):
        at = pl.ds(pl.multiple_of(step * block, block), block)
        r.da[at, :head_cols] = right_t(gx_ref[at, :], att_ref[...]).astype(low)
        r.da[at, head_cols : head_cols + early_rows] = right_t(ln_ref[at, :], head_grad[:early_rows]).astype(low)
        return carry

    def mixed_late(step, carry):
        at = pl.ds(pl.multiple_of(step * block, block), block)
        r.da[at, head_cols + early_rows :] = right_t(ln_ref[at, :], head_grad[early_rows:]).astype(low)
        return carry

    ones = []

    def norm_side(seq):
        lax.fori_loop(2 * seq, 2 * seq + 2, backward, 0)
        ones.append(Reduce(out_sems.n, in_sems.n, r.n_got, r.n_middle, seq, slab_spot(back, spans[seq])))

    gxs[0].end()
    lax.fori_loop(0, 2, head_side, 0)
    for head in range(early):
        attend_back(0, head)
    over_finish(0)
    attend_back(0, early)
    gxs[1].end()
    lax.fori_loop(2, 4, head_side, 0)
    for head in range(early):
        attend_back(1, head)
    lax.fori_loop(0, 4, mixed_early, 0)
    pair_start(2)
    for head in range(early + 1, heads):
        attend_back(0, head)
    norm_side(0)
    pair_finish(2)
    ones[0].two()
    line_start(0)
    attend_back(1, early)
    over_finish(1)
    for head in range(early + 1, heads):
        attend_back(1, head)
    norm_side(1)
    lax.fori_loop(0, 4, mixed_late, 0)
    pair_start(3)
    ones[1].two()
    over_finish(2)
    pair_finish(3)
    line_start(1)

    count = jnp.ones((8, tokens), low)
    pack_own[6:7, :hidden] = right_t(count, gra[...])[0:1]
    pack_own[7:8, : 3 * head_cols] = right_t(count, head_grad[...])[0:1]
    stat_own, stat_side, stat_near, stat_sum = r.stat_own, r.stat_side, r.stat_near, r.stat_sum
    gain = vcol_ref[slab, 0:1]
    stat_own[...] = jnp.zeros_like(stat_own)
    scale_sum, shift_sum = 0.0, 0.0
    saved = []
    for seq, at in enumerate(spans):
        grad = ones[seq].end()
        normal = (x_own[:, at].astype(full) - stat_ref[0:1, at]) * stat_ref[1:2, at]
        scaled = grad * gain
        stat_own[0:1, at] = jnp.sum(scaled, axis=0, keepdims=True)
        stat_own[1:2, at] = jnp.sum(scaled * normal, axis=0, keepdims=True)
        saved.append((scaled, normal))
        scale_sum = scale_sum + grad * normal
        shift_sum = shift_sum + grad
    stat_copies = [remote(twin_id, stat_own, stat_side, out_sems.stat.at[0], in_sems.stat.at[0])]
    pack_own[4:5, :share] = lane_sums(scale_sum)[0:1]
    pack_own[5:6, :share] = lane_sums(shift_sum)[0:1]
    stat_copies[0].wait_recv()
    stat_sum[...] = stat_own[...] + stat_side[...]
    stat_copies.append(remote(near_id, stat_sum, stat_near, out_sems.stat.at[1], in_sems.stat.at[1]))
    pack_all, mid_own, mid_pair, blocks = r.pack_all, r.mid_own, r.mid_pair, r.blocks
    keep(pack_own, pack_all.at[row], in_sems.pack.at[row])
    small_copies += [
        send("row", peer, pack_own, pack_all.at[row], out_sems.pack.at[step], in_sems.pack.at[row])
        for step, peer in enumerate(row_peers)
    ]
    line_start(2)
    ys = Reduce(out_sems.y, in_sems.y, r.y_got, r.y_middle, 0, slab_spot(y_ref, pl.ds(0, tokens)))
    stat_copies[1].wait_recv()
    total = (stat_sum[...] + stat_near[...]) * (1.0 / width)
    for seq, at in enumerate(spans):
        scaled, normal = saved[seq]
        here = slice(seq * length, (seq + 1) * length)
        result = stat_ref[1:2, at] * (scaled - total[0:1, here] - normal * total[1:2, here])
        r.gin_own[:, at] = (gx_ref[slab, at].astype(full) + result).astype(low)
    for seq, at in enumerate(spans):
        swap_sent(x_ref.at[:, at], out_sems.xs.at[seq])
    swap(r.gin_own, r.gin, out_sems.gs.at[0], in_sems.gs.at[0])
    wait_recv_all(pack_own, in_sems.pack, rows)
    total = pack_all[0, 0:4]
    for index in range(1, rows):
        total = total + pack_all[index, 0:4]
    mid_own[0, 4:8] = total
    for index in range(2):
        mid_own[index, 0:4] = pack_all[index, 4:8] + pack_all[2 + index, 4:8]
    mid_own[1, 4:8] = total
    small_copies.append(remote(twin_id, mid_own, mid_pair, out_sems.mid.at[0], in_sems.mid.at[0]))
    ys.two()
    landed(mid_own, in_sems.mid.at[0])
    total = mid_own[0, 4:8] + mid_pair[0, 4:8]
    for index in range(2):
        blocks[2 * core + index, 0:4] = mid_own[index, 0:4]
        blocks[2 * twin + index, 0:4] = mid_pair[index, 0:4]
    for index in range(rows):
        blocks[index, 4:8] = total
    a_all, b_all = r.a_all, r.b_all
    keep(blocks.at[row], a_all.at[col], in_sems.t.at[0, col])
    keep(blocks.at[col], b_all.at[col], in_sems.t.at[1, col])
    for step, peer in enumerate(col_peers):
        small_copies += [
            send("col", peer, blocks.at[row], a_all.at[col], out_sems.t.at[0, step], in_sems.t.at[0, col]),
            send("col", peer, blocks.at[peer], b_all.at[col], out_sems.t.at[1, step], in_sems.t.at[1, col]),
        ]
    over_finish(3)
    line_finish(0)
    line_finish(1)
    line_start(3)
    wait_recv_all(pack_own, in_sems.t.at[0], cols)
    wait_recv_all(pack_own, in_sems.t.at[1], cols)
    a_total, b_total = a_all[0], b_all[0]
    for index in range(1, cols):
        a_total, b_total = a_total + a_all[index], b_total + b_all[index]
    wide = jnp.zeros((4, share), full)
    for index in range(rows):
        wide = wide + jnp.where(row == index, a_total[4:8, index * share : (index + 1) * share], 0.0)
    r.g_gains[0:1, :] = a_total[0:1, :share]
    r.g_gains[1:2, :] = wide[0:1]
    r.g_biases[0:1, :] = a_total[1:2, :share]
    r.g_biases[1:4, :] = wide[1:4]
    r.g_up_bias[...] = b_total[2, :hidden]
    for head in range(heads):
        top, of_head = 3 * HEAD * head, slice(head * HEAD, (head + 1) * HEAD)
        r.g_qv[0:1, of_head] = b_total[3:4, top : top + HEAD]
        r.g_qv[1:2, of_head] = b_total[3:4, top + 2 * HEAD : top + 3 * HEAD]
    r.out_own[...] = ys.end().astype(low)
    swap_sent(c_ref, out_sems.cs.at[0])
    swap(r.out_own, r.out, out_sems.gs.at[1], in_sems.gs.at[1])
    line_finish(2)
    line_finish(3)
    for part, (index, strip) in enumerate(parts):
        landed(finals[index].at[pl.ds(0, half), strip], in_sems.final.at[part])
    for index in range(3):
        for head in range(heads):
            first = head_cols + (3 * head + index) * HEAD
            r.g_wq[index, :, head * HEAD : (head + 1) * HEAD] = r.ga[:, first : first + HEAD]
    r.g_wo[...] = r.ga[:, :head_cols].T
    landed(r.gin, in_sems.gs.at[0])
    landed(r.out, in_sems.gs.at[1])
    swap_sent(r.gin, out_sems.gs.at[0])
    swap_sent(r.out, out_sems.gs.at[1])
    sent(small_copies, stat_copies, weight_copies, grad_copies)
    sent(*[move.copies for move in xs + cots + outs + l2s + gls + gxs + ones + [ys]])


def settle_kernel(count, *refs):
    for index in range(count):
        refs[count + index][...] = refs[index][...]


def settle(arrays):
    count = len(arrays)
    return pl.pallas_call(
        functools.partial(settle_kernel, count),
        out_shape=[jax.ShapeDtypeStruct(array.shape, array.dtype) for array in arrays],
        in_specs=[pl.BlockSpec(memory_space=pltpu.VMEM)] * count,
        out_specs=[pl.BlockSpec(memory_space=pltpu.VMEM)] * count,
    )(*arrays)


def square_body(
    block_input, norm_gains, row_biases, w_qkv, qv_bias, w_out, w_up, up_bias, w_down, cotangent
):
    low, full = jnp.bfloat16, jnp.float32
    share, tokens = block_input.shape
    rows, cols = lax.axis_size("row"), lax.axis_size("col")
    width = share * rows
    head_cols = w_out.shape[0]
    mixed = 3 * head_cols + share
    hidden = w_up.shape[1]
    seqs = tokens // LENGTH
    heads = head_cols // HEAD
    piece = LENGTH // rows
    half = share // 2
    lanes = -(-share // 128) * 128
    tips = -(-(2 + hidden // lanes) // 8) * 8
    inputs = dict(
        x=block_input,
        c=cotangent,
        gains=norm_gains,
        biases=row_biases,
        qv_bias=qv_bias,
        up_bias=up_bias,
        wq=w_qkv.transpose(1, 0, 2),
        wo=w_out,
        wu=w_up,
        wd=w_down,
    )
    outputs = dict(
        out=((share, tokens), low),
        gin=((share, tokens), low),
        g_gains=((2, share), full),
        g_biases=((4, share), full),
        g_wq=((3, share, head_cols), full),
        g_qv=((2, head_cols), full),
        g_wo=((head_cols, share), full),
        gu=((share, hidden), full),
        g_up_bias=((hidden,), full),
        gd=((share, hidden), full),
    )
    token_got, token_middle = (seqs, 3, width, piece), (seqs, width, piece)
    buffers = dict(
        x_all=((width, tokens), low),
        c_all=((width, tokens), low),
        wa_all=((width, mixed), low),
        wu_all=((width, hidden), low),
        wd_all=((width, hidden), low),
        ln=((width, tokens), low),
        qkv=((3 * head_cols, tokens), low),
        att=((head_cols, tokens), low),
        lse=((seqs * heads, 8, LENGTH), full),
        stat=((8, tokens), full),
        x1=((width, seqs * piece), full),
        l2=((width, tokens), low),
        gx=((width, tokens), low),
        vcol=((width, 8), full),
        tcol=((hidden, 8), full),
        wa_own=((share, mixed), low),
        vec_own=((8, lanes), full),
        tip_own=((tips, lanes), full),
        vec_all=((rows, 8, lanes), full),
        tip_all=((cols, tips, lanes), full),
        zbuf=((3, cols, half, mixed), low),
        relay=((3, 3, half, mixed), low),
        x_own=((share, tokens), low),
        c_own=((share, tokens), low),
        gin_own=((share, tokens), low),
        out_own=((share, tokens), low),
        o_part=((seqs * rows, width, piece), low),
        o_got=(token_got, low),
        o_middle=(token_middle, low),
        wu_t=((hidden, width), low),
        wd_t=((hidden, width), low),
        hid=((hidden, tokens), low),
        gra=((hidden, tokens), low),
        slope=((hidden, tokens), full),
        g_part=((seqs * rows, width, piece), low),
        g_got=(token_got, low),
        g_middle=(token_middle, low),
        y=((width, tokens), low),
        y_got=((1, 3, share, tokens), low),
        y_middle=((1, share, tokens), low),
        du=((width, hidden), low),
        dd=((width, hidden), low),
        da=((width, mixed), low),
        pack_own=((8, width), full),
        mixed_grad=((head_cols, tokens), low),
        head_grad=((3 * head_cols, tokens), low),
        back=((width, tokens), low),
        n_got=((seqs, 3, share, LENGTH), low),
        n_middle=((seqs, share, LENGTH), low),
        ga=((share, mixed), full),
        stat_own=((8, tokens), full),
        stat_side=((8, tokens), full),
        stat_near=((8, tokens), full),
        stat_sum=((8, tokens), full),
        pair=((3, rows, half, mixed), low),
        over=((3, 4, half, mixed), low),
        aside=((3, 2, half, mixed), low),
        plane=((3, cols, half, mixed), low),
        line=((3, cols, half, mixed), low),
        pack_all=((rows, 8, width), full),
        mid_own=((2, 8, width), full),
        mid_pair=((2, 8, width), full),
        blocks=((rows, 8, width), full),
        a_all=((cols, 8, width), full),
        b_all=((cols, 8, width), full),
    )
    arrivals = dict(
        x=((seqs, 3), (seqs, 3)),
        c=((seqs, 3), (seqs, 3)),
        l=((seqs, 3), (seqs, 3)),
        gx=((seqs, 3), (seqs, 3)),
        o=((seqs, 3), (seqs, 3)),
        g=((seqs, 3), (seqs, 3)),
        n=((seqs, 3), (seqs, 3)),
        y=((1, 3), (1, 3)),
        xs=((seqs,), (seqs,)),
        cs=((1,), (1,)),
        gs=((2,), (2,)),
        vec=((rows - 1,), (rows,)),
        tip=((cols - 1,), (cols,)),
        wz=((4, cols - 1), (4, cols)),
        wm=((4, 10), (4, 10)),
        wl=((4,), (4,)),
        pair=((4, rows), (4, rows)),
        over=((4, 4), (4, 4)),
        aside=((4, 2), (4, 2)),
        line=((4, cols - 1), (4, cols)),
        final=((4,), (4,)),
        stat=((2,), (2,)),
        pack=((rows - 1,), (rows,)),
        mid=((1,), (1,)),
        t=((2, cols - 1), (2, cols)),
    )
    names = (list(inputs) + list(outputs) + list(buffers), list(arrivals))
    scratch = [pltpu.VMEM(*shape) for shape in buffers.values()]
    for sends, receives in arrivals.values():
        scratch += [pltpu.SemaphoreType.DMA(sends), pltpu.SemaphoreType.DMA(receives)]
    results = pl.pallas_call(
        functools.partial(block_kernel, names, seqs),
        out_shape=[jax.ShapeDtypeStruct(*shape) for shape in outputs.values()],
        in_specs=[pl.BlockSpec(memory_space=pltpu.VMEM)] * len(inputs),
        out_specs=[pl.BlockSpec(memory_space=pltpu.VMEM)] * len(outputs),
        scratch_shapes=scratch,
        compiler_params=pltpu.CompilerParams(
            collective_id=0, has_side_effects=True, vmem_limit_bytes=BIG
        ),
    )(*inputs.values())
    out, gin, gains, biases, g_wq, g_qv, g_wo, gu, g_up_bias, gd = settle(results)
    return (out, gin, gains, biases, g_wq.transpose(1, 0, 2), g_qv, g_wo, gu, g_up_bias, gd)


def fits(mesh):
    sizes = mesh.shape
    return sizes["row"] == 4 and sizes["col"] == 4 and sizes["dp"] == 2


def solution(mesh):
    in_specs = (
        P("row", ("dp", "col")),
        P(None, "row"),
        P(None, "row"),
        P("row", None, "col"),
        P(None, "col"),
        P("col", "row"),
        P("row", "col"),
        P("col"),
        P("row", "col"),
        P("row", ("dp", "col")),
    )
    out_specs = (
        P("row", ("dp", "col")),
        P("row", ("dp", "col")),
        P(None, "row"),
        P(None, "row"),
        P("row", None, "col"),
        P(None, "col"),
        P("col", "row"),
        P("row", "col"),
        P("col"),
        P("row", "col"),
    )
    chosen = square_body if fits(mesh) else body
    return jax.shard_map(chosen, mesh=mesh, in_specs=in_specs, out_specs=out_specs, check_vma=False)
```
